32 devices in a mesh: win: 2 (over x), wide: 8 (over z, y), narrow: 2 (over core).
Axes of the slice: x: 2, y: 2, z: 4, core: 2. Of those that a mesh axis runs over, the one named last changes fastest.
Arguments:
- window_data: float32 [384, 128, 256], P(('win', 'wide'), 'narrow'), parts along dimension 0, may hold values from -6 to 6
- factor_one: float32 [256, 48], P(('win', 'narrow')), parts along dimension 0, may hold values from -0.5 to 0.5
- factor_two: float32 [512, 48], P('win'), parts along dimension 0, may hold values from -0.375 to 0.375
- factor_three: float32 [384, 48], P(('win', 'wide')), parts along dimension 0, may hold values from -0.4375 to 0.4375
Outputs:
- basis_one: float32 [256, 48], P(('win', 'narrow')), parts along dimension 0
- basis_two: float32 [512, 48], P('win'), parts along dimension 0
- basis_three: float32 [384, 48], P(('win', 'wide')), parts along dimension 0
- core_unfolded: float32 [48, 4608], P(None, ('win', 'wide', 'narrow')), parts along dimension 1
The draws below stay inside these ranges and needn't reach their ends.
There are 2 independent parts, one for each index of `win`. The reference program is written for one: setup_inputs(seed, part) draws one part's arguments, and reference() takes and returns one part's arrays. A program takes and returns all parts, laid end to end along the dimension named above; each array names one. Nothing has to cross between parts.
All inputs are finite; a program needn't handle non-finite values.
Results may differ from the reference program's by a relative error of at most 0.0003.
Values sent between devices are 32-bit elements; how exact they have to be, the bound alone decides.
No kernel may reach another device: no remote copies, remote signals or barrier semaphores. Data moves between devices by JAX's collectives and lax.ppermute only.
A program may use at most 64 MiB of HBM per device.

```python
import jax
import jax.numpy as jnp
from jax import lax

R = 48
I2 = 256
I1 = 128
I3 = 192


def levels(key, dims, pieces, low, high):
    gain = 1.0
    for axis_at, blocks in pieces:
        steps = jax.random.uniform(jax.random.fold_in(jax.random.fold_in(key, 6), axis_at), (blocks,), jnp.float32, low / len(pieces), high / len(pieces))
        gain = gain * jnp.repeat(jnp.exp(steps), dims[axis_at] // blocks).reshape((-1,) + (1,) * (len(dims) - 1 - axis_at))
    return gain


def normal_values(key, shape, scale, reach, cuts=(), kind=jnp.bfloat16):
    entries = scale * jax.random.normal(key, shape, jnp.float32)
    if cuts:
        entries = entries * levels(key, shape, cuts, -0.22, 0.18)
    return jnp.clip(entries, -reach, reach).astype(kind)


def setup_inputs(seed: int = 0, part: int = 0) -> dict:
    seeds = jax.random.split(jax.random.key(seed), 5)
    part_splits = jax.random.split(jax.random.fold_in(seeds[4], part), 5)
    window_data = normal_values(part_splits[0], (I3, I1, I2), 1.0, 6.0, ((0, 8), (1, 2)), jnp.float32)
    factor_one = normal_values(part_splits[1], (I1, R), I1 ** -0.5, 0.5, ((0, 2),), jnp.float32)
    factor_two = normal_values(part_splits[2], (I2, R), I2 ** -0.5, 0.375, (), jnp.float32)
    factor_three = normal_values(part_splits[3], (I3, R), I3 ** -0.5, 0.4375, ((0, 8),), jnp.float32)
    return {"window_data": window_data, "factor_one": factor_one, "factor_two": factor_two, "factor_three": factor_three}


highest = lax.Precision.HIGHEST

def contract(form, left, right):
    return jnp.einsum(form, left, right, precision=highest)

def orthonormal(basis):
    gram = jnp.dot(basis.T, basis, precision=highest)
    lower = jnp.linalg.cholesky(gram)
    return lax.linalg.triangular_solve(lower, basis, left_side=False, lower=True, transpose_a=True)

def reference(window_data, factor_one, factor_two, factor_three):
    along_two = contract('kij,jb->kib', window_data, factor_two)
    unfold_one = contract('kib,kc->ibc', along_two, factor_three)
    weights_one = contract('ibc,ia->bca', unfold_one, factor_one)
    basis_one = orthonormal(contract('ibc,bca->ia', unfold_one, weights_one))
    along_one = contract('kij,ia->kaj', window_data, basis_one)
    unfold_two = contract('kaj,kc->jac', along_one, factor_three)
    weights_two = contract('jac,jb->acb', unfold_two, factor_two)
    basis_two = orthonormal(contract('jac,acb->jb', unfold_two, weights_two))
    along_new = contract('kij,jb->kib', window_data, basis_two)
    unfold_three = contract('kib,ia->kab', along_new, basis_one)
    weights_three = contract('kab,kc->abc', unfold_three, factor_three)
    basis_three = orthonormal(contract('kab,abc->kc', unfold_three, weights_three))
    core = contract('kab,kc->abc', unfold_three, basis_three).reshape(R, R * R)
    return (basis_one, basis_two, basis_three, core)
```

```python
import jax
import jax.numpy as jnp
from jax import lax
from jax.sharding import PartitionSpec as P

highest = lax.Precision.HIGHEST
fine = lax.Precision.HIGH
group = ("wide", "narrow")


def contract(form, left, right, precision=fine):
    return jnp.einsum(form, left, right, precision=precision)


def total(part, axis):
    size = lax.axis_size(axis)
    if size & (size - 1):
        return lax.psum(part, axis)
    step = 1
    while step < size:
        part = part + lax.ppermute(part, axis, [(at, at ^ step) for at in range(size)])
        step *= 2
    return part


def orthonormal(product_t):
    gram = jnp.einsum("an,bn->ab", product_t, product_t, precision=highest)
    lower = jnp.linalg.cholesky(gram)
    return lax.linalg.triangular_solve(lower, product_t, left_side=True, lower=True)


def swap(value):
    return lax.ppermute(value, "narrow", [(0, 1), (1, 0)])


def on_device(window_data, factor_one, factor_two, factor_three):
    wide = lax.axis_size("wide")
    narrow = lax.axis_size("narrow")
    count = wide * narrow
    depth, rows, cols = window_data.shape
    rank = factor_one.shape[1]
    share = -(-rank // count)
    spare = share * count - rank
    half = depth // narrow
    core_at = lax.axis_index("narrow")

    own = lax.dynamic_slice_in_dim(window_data, core_at * half, half, 0)
    sent = lax.dynamic_slice_in_dim(window_data, (1 - core_at) * half, half, 0)
    other = swap(sent)
    factor_other = swap(factor_one)

    two_t = jnp.pad(factor_two.T, ((0, spare), (0, 0)))
    along = contract("bj,kij->bki", two_t, window_data).reshape(count, share, depth * rows)
    three_own = lax.dynamic_slice_in_dim(factor_three, core_at * half, half, 0)
    three_flat = jnp.broadcast_to(three_own.reshape(1, 1, half * rank), (count, 1, half * rank))
    packed = jnp.concatenate([along.reshape(count, -1), three_flat.reshape(count, -1)], axis=1)
    width = packed.shape[1]
    full = -(-width // 1024) * 1024
    packed = jnp.pad(packed, ((0, 0), (0, full - width))).reshape(count, full // 128, 128)
    got = lax.all_to_all(packed, group, 0, 0, tiled=True).reshape(count, full)
    three = got[:, share * depth * rows : width].reshape(wide, depth, rank)
    got = got[:, : share * depth * rows].reshape(wide, narrow, share, depth, rows)
    first = jnp.where(core_at == 0, factor_one, factor_other)
    second = jnp.where(core_at == 0, factor_other, factor_one)
    one = jnp.stack([first, second])
    unfold = contract("wnbki,wkc->bcni", got, three)
    weights = contract("bcni,nia->bca", unfold, one)
    product = contract("bcni,bca->ani", unfold, weights).reshape(rank, narrow * rows)
    product = total(total(product, "narrow"), "wide")
    one_t = orthonormal(product)

    one_pad = jnp.pad(one_t, ((0, spare), (0, 0)))
    one_own = lax.dynamic_slice_in_dim(one_pad, core_at * rows, rows, 1)
    one_other = lax.dynamic_slice_in_dim(one_pad, (1 - core_at) * rows, rows, 1)
    along = contract("ai,kij->akj", one_own, own) + contract("ai,kij->akj", one_other, other)
    got = lax.all_to_all(
        along.reshape(count, share * half * cols // 128, 128), group, 0, 0, tiled=True
    ).reshape(count, share, half, cols)
    three = three.reshape(count, half, rank)
    unfold = contract("dakj,dkc->acj", got, three)
    weights = contract("acj,jb->acb", unfold, factor_two)
    product = contract("acj,acb->bj", unfold, weights)
    product = total(total(product, "narrow"), "wide")
    two_t = orthonormal(product)

    unfold = contract("dakj,bj->dakb", got, two_t)
    weights = contract("dakb,dkc->abc", unfold, three)
    product = contract("dakb,abc->cdk", unfold, weights).reshape(rank, count * half)
    product = total(total(product, "narrow"), "wide")
    three_t = orthonormal(product)
    core = contract("dakb,cdk->abc", unfold, three_t.reshape(rank, count, half))
    core = core.reshape(share, count, rank * rank // count).transpose(1, 0, 2)
    core = lax.all_to_all(core, group, 0, 0, tiled=True)
    core = core.reshape(count * share, rank * rank // count)[:rank]
    basis_three = lax.dynamic_slice_in_dim(three_t, lax.axis_index("wide") * depth, depth, 1).T
    return (one_own[:rank].T, two_t.T, basis_three, core)


def solution(mesh):
    return jax.shard_map(
        on_device,
        mesh=mesh,
        in_specs=(
            P(("win", "wide"), "narrow", None),
            P(("win", "narrow"), None),
            P("win", None),
            P(("win", "wide"), None),
        ),
        out_specs=(
            P(("win", "narrow"), None),
            P("win", None),
            P(("win", "wide"), None),
            P(None, ("win", "wide", "narrow")),
        ),
        check_vma=False,
    )
```

```python
import jax
import jax.numpy as jnp
from jax import lax
from jax.experimental import pallas as pl
from jax.experimental.pallas import tpu as pltpu
from jax.sharding import PartitionSpec as P

highest = lax.Precision.HIGHEST
fine = lax.Precision.HIGH
group = ("wide", "narrow")
lanes = 128
nn = (((1,), (0,)), ((), ()))
nt = (((1,), (1,)), ((), ()))
tn = (((0,), (0,)), ((), ()))


def contract(form, left, right, precision=fine):
    return jnp.einsum(form, left, right, precision=precision)


def total(part, axis):
    size = lax.axis_size(axis)
    if size & (size - 1):
        return lax.psum(part, axis)
    step = 1
    while step < size:
        part = part + lax.ppermute(part, axis, [(at, at ^ step) for at in range(size)])
        step *= 2
    return part


def swap(value):
    return lax.ppermute(value, "narrow", [(0, 1), (1, 0)])


def dot(left, right, dims=nn):
    return lax.dot_general(
        left, right, dims, precision=highest, preferred_element_type=jnp.float32
    )


def split(value):
    high = value.astype(jnp.bfloat16)
    return high, (value - high.astype(jnp.float32)).astype(jnp.bfloat16)


def dot3(left, right, dims=nn):
    left_high, left_low = left if isinstance(left, tuple) else split(left)
    right_high, right_low = right if isinstance(right, tuple) else split(right)

    def one(a, b):
        return lax.dot_general(a, b, dims, preferred_element_type=jnp.float32)

    return one(left_high, right_high) + (one(left_high, right_low) + one(left_low, right_high))


def eliminate(table, rank):
    width = table.shape[1]
    row = lax.broadcasted_iota(jnp.int32, (8, width), 0)
    tiles = [table[8 * at : 8 * at + 8] for at in range(rank // 8)]
    for at in range(rank // 8):
        live = tiles[at:]
        columns = [
            [jnp.broadcast_to(x[:, 8 * at + k : 8 * at + k + 1], (8, width)) for x in live]
            for k in range(8)
        ]
        for j in range(8):
            heads = [jnp.broadcast_to(columns[k][0][j : j + 1], (8, width)) for k in range(j, 8)]
            inverse = 1.0 / heads[0]
            scale = [x * inverse for x in columns[j]]
            scale[0] = jnp.where(row > j, scale[0], 0.0)
            for k in range(j + 1, 8):
                columns[k] = [x - y * heads[k - j] for x, y in zip(columns[k], scale)]
            lead = jnp.broadcast_to(live[0][j : j + 1], (8, width))
            live = [x - y * lead for x, y in zip(live, scale)]
        tiles[at:] = live
    return jnp.concatenate(tiles, axis=0)


def orthonormal(part):
    rank, size = part.shape
    width = -(-2 * rank // lanes) * lanes
    below = jnp.zeros((width - rank, size), part.dtype)
    gram = dot(part, jnp.concatenate([part, below]), nt)
    row = lax.broadcasted_iota(jnp.int32, (rank, width), 0)
    lane = lax.broadcasted_iota(jnp.int32, (rank, width), 1)
    table = eliminate(jnp.where(lane == row + rank, 1.0, gram), rank)
    pivots = jnp.sum(jnp.where(lane == row, table, 0.0), axis=1, keepdims=True)
    table = jnp.where(lane < rank, 0.0, table * lax.rsqrt(pivots))
    padded = [jnp.zeros((rank, size), part.dtype), part]
    if width > 2 * rank:
        padded.append(jnp.zeros((width - 2 * rank, size), part.dtype))
    return dot(table, jnp.concatenate(padded))


def orthonormal_body(part, out):
    out[...] = orthonormal(part[...])


def call(body, shapes, *operands, **settings):
    shapes = [jax.ShapeDtypeStruct(shape, jnp.float32) for shape in shapes]
    return pl.pallas_call(body, out_shape=shapes, **settings)(*operands)


def general(window_data, factor_one, factor_two, factor_three):
    wide = lax.axis_size("wide")
    narrow = lax.axis_size("narrow")
    count = wide * narrow
    depth, rows, cols = window_data.shape
    rank = factor_one.shape[1]
    share = -(-rank // count)
    spare = share * count - rank
    half = depth // narrow
    core_at = lax.axis_index("narrow")

    own = lax.dynamic_slice_in_dim(window_data, core_at * half, half, 0)
    sent = lax.dynamic_slice_in_dim(window_data, (1 - core_at) * half, half, 0)
    other = swap(sent)
    factor_other = swap(factor_one)

    two_t = jnp.pad(factor_two.T, ((0, spare), (0, 0)))
    along = contract("bj,kij->bki", two_t, window_data).reshape(count, share, depth * rows)
    three_own = lax.dynamic_slice_in_dim(factor_three, core_at * half, half, 0)
    three_flat = jnp.broadcast_to(three_own.reshape(1, 1, half * rank), (count, 1, half * rank))
    packed = jnp.concatenate([along.reshape(count, -1), three_flat.reshape(count, -1)], axis=1)
    width = packed.shape[1]
    full = -(-width // 1024) * 1024
    packed = jnp.pad(packed, ((0, 0), (0, full - width))).reshape(count, full // 128, 128)
    got = lax.all_to_all(packed, group, 0, 0, tiled=True).reshape(count, full)
    three = got[:, share * depth * rows : width].reshape(wide, depth, rank)
    got = got[:, : share * depth * rows].reshape(wide, narrow, share, depth, rows)
    first = jnp.where(core_at == 0, factor_one, factor_other)
    second = jnp.where(core_at == 0, factor_other, factor_one)
    one = jnp.stack([first, second])
    unfold = contract("wnbki,wkc->bcni", got, three)
    weights = contract("bcni,nia->bca", unfold, one)
    product = contract("bcni,bca->ani", unfold, weights).reshape(rank, narrow * rows)
    product = total(total(product, "narrow"), "wide")
    one_t = call(orthonormal_body, [product.shape], product)[0]

    one_pad = jnp.pad(one_t, ((0, spare), (0, 0)))
    one_own = lax.dynamic_slice_in_dim(one_pad, core_at * rows, rows, 1)
    one_other = lax.dynamic_slice_in_dim(one_pad, (1 - core_at) * rows, rows, 1)
    along = contract("ai,kij->akj", one_own, own) + contract("ai,kij->akj", one_other, other)
    got = lax.all_to_all(
        along.reshape(count, share * half * cols // 128, 128), group, 0, 0, tiled=True
    ).reshape(count, share, half, cols)
    three = three.reshape(count, half, rank)
    unfold = contract("dakj,dkc->acj", got, three)
    weights = contract("acj,jb->acb", unfold, factor_two)
    product = contract("acj,acb->bj", unfold, weights)
    product = total(total(product, "narrow"), "wide")
    two_t = call(orthonormal_body, [product.shape], product)[0]

    unfold = contract("dakj,bj->dakb", got, two_t)
    weights = contract("dakb,dkc->abc", unfold, three)
    product = contract("dakb,abc->cdk", unfold, weights).reshape(rank, count * half)
    product = total(total(product, "narrow"), "wide")
    three_t = call(orthonormal_body, [product.shape], product)[0]
    core = contract("dakb,cdk->abc", unfold, three_t.reshape(rank, count, half))
    core = core.reshape(share, count, rank * rank // count).transpose(1, 0, 2)
    core = lax.all_to_all(core, group, 0, 0, tiled=True)
    core = core.reshape(count * share, rank * rank // count)[:rank]
    basis_three = lax.dynamic_slice_in_dim(three_t, lax.axis_index("wide") * depth, depth, 1).T
    return (one_own[:rank].T, two_t.T, basis_three, core)


def pack_one(field, two, three, out, *, share, half, count):
    at = pl.program_id(0)
    steps, rows, cols = field.shape[1:]
    rank = two.shape[0]
    slots = share + 1
    two_high, two_low = split(two[...])
    both = jnp.concatenate([two_high, two_low])
    for q in range(steps):
        high, low = split(field[:, q].reshape(2 * rows, cols))
        first = lax.dot_general(both, high, nt, preferred_element_type=jnp.float32)
        second = lax.dot_general(two_high, low, nt, preferred_element_type=jnp.float32)
        along = first[:rank] + (first[rank:] + second)
        for s in range(share):
            start = (at * steps + q) * slots + s
            out[pl.ds(start, count, stride=half * slots), :] = along[s * count : (s + 1) * count]

    @pl.when(at == 0)
    def _():
        first = three[:half]
        second = three[half:]
        room = jnp.zeros((half, lanes // 2 - rank), jnp.float32)
        both = jnp.concatenate([first, room, second, room], axis=1)
        for d in range(count):
            out[pl.ds(d * half * slots + share, half, stride=slots), :] = both


def work_one(got, own, other, out, three, *, share, half, count):
    rank = own.shape[1]
    slots = share + 1
    size = count * half
    at = lax.axis_index("narrow")
    low = jnp.where(at == 0, own[...], other[...])
    high = jnp.where(at == 0, other[...], own[...])
    one = jnp.concatenate([low, high])
    table = got[pl.ds(share, size, stride=slots), :]
    row = lax.broadcasted_iota(jnp.int32, (size, lanes), 0)
    odd = (row // half) % 2 == 1
    part = lanes // 2
    three[...] = jnp.where(odd, pltpu.roll(table, part, 1), table)[:, :rank]
    table = jnp.concatenate([jnp.where(odd, 0.0, table), jnp.where(odd, table, 0.0)], axis=1)
    table = split(table)
    lane = lax.broadcasted_iota(jnp.int32, (rank, lanes), 1)
    pieces = []
    for s in range(share):
        value = dot3(table, got[pl.ds(s, size, stride=slots), :], tn)
        first = value[:rank] + pltpu.roll(value[part : part + rank], part, 1)
        second = (
            pltpu.roll(value[2 * part : 2 * part + rank], part, 1)
            + value[3 * part : 3 * part + rank]
        )
        pieces.append(jnp.where(lane < part, first, second))
    unfold = split(jnp.concatenate(pieces))
    out[...] = dot3(dot3(unfold, one), unfold, tn)


def pack_two(part, own, other, basis, out, *, share, half, count):
    rows, cols = own.shape[1:]
    value = orthonormal(part[...])
    basis[...] = value
    slots = share * (cols // lanes)
    at = lax.axis_index("narrow")
    value = split(jnp.where(at == 0, value, pltpu.roll(value, rows, 1)))
    both = jnp.concatenate(value)
    rank = part.shape[0]
    for k in range(half):
        high, low = split(jnp.concatenate([own[k], other[k]]))
        first = lax.dot_general(both, high, nn, preferred_element_type=jnp.float32)
        second = lax.dot_general(value[0], low, nn, preferred_element_type=jnp.float32)
        along = first[:rank] + (first[rank:] + second)
        for s in range(share):
            for h in range(cols // lanes):
                start = k * slots + s * (cols // lanes) + h
                out[pl.ds(start, count, stride=half * slots), :] = along[
                    s * count : (s + 1) * count, h * lanes : (h + 1) * lanes
                ]


def taken(got, s, parts, slots, size):
    return jnp.concatenate(
        [got[pl.ds(s * parts + h, size, stride=slots), :] for h in range(parts)], axis=1
    )


def work_two(got, two, three, out, *, share, half, count):
    parts = two.shape[0] // lanes
    size = count * half
    table = split(three[...])
    unfold = split(
        jnp.concatenate(
            [
                dot3(table, taken(got, s, parts, share * parts, size), tn)
                for s in range(share)
            ]
        )
    )
    out[...] = dot3(dot3(unfold, two[...]), unfold, tn)


def work_three(part, got, three, basis, out, sent, room, *, share, half, count):
    rank, cols = part.shape
    parts = cols // lanes
    size = count * half
    tall = -(-size // lanes)
    pitch = sent.shape[0] // count
    value = orthonormal(part[...])
    basis[...] = value
    for h in range(parts):
        room[h * rank : (h + 1) * rank, :] = value[:, h * lanes : (h + 1) * lanes]
    second = split(
        jnp.concatenate(
            [
                jnp.concatenate(
                    [room[pl.ds(h * rank + b, count, stride=share), :] for h in range(parts)],
                    axis=1,
                )
                for b in range(share)
            ]
        )
    )
    table = split(three[...])
    result = None
    for s in range(share):
        value = dot3(second, taken(got, s, parts, share * parts, size), nt)
        for b in range(share):
            for h in range(tall):
                wide = min(lanes, size - h * lanes)
                start = (b * share + s) * tall + h
                sent[pl.ds(start, count, stride=pitch), :wide] = value[
                    b * count : (b + 1) * count, h * lanes : h * lanes + wide
                ]
        value = split(value)
        term = dot3(dot3(value, table), value, tn)
        result = term if result is None else result + term
    out[...] = result


def finish(part, got, basis, core, *, share, half, count):
    rank, size = part.shape
    tall = -(-size // lanes)
    pitch = got.shape[0] // count
    value = orthonormal(part[...])
    basis[...] = value
    value = split(value)
    for b in range(share):
        rows = []
        for s in range(share):
            pieces = []
            for h in range(tall):
                wide = min(lanes, size - h * lanes)
                start = (b * share + s) * tall + h
                pieces.append(got[pl.ds(start, count, stride=pitch), :][:, :wide])
            rows.append(jnp.concatenate(pieces, axis=1))
        core[:, b * rank : (b + 1) * rank] = dot3(jnp.concatenate(rows), value, nt)


def exchange(value, count):
    rows = value.shape[0]
    value = value.reshape(count, rows // count, lanes)
    return lax.all_to_all(value, group, 0, 0, tiled=True).reshape(rows, lanes)


def special(window_data, factor_one, factor_two, factor_three):
    wide = lax.axis_size("wide")
    count = wide * lax.axis_size("narrow")
    depth, rows, cols = window_data.shape
    rank = factor_one.shape[1]
    share = rank // count
    half = depth // 2
    size = count * half
    facts = {"share": share, "half": half, "count": count}
    core_at = lax.axis_index("narrow")

    def stage(body):
        def run(*refs):
            body(*refs, **facts)

        run.__name__ = body.__name__
        return run

    steps = 3 if half % 3 == 0 else 1
    slots = share + 1
    packed = pl.pallas_call(
        stage(pack_one),
        grid=(steps,),
        in_specs=[
            pl.BlockSpec((2, half // steps, rows, cols), lambda at: (0, at, 0, 0)),
            pl.BlockSpec((rank, cols), lambda at: (0, 0)),
            pl.BlockSpec((depth, rank), lambda at: (0, 0)),
        ],
        out_specs=pl.BlockSpec((size * slots, lanes), lambda at: (0, 0)),
        out_shape=jax.ShapeDtypeStruct((size * slots, lanes), jnp.float32),
    )(window_data.reshape(2, half, rows, cols), factor_two.T, factor_three)
    got = exchange(packed, count)
    own = lax.dynamic_slice_in_dim(window_data, core_at * half, half, 0)
    other = swap(lax.dynamic_slice_in_dim(window_data, (1 - core_at) * half, half, 0))
    product, three = call(
        stage(work_one), [(rank, 2 * rows), (size, rank)], got, factor_one, swap(factor_one)
    )
    product = total(total(product, "narrow"), "wide")

    parts = cols // lanes
    one_t, packed = call(
        stage(pack_two), [product.shape, (size * share * parts, lanes)], product, own, other
    )
    got = exchange(packed, count)
    (product,) = call(stage(work_two), [(rank, cols)], got, factor_two, three)
    product = total(total(product, "narrow"), "wide")

    pitch = -(-share * share * -(-size // lanes) // 8) * 8
    two_t, product, sent = call(
        stage(work_three),
        [product.shape, (rank, size), (count * pitch, lanes)],
        product,
        got,
        three,
        scratch_shapes=[pltpu.VMEM((parts * rank, lanes), jnp.float32)],
    )
    got = exchange(sent, count)
    product = total(total(product, "narrow"), "wide")
    three_t, core = call(stage(finish), [product.shape, (rank, share * rank)], product, got)
    basis_one = lax.dynamic_slice_in_dim(one_t, core_at * rows, rows, 1).T
    basis_three = lax.dynamic_slice_in_dim(three_t, lax.axis_index("wide") * depth, depth, 1).T
    return (basis_one, two_t.T, basis_three, core)


def on_device(window_data, factor_one, factor_two, factor_three):
    count = lax.axis_size("wide") * lax.axis_size("narrow")
    depth, rows, cols = window_data.shape
    rank = factor_one.shape[1]
    fits = (
        lax.axis_size("narrow") == 2
        and rank % count == 0
        and count % 8 == 0
        and depth % 2 == 0
        and (depth // 2) * (rank // count + 1) % 8 == 0
        and (depth // 2) * (rank // count) * (cols // lanes) % 8 == 0
        and 2 * rows == lanes
        and 2 * rank <= lanes
        and cols % lanes == 0
    )
    return (special if fits else general)(window_data, factor_one, factor_two, factor_three)


def solution(mesh):
    return jax.shard_map(
        on_device,
        mesh=mesh,
        in_specs=(
            P(("win", "wide"), "narrow", None),
            P(("win", "narrow"), None),
            P("win", None),
            P(("win", "wide"), None),
        ),
        out_specs=(
            P(("win", "narrow"), None),
            P("win", None),
            P(("win", "wide"), None),
            P(None, ("win", "wide", "narrow")),
        ),
        check_vma=False,
    )
```

```python
import jax
import jax.numpy as jnp
from jax import lax
from jax.experimental import pallas as pl
from jax.experimental.pallas import tpu as pltpu
from jax.sharding import PartitionSpec as P

highest = lax.Precision.HIGHEST
fine = lax.Precision.HIGH
group = ("wide", "narrow")
lanes = 128
nn = (((1,), (0,)), ((), ()))
nt = (((1,), (1,)), ((), ()))
tn = (((0,), (0,)), ((), ()))


def contract(form, left, right, precision=fine):
    return jnp.einsum(form, left, right, precision=precision)


def total(part, axis):
    size = lax.axis_size(axis)
    if size & (size - 1):
        return lax.psum(part, axis)
    step = 1
    while step < size:
        part = part + lax.ppermute(part, axis, [(at, at ^ step) for at in range(size)])
        step *= 2
    return part


def swap(value):
    return lax.ppermute(value, "narrow", [(0, 1), (1, 0)])


def dot(left, right, dims=nn):
    return lax.dot_general(
        left, right, dims, precision=highest, preferred_element_type=jnp.float32
    )


def split(value):
    high = value.astype(jnp.bfloat16)
    return high, (value - high.astype(jnp.float32)).astype(jnp.bfloat16)


def dot3(left, right, dims=nn):
    left_high, left_low = left if isinstance(left, tuple) else split(left)
    right_high, right_low = right if isinstance(right, tuple) else split(right)

    def one(a, b):
        return lax.dot_general(a, b, dims, preferred_element_type=jnp.float32)

    return one(left_high, right_high) + (one(left_high, right_low) + one(left_low, right_high))


def eliminate(table, rank):
    width = table.shape[1]
    row = lax.broadcasted_iota(jnp.int32, (8, width), 0)
    tiles = [table[8 * at : 8 * at + 8] for at in range(rank // 8)]
    for at in range(rank // 8):
        live = tiles[at:]
        columns = [
            [jnp.broadcast_to(x[:, 8 * at + k : 8 * at + k + 1], (8, width)) for x in live]
            for k in range(8)
        ]
        for j in range(8):
            heads = [jnp.broadcast_to(columns[k][0][j : j + 1], (8, width)) for k in range(j, 8)]
            inverse = 1.0 / heads[0]
            scale = [x * inverse for x in columns[j]]
            scale[0] = jnp.where(row > j, scale[0], 0.0)
            for k in range(j + 1, 8):
                columns[k] = [x - y * heads[k - j] for x, y in zip(columns[k], scale)]
            lead = jnp.broadcast_to(live[0][j : j + 1], (8, width))
            live = [x - y * lead for x, y in zip(live, scale)]
        tiles[at:] = live
    return jnp.concatenate(tiles, axis=0)


def orthonormal(part):
    rank, size = part.shape
    width = -(-2 * rank // lanes) * lanes
    below = jnp.zeros((width - rank, size), part.dtype)
    gram = dot(part, jnp.concatenate([part, below]), nt)
    row = lax.broadcasted_iota(jnp.int32, (rank, width), 0)
    lane = lax.broadcasted_iota(jnp.int32, (rank, width), 1)
    table = eliminate(jnp.where(lane == row + rank, 1.0, gram), rank)
    pivots = jnp.sum(jnp.where(lane == row, table, 0.0), axis=1, keepdims=True)
    table = jnp.where(lane < rank, 0.0, table * lax.rsqrt(pivots))
    padded = [jnp.zeros((rank, size), part.dtype), part]
    if width > 2 * rank:
        padded.append(jnp.zeros((width - 2 * rank, size), part.dtype))
    return dot(table, jnp.concatenate(padded))


def orthonormal_body(part, out):
    out[...] = orthonormal(part[...])


def call(body, shapes, *operands, far=(), out_far=False, **settings):
    near = pl.BlockSpec(memory_space=pltpu.VMEM)
    away = pl.BlockSpec(memory_space=pl.ANY)
    placed = [
        x if at in far else pltpu.with_memory_space_constraint(x, pltpu.VMEM)
        for at, x in enumerate(operands)
    ]
    kind = jax.ShapeDtypeStruct if out_far else pltpu.VMEM
    return pl.pallas_call(
        body,
        in_specs=[away if at in far else near for at in range(len(operands))],
        out_specs=[near] * len(shapes),
        out_shape=[kind(shape, jnp.float32) for shape in shapes],
        **settings,
    )(*placed)


def general(window_data, factor_one, factor_two, factor_three):
    wide = lax.axis_size("wide")
    narrow = lax.axis_size("narrow")
    count = wide * narrow
    depth, rows, cols = window_data.shape
    rank = factor_one.shape[1]
    share = -(-rank // count)
    spare = share * count - rank
    half = depth // narrow
    core_at = lax.axis_index("narrow")

    own = lax.dynamic_slice_in_dim(window_data, core_at * half, half, 0)
    sent = lax.dynamic_slice_in_dim(window_data, (1 - core_at) * half, half, 0)
    other = swap(sent)
    factor_other = swap(factor_one)

    two_t = jnp.pad(factor_two.T, ((0, spare), (0, 0)))
    along = contract("bj,kij->bki", two_t, window_data).reshape(count, share, depth * rows)
    three_own = lax.dynamic_slice_in_dim(factor_three, core_at * half, half, 0)
    three_flat = jnp.broadcast_to(three_own.reshape(1, 1, half * rank), (count, 1, half * rank))
    packed = jnp.concatenate([along.reshape(count, -1), three_flat.reshape(count, -1)], axis=1)
    width = packed.shape[1]
    full = -(-width // 1024) * 1024
    packed = jnp.pad(packed, ((0, 0), (0, full - width))).reshape(count, full // 128, 128)
    got = lax.all_to_all(packed, group, 0, 0, tiled=True).reshape(count, full)
    three = got[:, share * depth * rows : width].reshape(wide, depth, rank)
    got = got[:, : share * depth * rows].reshape(wide, narrow, share, depth, rows)
    first = jnp.where(core_at == 0, factor_one, factor_other)
    second = jnp.where(core_at == 0, factor_other, factor_one)
    one = jnp.stack([first, second])
    unfold = contract("wnbki,wkc->bcni", got, three)
    weights = contract("bcni,nia->bca", unfold, one)
    product = contract("bcni,bca->ani", unfold, weights).reshape(rank, narrow * rows)
    product = total(total(product, "narrow"), "wide")
    one_t = call(orthonormal_body, [product.shape], product)[0]

    one_pad = jnp.pad(one_t, ((0, spare), (0, 0)))
    one_own = lax.dynamic_slice_in_dim(one_pad, core_at * rows, rows, 1)
    one_other = lax.dynamic_slice_in_dim(one_pad, (1 - core_at) * rows, rows, 1)
    along = contract("ai,kij->akj", one_own, own) + contract("ai,kij->akj", one_other, other)
    got = lax.all_to_all(
        along.reshape(count, share * half * cols // 128, 128), group, 0, 0, tiled=True
    ).reshape(count, share, half, cols)
    three = three.reshape(count, half, rank)
    unfold = contract("dakj,dkc->acj", got, three)
    weights = contract("acj,jb->acb", unfold, factor_two)
    product = contract("acj,acb->bj", unfold, weights)
    product = total(total(product, "narrow"), "wide")
    two_t = call(orthonormal_body, [product.shape], product)[0]

    unfold = contract("dakj,bj->dakb", got, two_t)
    weights = contract("dakb,dkc->abc", unfold, three)
    product = contract("dakb,abc->cdk", unfold, weights).reshape(rank, count * half)
    product = total(total(product, "narrow"), "wide")
    three_t = call(orthonormal_body, [product.shape], product)[0]
    core = contract("dakb,cdk->abc", unfold, three_t.reshape(rank, count, half))
    core = core.reshape(share, count, rank * rank // count).transpose(1, 0, 2)
    core = lax.all_to_all(core, group, 0, 0, tiled=True)
    core = core.reshape(count * share, rank * rank // count)[:rank]
    basis_three = lax.dynamic_slice_in_dim(three_t, lax.axis_index("wide") * depth, depth, 1).T
    return (one_own[:rank].T, two_t.T, basis_three, core)


def pack_one(field, two_far, three_far, out, room, two, three, arrived, landed, *, share, half, count):
    chunks, _, steps, rows, cols = room.shape
    rank = two.shape[0]
    slots = share + 1

    def fetch(at, h):
        source = field.at[pl.ds(h * half + at * steps, steps)]
        return pltpu.make_async_copy(source, room.at[at, h], arrived.at[at, h])

    copies = [
        pltpu.make_async_copy(three_far, three, landed.at[0]),
        pltpu.make_async_copy(two_far, two, landed.at[1]),
    ]
    for copy in copies:
        copy.start()
    for at in range(chunks):
        for h in range(2):
            fetch(at, h).start()
    copies[0].wait()
    first = three[:half]
    second = three[half:]
    empty = jnp.zeros((half, lanes // 2 - rank), jnp.float32)
    both = jnp.concatenate([first, empty, second, empty], axis=1)
    for d in range(count):
        out[pl.ds(d * half * slots + share, half, stride=slots), :] = both
    copies[1].wait()
    two_high, two_low = split(two[...])
    both = jnp.concatenate([two_high, two_low])
    for at in range(chunks):
        for h in range(2):
            fetch(at, h).wait()
        for q in range(steps):
            high, low = split(room[at, :, q].reshape(2 * rows, cols))
            first = lax.dot_general(both, high, nt, preferred_element_type=jnp.float32)
            second = lax.dot_general(two_high, low, nt, preferred_element_type=jnp.float32)
            along = first[:rank] + (first[rank:] + second)
            for s in range(share):
                start = (at * steps + q) * slots + s
                out[pl.ds(start, count, stride=half * slots), :] = along[
                    s * count : (s + 1) * count
                ]


def work_one(got, own, other, out, three, *, share, half, count):
    rank = own.shape[1]
    slots = share + 1
    size = count * half
    at = lax.axis_index("narrow")
    low = jnp.where(at == 0, own[...], other[...])
    high = jnp.where(at == 0, other[...], own[...])
    one = jnp.concatenate([low, high])
    table = got[pl.ds(share, size, stride=slots), :]
    row = lax.broadcasted_iota(jnp.int32, (size, lanes), 0)
    odd = (row // half) % 2 == 1
    part = lanes // 2
    three[...] = jnp.where(odd, pltpu.roll(table, part, 1), table)[:, :rank]
    table = jnp.concatenate([jnp.where(odd, 0.0, table), jnp.where(odd, table, 0.0)], axis=1)
    table = split(table)
    lane = lax.broadcasted_iota(jnp.int32, (rank, lanes), 1)
    pieces = []
    for s in range(share):
        value = dot3(table, got[pl.ds(s, size, stride=slots), :], tn)
        first = value[:rank] + pltpu.roll(value[part : part + rank], part, 1)
        second = (
            pltpu.roll(value[2 * part : 2 * part + rank], part, 1)
            + value[3 * part : 3 * part + rank]
        )
        pieces.append(jnp.where(lane < part, first, second))
    unfold = split(jnp.concatenate(pieces))
    out[...] = dot3(dot3(unfold, one), unfold, tn)


def pack_two(part, field, other, basis, out, room, arrived, *, share, half, count):
    rows, cols = other.shape[1:]
    at = lax.axis_index("narrow")
    own = pltpu.make_async_copy(
        field.at[pl.ds(at * half, half)],
        room.at[:, pl.ds(pl.multiple_of(at * rows, 8), rows), :],
        arrived.at[0],
    )
    rest = pltpu.make_async_copy(
        other, room.at[:, pl.ds(pl.multiple_of((1 - at) * rows, 8), rows), :], arrived.at[1]
    )
    own.start()
    rest.start()
    value = orthonormal(part[...])
    basis[...] = value
    slots = share * (cols // lanes)
    value = split(value)
    both = jnp.concatenate(value)
    rank = part.shape[0]
    own.wait()
    rest.wait()
    for k in range(half):
        high, low = split(room[k])
        first = lax.dot_general(both, high, nn, preferred_element_type=jnp.float32)
        second = lax.dot_general(value[0], low, nn, preferred_element_type=jnp.float32)
        along = first[:rank] + (first[rank:] + second)
        for s in range(share):
            for h in range(cols // lanes):
                start = k * slots + s * (cols // lanes) + h
                out[pl.ds(start, count, stride=half * slots), :] = along[
                    s * count : (s + 1) * count, h * lanes : (h + 1) * lanes
                ]


def taken(got, s, parts, slots, size):
    return jnp.concatenate(
        [got[pl.ds(s * parts + h, size, stride=slots), :] for h in range(parts)], axis=1
    )


def work_two(got, two, three, out, *, share, half, count):
    parts = two.shape[0] // lanes
    size = count * half
    table = split(three[...])
    unfold = split(
        jnp.concatenate(
            [
                dot3(table, taken(got, s, parts, share * parts, size), tn)
                for s in range(share)
            ]
        )
    )
    out[...] = dot3(dot3(unfold, two[...]), unfold, tn)


def work_three(part, got, three, basis, out, sent, room, *, share, half, count):
    rank, cols = part.shape
    parts = cols // lanes
    size = count * half
    tall = -(-size // lanes)
    pitch = sent.shape[0] // count
    value = orthonormal(part[...])
    basis[...] = value
    for h in range(parts):
        room[h * rank : (h + 1) * rank, :] = value[:, h * lanes : (h + 1) * lanes]
    second = split(
        jnp.concatenate(
            [
                jnp.concatenate(
                    [room[pl.ds(h * rank + b, count, stride=share), :] for h in range(parts)],
                    axis=1,
                )
                for b in range(share)
            ]
        )
    )
    table = split(three[...])
    result = None
    for s in range(share):
        value = dot3(second, taken(got, s, parts, share * parts, size), nt)
        for b in range(share):
            for h in range(tall):
                wide = min(lanes, size - h * lanes)
                start = (b * share + s) * tall + h
                sent[pl.ds(start, count, stride=pitch), :wide] = value[
                    b * count : (b + 1) * count, h * lanes : h * lanes + wide
                ]
        value = split(value)
        term = dot3(dot3(value, table), value, tn)
        result = term if result is None else result + term
    out[...] = result


def finish(part, got, basis, core, room, *, share, half, count):
    rank, size = part.shape
    tall = -(-size // lanes)
    pitch = got.shape[0] // count
    value = orthonormal(part[...])
    room[...] = value.T
    depth = basis.shape[0]
    basis[...] = room[pl.ds(pl.multiple_of(lax.axis_index("wide") * depth, 8), depth), :]
    value = split(value)
    for b in range(share):
        rows = []
        for s in range(share):
            pieces = []
            for h in range(tall):
                wide = min(lanes, size - h * lanes)
                start = (b * share + s) * tall + h
                pieces.append(got[pl.ds(start, count, stride=pitch), :][:, :wide])
            rows.append(jnp.concatenate(pieces, axis=1))
        core[:, b * rank : (b + 1) * rank] = dot3(jnp.concatenate(rows), value, nt)


def exchange(value, count):
    rows = value.shape[0]
    value = value.reshape(count, rows // count, lanes)
    return lax.all_to_all(value, group, 0, 0, tiled=True).reshape(rows, lanes)


def special(window_data, factor_one, factor_two, factor_three):
    wide = lax.axis_size("wide")
    count = wide * lax.axis_size("narrow")
    depth, rows, cols = window_data.shape
    rank = factor_one.shape[1]
    share = rank // count
    half = depth // 2
    size = count * half
    facts = {"share": share, "half": half, "count": count}
    core_at = lax.axis_index("narrow")

    def stage(body):
        def run(*refs):
            body(*refs, **facts)

        run.__name__ = body.__name__
        return run

    chunks = 3 if half % 3 == 0 else 1
    slots = share + 1
    (packed,) = call(
        stage(pack_one),
        [(size * slots, lanes)],
        window_data,
        factor_two.T,
        factor_three,
        far=(0, 1, 2),
        scratch_shapes=[
            pltpu.VMEM((chunks, 2, half // chunks, rows, cols), jnp.float32),
            pltpu.VMEM((rank, cols), jnp.float32),
            pltpu.VMEM((depth, rank), jnp.float32),
            pltpu.SemaphoreType.DMA((chunks, 2)),
            pltpu.SemaphoreType.DMA((2,)),
        ],
    )
    got = exchange(packed, count)
    field, _ = lax.optimization_barrier((window_data, packed))
    other = swap(lax.dynamic_slice_in_dim(field, (1 - core_at) * half, half, 0))
    product, three = call(
        stage(work_one), [(rank, 2 * rows), (size, rank)], got, factor_one, swap(factor_one)
    )
    product = total(total(product, "narrow"), "wide")

    parts = cols // lanes
    one_t, packed = call(
        stage(pack_two),
        [product.shape, (size * share * parts, lanes)],
        product,
        window_data,
        other,
        far=(1, 2),
        scratch_shapes=[
            pltpu.VMEM((half, 2 * rows, cols), jnp.float32),
            pltpu.SemaphoreType.DMA((2,)),
        ],
    )
    got = exchange(packed, count)
    (product,) = call(stage(work_two), [(rank, cols)], got, factor_two, three)
    product = total(total(product, "narrow"), "wide")

    pitch = -(-share * share * -(-size // lanes) // 8) * 8
    two_t, product, sent = call(
        stage(work_three),
        [product.shape, (rank, size), (count * pitch, lanes)],
        product,
        got,
        three,
        scratch_shapes=[pltpu.VMEM((parts * rank, lanes), jnp.float32)],
    )
    got = exchange(sent, count)
    product = total(total(product, "narrow"), "wide")
    basis_three, core = call(
        stage(finish),
        [(depth, rank), (rank, share * rank)],
        product,
        got,
        out_far=True,
        scratch_shapes=[pltpu.VMEM((size, rank), jnp.float32)],
    )
    basis_one = lax.dynamic_slice_in_dim(one_t, core_at * rows, rows, 1).T
    return (basis_one, two_t.T, basis_three, core)


def on_device(window_data, factor_one, factor_two, factor_three):
    count = lax.axis_size("wide") * lax.axis_size("narrow")
    depth, rows, cols = window_data.shape
    rank = factor_one.shape[1]
    fits = (
        lax.axis_size("narrow") == 2
        and rank % count == 0
        and count % 8 == 0
        and depth % 8 == 0
        and (depth // 2) * (rank // count + 1) % 8 == 0
        and (depth // 2) * (rank // count) * (cols // lanes) % 8 == 0
        and 2 * rows == lanes
        and 2 * rank <= lanes
        and cols % lanes == 0
    )
    return (special if fits else general)(window_data, factor_one, factor_two, factor_three)


def solution(mesh):
    return jax.shard_map(
        on_device,
        mesh=mesh,
        in_specs=(
            P(("win", "wide"), "narrow", None),
            P(("win", "narrow"), None),
            P("win", None),
            P(("win", "wide"), None),
        ),
        out_specs=(
            P(("win", "narrow"), None),
            P("win", None),
            P(("win", "wide"), None),
            P(None, ("win", "wide", "narrow")),
        ),
        check_vma=False,
    )
```

```python
import jax
import jax.numpy as jnp
from jax import lax
from jax.experimental import pallas as pl
from jax.experimental.pallas import tpu as pltpu
from jax.sharding import PartitionSpec as P

highest = lax.Precision.HIGHEST
fine = lax.Precision.HIGH
group = ("wide", "narrow")
lanes = 128
nn = (((1,), (0,)), ((), ()))
nt = (((1,), (1,)), ((), ()))
tn = (((0,), (0,)), ((), ()))


def contract(form, left, right, precision=fine):
    return jnp.einsum(form, left, right, precision=precision)


def total(part):
    narrow = lax.axis_size("narrow")
    count = lax.axis_size("wide") * narrow
    if narrow != 2 or count & (count - 1):
        return lax.psum(part, group)

    def moved(mask):
        return lax.ppermute(part, group, [(at, at ^ mask) for at in range(count)])

    part = part + moved(1)
    bits = []
    while narrow < count:
        bits.append(narrow)
        narrow *= 2
    single = len(bits) % 2
    parts = [bits[:single]] if single else []
    parts += [bits[at : at + 2] for at in range(single, len(bits), 2)]
    for low, *high in parts:
        if high:
            near, far, both = moved(low + 1), moved(high[0] + 1), moved(low + high[0] + 1)
            part = (part + near) + (far + both)
        else:
            part = part + moved(low + 1)
    return part


def swap(value):
    return lax.ppermute(value, "narrow", [(0, 1), (1, 0)])


def dot(left, right, dims=nn):
    return lax.dot_general(
        left, right, dims, precision=highest, preferred_element_type=jnp.float32
    )


def split(value):
    high = value.astype(jnp.bfloat16)
    return high, (value - high.astype(jnp.float32)).astype(jnp.bfloat16)


def dot3(left, right, dims=nn):
    left_high, left_low = left if isinstance(left, tuple) else split(left)
    right_high, right_low = right if isinstance(right, tuple) else split(right)

    def one(a, b):
        return lax.dot_general(a, b, dims, preferred_element_type=jnp.float32)

    return one(left_high, right_high) + (one(left_high, right_low) + one(left_low, right_high))


def eliminate(table, rank):
    width = table.shape[1]
    row = lax.broadcasted_iota(jnp.int32, (8, width), 0)
    tiles = [table[8 * at : 8 * at + 8] for at in range(rank // 8)]
    for at in range(rank // 8):
        live = tiles[at:]
        columns = [
            [jnp.broadcast_to(x[:, 8 * at + k : 8 * at + k + 1], (8, width)) for x in live]
            for k in range(8)
        ]
        for j in range(8):
            heads = [jnp.broadcast_to(columns[k][0][j : j + 1], (8, width)) for k in range(j, 8)]
            inverse = 1.0 / heads[0]
            scale = [x * inverse for x in columns[j]]
            scale[0] = jnp.where(row > j, scale[0], 0.0)
            for k in range(j + 1, 8):
                columns[k] = [x - y * heads[k - j] for x, y in zip(columns[k], scale)]
            lead = jnp.broadcast_to(live[0][j : j + 1], (8, width))
            live = [x - y * lead for x, y in zip(live, scale)]
        tiles[at:] = live
    return jnp.concatenate(tiles, axis=0)


def orthonormal(part):
    rank, size = part.shape
    width = -(-2 * rank // lanes) * lanes
    below = jnp.zeros((width - rank, size), part.dtype)
    gram = dot(part, jnp.concatenate([part, below]), nt)
    row = lax.broadcasted_iota(jnp.int32, (rank, width), 0)
    lane = lax.broadcasted_iota(jnp.int32, (rank, width), 1)
    table = eliminate(jnp.where(lane == row + rank, 1.0, gram), rank)
    pivots = jnp.sum(jnp.where(lane == row, table, 0.0), axis=1, keepdims=True)
    table = jnp.where(lane < rank, 0.0, table * lax.rsqrt(pivots))
    padded = [jnp.zeros((rank, size), part.dtype), part]
    if width > 2 * rank:
        padded.append(jnp.zeros((width - 2 * rank, size), part.dtype))
    return dot(table, jnp.concatenate(padded))


def orthonormal_body(part, out):
    out[...] = orthonormal(part[...])


def call(body, shapes, *operands, far=(), out_far=False, **settings):
    near = pl.BlockSpec(memory_space=pltpu.VMEM)
    away = pl.BlockSpec(memory_space=pl.ANY)
    placed = [
        x if at in far else pltpu.with_memory_space_constraint(x, pltpu.VMEM)
        for at, x in enumerate(operands)
    ]
    kind = jax.ShapeDtypeStruct if out_far else pltpu.VMEM
    return pl.pallas_call(
        body,
        in_specs=[away if at in far else near for at in range(len(operands))],
        out_specs=[near] * len(shapes),
        out_shape=[kind(shape, jnp.float32) for shape in shapes],
        **settings,
    )(*placed)


def general(window_data, factor_one, factor_two, factor_three):
    wide = lax.axis_size("wide")
    narrow = lax.axis_size("narrow")
    count = wide * narrow
    depth, rows, cols = window_data.shape
    rank = factor_one.shape[1]
    share = -(-rank // count)
    spare = share * count - rank
    half = depth // narrow
    core_at = lax.axis_index("narrow")

    own = lax.dynamic_slice_in_dim(window_data, core_at * half, half, 0)
    sent = lax.dynamic_slice_in_dim(window_data, (1 - core_at) * half, half, 0)
    other = swap(sent)
    factor_other = swap(factor_one)

    two_t = jnp.pad(factor_two.T, ((0, spare), (0, 0)))
    along = contract("bj,kij->bki", two_t, window_data).reshape(count, share, depth * rows)
    three_own = lax.dynamic_slice_in_dim(factor_three, core_at * half, half, 0)
    three_flat = jnp.broadcast_to(three_own.reshape(1, 1, half * rank), (count, 1, half * rank))
    packed = jnp.concatenate([along.reshape(count, -1), three_flat.reshape(count, -1)], axis=1)
    width = packed.shape[1]
    full = -(-width // 1024) * 1024
    packed = jnp.pad(packed, ((0, 0), (0, full - width))).reshape(count, full // 128, 128)
    got = lax.all_to_all(packed, group, 0, 0, tiled=True).reshape(count, full)
    three = got[:, share * depth * rows : width].reshape(wide, depth, rank)
    got = got[:, : share * depth * rows].reshape(wide, narrow, share, depth, rows)
    first = jnp.where(core_at == 0, factor_one, factor_other)
    second = jnp.where(core_at == 0, factor_other, factor_one)
    one = jnp.stack([first, second])
    unfold = contract("wnbki,wkc->bcni", got, three)
    weights = contract("bcni,nia->bca", unfold, one)
    product = contract("bcni,bca->ani", unfold, weights).reshape(rank, narrow * rows)
    product = total(product)
    one_t = call(orthonormal_body, [product.shape], product)[0]

    one_pad = jnp.pad(one_t, ((0, spare), (0, 0)))
    one_own = lax.dynamic_slice_in_dim(one_pad, core_at * rows, rows, 1)
    one_other = lax.dynamic_slice_in_dim(one_pad, (1 - core_at) * rows, rows, 1)
    along = contract("ai,kij->akj", one_own, own) + contract("ai,kij->akj", one_other, other)
    got = lax.all_to_all(
        along.reshape(count, share * half * cols // 128, 128), group, 0, 0, tiled=True
    ).reshape(count, share, half, cols)
    three = three.reshape(count, half, rank)
    unfold = contract("dakj,dkc->acj", got, three)
    weights = contract("acj,jb->acb", unfold, factor_two)
    product = contract("acj,acb->bj", unfold, weights)
    product = total(product)
    two_t = call(orthonormal_body, [product.shape], product)[0]

    unfold = contract("dakj,bj->dakb", got, two_t)
    weights = contract("dakb,dkc->abc", unfold, three)
    product = contract("dakb,abc->cdk", unfold, weights).reshape(rank, count * half)
    product = total(product)
    three_t = call(orthonormal_body, [product.shape], product)[0]
    core = contract("dakb,cdk->abc", unfold, three_t.reshape(rank, count, half))
    core = core.reshape(share, count, rank * rank // count).transpose(1, 0, 2)
    core = lax.all_to_all(core, group, 0, 0, tiled=True)
    core = core.reshape(count * share, rank * rank // count)[:rank]
    basis_three = lax.dynamic_slice_in_dim(three_t, lax.axis_index("wide") * depth, depth, 1).T
    return (one_own[:rank].T, two_t.T, basis_three, core)


def pack_one(field, two_far, three_far, out, room, two, three, arrived, landed, *, share, half, count):
    chunks, _, steps, rows, cols = room.shape
    rank = two.shape[0]
    slots = share + 1

    def fetch(at, h):
        source = field.at[pl.ds(h * half + at * steps, steps)]
        return pltpu.make_async_copy(source, room.at[at, h], arrived.at[at, h])

    copies = [
        pltpu.make_async_copy(three_far, three, landed.at[0]),
        pltpu.make_async_copy(two_far, two, landed.at[1]),
    ]
    for copy in copies:
        copy.start()
    for at in range(chunks):
        for h in range(2):
            fetch(at, h).start()
    copies[0].wait()
    first = three[:half]
    second = three[half:]
    empty = jnp.zeros((half, lanes // 2 - rank), jnp.float32)
    both = jnp.concatenate([first, empty, second, empty], axis=1)
    for d in range(count):
        out[pl.ds(d * half * slots + share, half, stride=slots), :] = both
    copies[1].wait()
    two_high, two_low = split(two[...])
    both = jnp.concatenate([two_high, two_low])
    for at in range(chunks):
        for h in range(2):
            fetch(at, h).wait()
        for q in range(steps):
            high, low = split(room[at, :, q].reshape(2 * rows, cols))
            first = lax.dot_general(both, high, nt, preferred_element_type=jnp.float32)
            second = lax.dot_general(two_high, low, nt, preferred_element_type=jnp.float32)
            along = first[:rank] + (first[rank:] + second)
            for s in range(share):
                start = (at * steps + q) * slots + s
                out[pl.ds(start, count, stride=half * slots), :] = along[
                    s * count : (s + 1) * count
                ]


def work_one(got, own, other, out, three, *, share, half, count):
    rank = own.shape[1]
    slots = share + 1
    size = count * half
    at = lax.axis_index("narrow")
    low = jnp.where(at == 0, own[...], other[...])
    high = jnp.where(at == 0, other[...], own[...])
    one = jnp.concatenate([low, high])
    table = got[pl.ds(share, size, stride=slots), :]
    row = lax.broadcasted_iota(jnp.int32, (size, lanes), 0)
    odd = (row // half) % 2 == 1
    part = lanes // 2
    three[...] = jnp.where(odd, pltpu.roll(table, part, 1), table)[:, :rank]
    table = jnp.concatenate([jnp.where(odd, 0.0, table), jnp.where(odd, table, 0.0)], axis=1)
    table = split(table)
    lane = lax.broadcasted_iota(jnp.int32, (rank, lanes), 1)
    pieces = []
    for s in range(share):
        value = dot3(table, got[pl.ds(s, size, stride=slots), :], tn)
        first = value[:rank] + pltpu.roll(value[part : part + rank], part, 1)
        second = (
            pltpu.roll(value[2 * part : 2 * part + rank], part, 1)
            + value[3 * part : 3 * part + rank]
        )
        pieces.append(jnp.where(lane < part, first, second))
    unfold = split(jnp.concatenate(pieces))
    out[...] = dot3(dot3(unfold, one), unfold, tn)


def pack_two(part, field, other, basis, out, room, arrived, *, share, half, count):
    rows, cols = other.shape[1:]
    at = lax.axis_index("narrow")
    own = pltpu.make_async_copy(
        field.at[pl.ds(at * half, half)],
        room.at[:, pl.ds(pl.multiple_of(at * rows, 8), rows), :],
        arrived.at[0],
    )
    rest = pltpu.make_async_copy(
        other, room.at[:, pl.ds(pl.multiple_of((1 - at) * rows, 8), rows), :], arrived.at[1]
    )
    own.start()
    rest.start()
    value = orthonormal(part[...])
    basis[...] = value
    slots = share * (cols // lanes)
    value = split(value)
    both = jnp.concatenate(value)
    rank = part.shape[0]
    own.wait()
    rest.wait()
    for k in range(half):
        high, low = split(room[k])
        first = lax.dot_general(both, high, nn, preferred_element_type=jnp.float32)
        second = lax.dot_general(value[0], low, nn, preferred_element_type=jnp.float32)
        along = first[:rank] + (first[rank:] + second)
        for s in range(share):
            for h in range(cols // lanes):
                start = k * slots + s * (cols // lanes) + h
                out[pl.ds(start, count, stride=half * slots), :] = along[
                    s * count : (s + 1) * count, h * lanes : (h + 1) * lanes
                ]


def taken(got, s, parts, slots, size):
    return jnp.concatenate(
        [got[pl.ds(s * parts + h, size, stride=slots), :] for h in range(parts)], axis=1
    )


def work_two(got, two, three, out, *, share, half, count):
    parts = two.shape[0] // lanes
    size = count * half
    table = split(three[...])
    unfold = split(
        jnp.concatenate(
            [
                dot3(table, taken(got, s, parts, share * parts, size), tn)
                for s in range(share)
            ]
        )
    )
    out[...] = dot3(dot3(unfold, two[...]), unfold, tn)


def work_three(part, got, three, basis, out, sent, room, *, share, half, count):
    rank, cols = part.shape
    parts = cols // lanes
    size = count * half
    tall = -(-size // lanes)
    pitch = sent.shape[0] // count
    value = orthonormal(part[...])
    basis[...] = value
    for h in range(parts):
        room[h * rank : (h + 1) * rank, :] = value[:, h * lanes : (h + 1) * lanes]
    second = split(
        jnp.concatenate(
            [
                jnp.concatenate(
                    [room[pl.ds(h * rank + b, count, stride=share), :] for h in range(parts)],
                    axis=1,
                )
                for b in range(share)
            ]
        )
    )
    table = split(three[...])
    result = None
    for s in range(share):
        value = dot3(second, taken(got, s, parts, share * parts, size), nt)
        for b in range(share):
            for h in range(tall):
                wide = min(lanes, size - h * lanes)
                start = (b * share + s) * tall + h
                sent[pl.ds(start, count, stride=pitch), :wide] = value[
                    b * count : (b + 1) * count, h * lanes : h * lanes + wide
                ]
        value = split(value)
        term = dot3(dot3(value, table), value, tn)
        result = term if result is None else result + term
    out[...] = result


def finish(part, got, basis, core, room, *, share, half, count):
    rank, size = part.shape
    tall = -(-size // lanes)
    pitch = got.shape[0] // count
    value = orthonormal(part[...])
    room[...] = value.T
    depth = basis.shape[0]
    basis[...] = room[pl.ds(pl.multiple_of(lax.axis_index("wide") * depth, 8), depth), :]
    value = split(value)
    for b in range(share):
        rows = []
        for s in range(share):
            pieces = []
            for h in range(tall):
                wide = min(lanes, size - h * lanes)
                start = (b * share + s) * tall + h
                pieces.append(got[pl.ds(start, count, stride=pitch), :][:, :wide])
            rows.append(jnp.concatenate(pieces, axis=1))
        core[:, b * rank : (b + 1) * rank] = dot3(jnp.concatenate(rows), value, nt)


def exchange(value, count):
    rows = value.shape[0]
    value = value.reshape(count, rows // count, lanes)
    return lax.all_to_all(value, group, 0, 0, tiled=True).reshape(rows, lanes)


def special(window_data, factor_one, factor_two, factor_three):
    wide = lax.axis_size("wide")
    count = wide * lax.axis_size("narrow")
    depth, rows, cols = window_data.shape
    rank = factor_one.shape[1]
    share = rank // count
    half = depth // 2
    size = count * half
    facts = {"share": share, "half": half, "count": count}
    core_at = lax.axis_index("narrow")

    def stage(body):
        def run(*refs):
            body(*refs, **facts)

        run.__name__ = body.__name__
        return run

    chunks = 3 if half % 3 == 0 else 1
    slots = share + 1
    (packed,) = call(
        stage(pack_one),
        [(size * slots, lanes)],
        window_data,
        factor_two.T,
        factor_three,
        far=(0, 1, 2),
        scratch_shapes=[
            pltpu.VMEM((chunks, 2, half // chunks, rows, cols), jnp.float32),
            pltpu.VMEM((rank, cols), jnp.float32),
            pltpu.VMEM((depth, rank), jnp.float32),
            pltpu.SemaphoreType.DMA((chunks, 2)),
            pltpu.SemaphoreType.DMA((2,)),
        ],
    )
    got = exchange(packed, count)
    field, _ = lax.optimization_barrier((window_data, packed))
    other = swap(lax.dynamic_slice_in_dim(field, (1 - core_at) * half, half, 0))
    got, other = lax.optimization_barrier((got, other))
    product, three = call(
        stage(work_one), [(rank, 2 * rows), (size, rank)], got, factor_one, swap(factor_one)
    )
    product = total(product)

    parts = cols // lanes
    one_t, packed = call(
        stage(pack_two),
        [product.shape, (size * share * parts, lanes)],
        product,
        window_data,
        other,
        far=(1, 2),
        scratch_shapes=[
            pltpu.VMEM((half, 2 * rows, cols), jnp.float32),
            pltpu.SemaphoreType.DMA((2,)),
        ],
    )
    got = exchange(packed, count)
    (product,) = call(stage(work_two), [(rank, cols)], got, factor_two, three)
    product = total(product)

    pitch = -(-share * share * -(-size // lanes) // 8) * 8
    two_t, product, sent = call(
        stage(work_three),
        [product.shape, (rank, size), (count * pitch, lanes)],
        product,
        got,
        three,
        scratch_shapes=[pltpu.VMEM((parts * rank, lanes), jnp.float32)],
    )
    got = exchange(sent, count)
    product = total(product)
    basis_three, core = call(
        stage(finish),
        [(depth, rank), (rank, share * rank)],
        product,
        got,
        out_far=True,
        scratch_shapes=[pltpu.VMEM((size, rank), jnp.float32)],
    )
    basis_one = lax.dynamic_slice_in_dim(one_t, core_at * rows, rows, 1).T
    return (basis_one, two_t.T, basis_three, core)


def on_device(window_data, factor_one, factor_two, factor_three):
    count = lax.axis_size("wide") * lax.axis_size("narrow")
    depth, rows, cols = window_data.shape
    rank = factor_one.shape[1]
    fits = (
        lax.axis_size("narrow") == 2
        and rank % count == 0
        and count % 8 == 0
        and depth % 8 == 0
        and (depth // 2) * (rank // count + 1) % 8 == 0
        and (depth // 2) * (rank // count) * (cols // lanes) % 8 == 0
        and 2 * rows == lanes
        and 2 * rank <= lanes
        and cols % lanes == 0
    )
    return (special if fits else general)(window_data, factor_one, factor_two, factor_three)


def solution(mesh):
    return jax.shard_map(
        on_device,
        mesh=mesh,
        in_specs=(
            P(("win", "wide"), "narrow", None),
            P(("win", "narrow"), None),
            P("win", None),
            P(("win", "wide"), None),
        ),
        out_specs=(
            P(("win", "narrow"), None),
            P("win", None),
            P(("win", "wide"), None),
            P(None, ("win", "wide", "narrow")),
        ),
        check_vma=False,
    )
```

```python
import jax
import jax.numpy as jnp
from jax import lax
from jax.experimental import pallas as pl
from jax.experimental.pallas import tpu as pltpu
from jax.sharding import PartitionSpec as P

highest = lax.Precision.HIGHEST
fine = lax.Precision.HIGH
group = ("wide", "narrow")
lanes = 128
nn = (((1,), (0,)), ((), ()))
nt = (((1,), (1,)), ((), ()))
tn = (((0,), (0,)), ((), ()))


def contract(form, left, right, precision=fine):
    return jnp.einsum(form, left, right, precision=precision)


def total(part):
    narrow = lax.axis_size("narrow")
    count = lax.axis_size("wide") * narrow
    if narrow != 2 or count & (count - 1):
        return lax.psum(part, group)

    def moved(mask):
        return lax.ppermute(part, group, [(at, at ^ mask) for at in range(count)])

    part = part + moved(1)
    bits = []
    while narrow < count:
        bits.append(narrow)
        narrow *= 2
    single = len(bits) % 2
    parts = [bits[:single]] if single else []
    parts += [bits[at : at + 2] for at in range(single, len(bits), 2)]
    for low, *high in parts:
        if high:
            near, far, both = moved(low + 1), moved(high[0] + 1), moved(low + high[0] + 1)
            part = (part + near) + (far + both)
        else:
            part = part + moved(low + 1)
    return part


def swap(value):
    return lax.ppermute(value, "narrow", [(0, 1), (1, 0)])


def dot(left, right, dims=nn):
    return lax.dot_general(
        left, right, dims, precision=highest, preferred_element_type=jnp.float32
    )


def split(value):
    high = value.astype(jnp.bfloat16)
    return high, (value - high.astype(jnp.float32)).astype(jnp.bfloat16)


def dot3(left, right, dims=nn):
    left_high, left_low = left if isinstance(left, tuple) else split(left)
    right_high, right_low = right if isinstance(right, tuple) else split(right)

    def one(a, b):
        return lax.dot_general(a, b, dims, preferred_element_type=jnp.float32)

    return one(left_high, right_high) + (one(left_high, right_low) + one(left_low, right_high))


def eliminate(table, rank):
    width = table.shape[1]
    row = lax.broadcasted_iota(jnp.int32, (8, width), 0)
    tiles = [table[8 * at : 8 * at + 8] for at in range(rank // 8)]
    for at in range(rank // 8):
        live = tiles[at:]
        columns = [
            [jnp.broadcast_to(x[:, 8 * at + k : 8 * at + k + 1], (8, width)) for x in live]
            for k in range(8)
        ]
        for j in range(8):
            heads = [jnp.broadcast_to(columns[k][0][j : j + 1], (8, width)) for k in range(j, 8)]
            inverse = 1.0 / heads[0]
            scale = [x * inverse for x in columns[j]]
            scale[0] = jnp.where(row > j, scale[0], 0.0)
            for k in range(j + 1, 8):
                columns[k] = [x - y * heads[k - j] for x, y in zip(columns[k], scale)]
            lead = jnp.broadcast_to(live[0][j : j + 1], (8, width))
            live = [x - y * lead for x, y in zip(live, scale)]
        tiles[at:] = live
    return jnp.concatenate(tiles, axis=0)


def orthonormal(part):
    rank, size = part.shape
    width = -(-2 * rank // lanes) * lanes
    below = jnp.zeros((width - rank, size), part.dtype)
    gram = dot(part, jnp.concatenate([part, below]), nt)
    row = lax.broadcasted_iota(jnp.int32, (rank, width), 0)
    lane = lax.broadcasted_iota(jnp.int32, (rank, width), 1)
    table = eliminate(jnp.where(lane == row + rank, 1.0, gram), rank)
    pivots = jnp.sum(jnp.where(lane == row, table, 0.0), axis=1, keepdims=True)
    table = jnp.where(lane < rank, 0.0, table * lax.rsqrt(pivots))
    padded = [jnp.zeros((rank, size), part.dtype), part]
    if width > 2 * rank:
        padded.append(jnp.zeros((width - 2 * rank, size), part.dtype))
    return dot(table, jnp.concatenate(padded))


def orthonormal_body(part, out):
    out[...] = orthonormal(part[...])


def near(*shape, dtype=jnp.float32):
    return pltpu.VMEM(shape, dtype)


def far(*shape, dtype=jnp.float32):
    return jax.ShapeDtypeStruct(shape, dtype)


def call(body, shapes, *operands, away=(), away_out=(), **settings):
    inside = pl.BlockSpec(memory_space=pltpu.VMEM)
    outside = pl.BlockSpec(memory_space=pl.ANY)
    placed = [
        x if at in away else pltpu.with_memory_space_constraint(x, pltpu.VMEM)
        for at, x in enumerate(operands)
    ]
    return pl.pallas_call(
        body,
        in_specs=[outside if at in away else inside for at in range(len(operands))],
        out_specs=[outside if at in away_out else inside for at in range(len(shapes))],
        out_shape=shapes,
        **settings,
    )(*placed)


def general(window_data, factor_one, factor_two, factor_three):
    wide = lax.axis_size("wide")
    narrow = lax.axis_size("narrow")
    count = wide * narrow
    depth, rows, cols = window_data.shape
    rank = factor_one.shape[1]
    share = -(-rank // count)
    spare = share * count - rank
    half = depth // narrow
    core_at = lax.axis_index("narrow")

    own = lax.dynamic_slice_in_dim(window_data, core_at * half, half, 0)
    sent = lax.dynamic_slice_in_dim(window_data, (1 - core_at) * half, half, 0)
    other = swap(sent)
    factor_other = swap(factor_one)

    two_t = jnp.pad(factor_two.T, ((0, spare), (0, 0)))
    along = contract("bj,kij->bki", two_t, window_data).reshape(count, share, depth * rows)
    three_own = lax.dynamic_slice_in_dim(factor_three, core_at * half, half, 0)
    three_flat = jnp.broadcast_to(three_own.reshape(1, 1, half * rank), (count, 1, half * rank))
    packed = jnp.concatenate([along.reshape(count, -1), three_flat.reshape(count, -1)], axis=1)
    width = packed.shape[1]
    full = -(-width // 1024) * 1024
    packed = jnp.pad(packed, ((0, 0), (0, full - width))).reshape(count, full // 128, 128)
    got = lax.all_to_all(packed, group, 0, 0, tiled=True).reshape(count, full)
    three = got[:, share * depth * rows : width].reshape(wide, depth, rank)
    got = got[:, : share * depth * rows].reshape(wide, narrow, share, depth, rows)
    first = jnp.where(core_at == 0, factor_one, factor_other)
    second = jnp.where(core_at == 0, factor_other, factor_one)
    one = jnp.stack([first, second])
    unfold = contract("wnbki,wkc->bcni", got, three)
    weights = contract("bcni,nia->bca", unfold, one)
    product = contract("bcni,bca->ani", unfold, weights).reshape(rank, narrow * rows)
    product = total(product)
    one_t = call(orthonormal_body, [near(*product.shape)], product)[0]

    one_pad = jnp.pad(one_t, ((0, spare), (0, 0)))
    one_own = lax.dynamic_slice_in_dim(one_pad, core_at * rows, rows, 1)
    one_other = lax.dynamic_slice_in_dim(one_pad, (1 - core_at) * rows, rows, 1)
    along = contract("ai,kij->akj", one_own, own) + contract("ai,kij->akj", one_other, other)
    got = lax.all_to_all(
        along.reshape(count, share * half * cols // 128, 128), group, 0, 0, tiled=True
    ).reshape(count, share, half, cols)
    three = three.reshape(count, half, rank)
    unfold = contract("dakj,dkc->acj", got, three)
    weights = contract("acj,jb->acb", unfold, factor_two)
    product = contract("acj,acb->bj", unfold, weights)
    product = total(product)
    two_t = call(orthonormal_body, [near(*product.shape)], product)[0]

    unfold = contract("dakj,bj->dakb", got, two_t)
    weights = contract("dakb,dkc->abc", unfold, three)
    product = contract("dakb,abc->cdk", unfold, weights).reshape(rank, count * half)
    product = total(product)
    three_t = call(orthonormal_body, [near(*product.shape)], product)[0]
    core = contract("dakb,cdk->abc", unfold, three_t.reshape(rank, count, half))
    core = core.reshape(share, count, rank * rank // count).transpose(1, 0, 2)
    core = lax.all_to_all(core, group, 0, 0, tiled=True)
    core = core.reshape(count * share, rank * rank // count)[:rank]
    basis_three = lax.dynamic_slice_in_dim(three_t, lax.axis_index("wide") * depth, depth, 1).T
    return (one_own[:rank].T, two_t.T, basis_three, core)


def pack_one(field, two_far, three_far, out, sent, room, flat, two, three, sems, *, share, half, count):
    chunks, _, steps, rows, cols = room.shape
    rank = two.shape[0]
    slots = share + 1
    at_core = lax.axis_index("narrow")
    tall = steps * slots

    def fetch(at, h):
        source = field.at[pl.ds(h * half + at * steps, steps)]
        return pltpu.make_async_copy(source, room.at[at, h], sems.at[2 * at + h])

    def leave(at):
        source = flat.reshape(count, half * slots, lanes).at[:, at * tall : (at + 1) * tall]
        return pltpu.make_async_copy(
            source, out.at[:, at * tall : (at + 1) * tall], sems.at[2 * chunks + at]
        )

    def hand(at):
        target = sent.at[pl.ds(at * steps, steps)]
        return pltpu.make_async_copy(room.at[at, 1 - at_core], target, sems.at[3 * chunks + at])

    copies = [
        pltpu.make_async_copy(three_far, three, sems.at[4 * chunks]),
        pltpu.make_async_copy(two_far, two, sems.at[4 * chunks + 1]),
    ]
    for copy in copies:
        copy.start()
    for at in range(chunks):
        for h in range(2):
            fetch(at, h).start()
    copies[0].wait()
    first = three[:half]
    second = three[half:]
    empty = jnp.zeros((half, lanes // 2 - rank), jnp.float32)
    both = jnp.concatenate([first, empty, second, empty], axis=1)
    for d in range(count):
        flat[pl.ds(d * half * slots + share, half, stride=slots), :] = both
    copies[1].wait()
    two_high, two_low = split(two[...])
    both = jnp.concatenate([two_high, two_low])
    for at in range(chunks):
        for h in range(2):
            fetch(at, h).wait()
        hand(at).start()
        for q in range(steps):
            high, low = split(room[at, :, q].reshape(2 * rows, cols))
            first = lax.dot_general(both, high, nt, preferred_element_type=jnp.float32)
            second = lax.dot_general(two_high, low, nt, preferred_element_type=jnp.float32)
            along = first[:rank] + (first[rank:] + second)
            for s in range(share):
                start = (at * steps + q) * slots + s
                flat[pl.ds(start, count, stride=half * slots), :] = along[
                    s * count : (s + 1) * count
                ]
        leave(at).start()
    for at in range(chunks):
        hand(at).wait()
        leave(at).wait()


def prepare(field, other, high, low, own, sem):
    half, rows, cols = other.shape
    at = lax.axis_index("narrow")
    copy = pltpu.make_async_copy(field.at[pl.ds(at * half, half)], own, sem)
    copy.start()

    def put(value, core):
        top, rest = split(value[...])
        high[:, pl.ds(pl.multiple_of(core * rows, 16), rows), :] = top
        low[:, pl.ds(pl.multiple_of(core * rows, 16), rows), :] = rest

    put(other, 1 - at)
    copy.wait()
    put(own, at)


def work_one(got, own, other, out, three, *, share, half, count):
    rank = own.shape[1]
    slots = share + 1
    size = count * half
    at = lax.axis_index("narrow")
    low = jnp.where(at == 0, own[...], other[...])
    high = jnp.where(at == 0, other[...], own[...])
    one = jnp.concatenate([low, high])
    table = got[pl.ds(share, size, stride=slots), :]
    row = lax.broadcasted_iota(jnp.int32, (size, lanes), 0)
    odd = (row // half) % 2 == 1
    part = lanes // 2
    three[...] = jnp.where(odd, pltpu.roll(table, part, 1), table)[:, :rank]
    table = jnp.concatenate([jnp.where(odd, 0.0, table), jnp.where(odd, table, 0.0)], axis=1)
    table = split(table)
    lane = lax.broadcasted_iota(jnp.int32, (rank, lanes), 1)
    pieces = []
    for s in range(share):
        value = dot3(table, got[pl.ds(s, size, stride=slots), :], tn)
        first = value[:rank] + pltpu.roll(value[part : part + rank], part, 1)
        second = (
            pltpu.roll(value[2 * part : 2 * part + rank], part, 1)
            + value[3 * part : 3 * part + rank]
        )
        pieces.append(jnp.where(lane < part, first, second))
    unfold = split(jnp.concatenate(pieces))
    out[...] = dot3(dot3(unfold, one), unfold, tn)


def pack_two(part, high, low, basis, out, flat, sems, *, share, half, count):
    rank = part.shape[0]
    parts = high.shape[2] // lanes
    slots = share * parts
    chunks = sems.shape[0]
    tall = half // chunks * slots

    def leave(at):
        source = flat.reshape(count, half * slots, lanes).at[:, at * tall : (at + 1) * tall]
        return pltpu.make_async_copy(source, out.at[:, at * tall : (at + 1) * tall], sems.at[at])

    value = orthonormal(part[...])
    basis[...] = value
    value = split(value)
    both = jnp.concatenate(value)
    for at in range(chunks):
        for k in range(at * half // chunks, (at + 1) * half // chunks):
            first = lax.dot_general(both, high[k], nn, preferred_element_type=jnp.float32)
            second = lax.dot_general(value[0], low[k], nn, preferred_element_type=jnp.float32)
            along = first[:rank] + (first[rank:] + second)
            for s in range(share):
                for h in range(parts):
                    start = k * slots + s * parts + h
                    flat[pl.ds(start, count, stride=half * slots), :] = along[
                        s * count : (s + 1) * count, h * lanes : (h + 1) * lanes
                    ]
        leave(at).start()
    for at in range(chunks):
        leave(at).wait()


def taken(got, s, parts, slots, size):
    return jnp.concatenate(
        [got[pl.ds(s * parts + h, size, stride=slots), :] for h in range(parts)], axis=1
    )


def work_two(got, two, three, out, high, low, *, share, half, count):
    parts = two.shape[0] // lanes
    size = count * half
    table = split(three[...])
    pieces = []
    for s in range(share):
        value = split(taken(got, s, parts, share * parts, size))
        high[s], low[s] = value
        pieces.append(dot3(table, value, tn))
    unfold = split(jnp.concatenate(pieces))
    out[...] = dot3(dot3(unfold, two[...]), unfold, tn)


def work_three(part, high, low, three, basis, out, sent, room, *, share, half, count):
    rank, cols = part.shape
    parts = cols // lanes
    size = count * half
    tall = -(-size // lanes)
    pitch = sent.shape[0] // count
    value = orthonormal(part[...])
    basis[...] = value
    for h in range(parts):
        room[h * rank : (h + 1) * rank, :] = value[:, h * lanes : (h + 1) * lanes]
    second = split(
        jnp.concatenate(
            [
                jnp.concatenate(
                    [room[pl.ds(h * rank + b, count, stride=share), :] for h in range(parts)],
                    axis=1,
                )
                for b in range(share)
            ]
        )
    )
    table = split(three[...])
    result = None
    for s in range(share):
        value = dot3(second, (high[s], low[s]), nt)
        for b in range(share):
            for h in range(tall):
                wide = min(lanes, size - h * lanes)
                start = (b * share + s) * tall + h
                sent[pl.ds(start, count, stride=pitch), :wide] = value[
                    b * count : (b + 1) * count, h * lanes : h * lanes + wide
                ]
        value = split(value)
        term = dot3(dot3(value, table), value, tn)
        result = term if result is None else result + term
    out[...] = result


def finish(part, got, basis, core, room, *, share, half, count):
    rank, size = part.shape
    tall = -(-size // lanes)
    pitch = got.shape[0] // count
    value = orthonormal(part[...])
    room[...] = value.T
    depth = basis.shape[0]
    basis[...] = room[pl.ds(pl.multiple_of(lax.axis_index("wide") * depth, 8), depth), :]
    value = split(value)
    for b in range(share):
        rows = []
        for s in range(share):
            pieces = []
            for h in range(tall):
                wide = min(lanes, size - h * lanes)
                start = (b * share + s) * tall + h
                pieces.append(got[pl.ds(start, count, stride=pitch), :][:, :wide])
            rows.append(jnp.concatenate(pieces, axis=1))
        core[:, b * rank : (b + 1) * rank] = dot3(jnp.concatenate(rows), value, nt)


def exchange(value):
    count, rows, _ = value.shape
    return lax.all_to_all(value, group, 0, 0, tiled=True).reshape(count * rows, lanes)


def special(window_data, factor_one, factor_two, factor_three):
    wide = lax.axis_size("wide")
    count = wide * lax.axis_size("narrow")
    depth, rows, cols = window_data.shape
    rank = factor_one.shape[1]
    share = rank // count
    half = depth // 2
    size = count * half
    facts = {"share": share, "half": half, "count": count}
    core_at = lax.axis_index("narrow")

    def stage(body):
        def run(*refs):
            body(*refs, **facts)

        run.__name__ = body.__name__
        return run

    slots = share + 1
    parts = cols // lanes
    chunks = 3 if half % 3 == 0 and half // 3 * slots % 8 == 0 else 1
    packed, sent = call(
        stage(pack_one),
        [far(count, half * slots, lanes), far(half, rows, cols)],
        window_data,
        factor_two.T,
        factor_three,
        away=(0, 1, 2),
        away_out=(0, 1),
        scratch_shapes=[
            near(chunks, 2, half // chunks, rows, cols),
            near(size * slots, lanes),
            near(rank, cols),
            near(depth, rank),
            pltpu.SemaphoreType.DMA((4 * chunks + 2,)),
        ],
    )
    got = exchange(packed)
    high, low = call(
        prepare,
        [near(half, 2 * rows, cols, dtype=jnp.bfloat16)] * 2,
        window_data,
        swap(sent),
        away=(0,),
        scratch_shapes=[near(half, rows, cols), pltpu.SemaphoreType.DMA],
    )
    one_other = swap(factor_one)
    got, high, low = lax.optimization_barrier((got, high, low))
    product, three = call(
        stage(work_one), [near(rank, 2 * rows), near(size, rank)], got, factor_one, one_other
    )
    product = total(product)

    chunks = 3 if half % 3 == 0 and half // 3 * share * parts % 8 == 0 else 1
    one_t, packed = call(
        stage(pack_two),
        [near(*product.shape), far(count, half * share * parts, lanes)],
        product,
        high,
        low,
        away_out=(1,),
        scratch_shapes=[
            near(size * share * parts, lanes),
            pltpu.SemaphoreType.DMA((chunks,)),
        ],
    )
    got = exchange(packed)
    product, high, low = call(
        stage(work_two),
        [near(rank, cols)] + [near(share, size, cols, dtype=jnp.bfloat16)] * 2,
        got,
        factor_two,
        three,
    )
    product = total(product)

    pitch = -(-share * share * -(-size // lanes) // 8) * 8
    two_t, product, sent = call(
        stage(work_three),
        [near(*product.shape), near(rank, size), far(count * pitch, lanes)],
        product,
        high,
        low,
        three,
        scratch_shapes=[near(parts * rank, lanes)],
    )
    got = exchange(sent.reshape(count, pitch, lanes))
    product = total(product)
    basis_three, core = call(
        stage(finish),
        [far(depth, rank), far(rank, share * rank)],
        product,
        got,
        scratch_shapes=[near(size, rank)],
    )
    basis_one = lax.dynamic_slice_in_dim(one_t, core_at * rows, rows, 1).T
    return (basis_one, two_t.T, basis_three, core)


def on_device(window_data, factor_one, factor_two, factor_three):
    count = lax.axis_size("wide") * lax.axis_size("narrow")
    depth, rows, cols = window_data.shape
    rank = factor_one.shape[1]
    fits = (
        lax.axis_size("narrow") == 2
        and rank % count == 0
        and count % 8 == 0
        and depth % 8 == 0
        and (depth // 2) * (rank // count + 1) % 8 == 0
        and (depth // 2) * (rank // count) * (cols // lanes) % 8 == 0
        and 2 * rows == lanes
        and 2 * rank <= lanes
        and cols % lanes == 0
    )
    return (special if fits else general)(window_data, factor_one, factor_two, factor_three)


def solution(mesh):
    return jax.shard_map(
        on_device,
        mesh=mesh,
        in_specs=(
            P(("win", "wide"), "narrow", None),
            P(("win", "narrow"), None),
            P("win", None),
            P(("win", "wide"), None),
        ),
        out_specs=(
            P(("win", "narrow"), None),
            P("win", None),
            P(("win", "wide"), None),
            P(None, ("win", "wide", "narrow")),
        ),
        check_vma=False,
    )
```

```python
import jax
import jax.numpy as jnp
from jax import lax
from jax.experimental import pallas as pl
from jax.experimental.pallas import tpu as pltpu
from jax.sharding import PartitionSpec as P

highest = lax.Precision.HIGHEST
fine = lax.Precision.HIGH
group = ("wide", "narrow")
lanes = 128
nn = (((1,), (0,)), ((), ()))
nt = (((1,), (1,)), ((), ()))
tn = (((0,), (0,)), ((), ()))


def contract(form, left, right, precision=fine):
    return jnp.einsum(form, left, right, precision=precision)


def total(part):
    narrow = lax.axis_size("narrow")
    count = lax.axis_size("wide") * narrow
    if narrow != 2 or count & (count - 1):
        return lax.psum(part, group)

    def moved(mask):
        return lax.ppermute(part, group, [(at, at ^ mask) for at in range(count)])

    part = part + moved(1)
    bits = []
    while narrow < count:
        bits.append(narrow)
        narrow *= 2
    parts = [bits[-1:]] if len(bits) % 2 else []
    parts += [bits[at : at + 2] for at in range(0, len(bits) - 1, 2)]
    for low, *high in parts:
        if high:
            near_sum, far_sum = moved(low + 1), moved(high[0] + 1)
            part = (part + near_sum) + (far_sum + moved(low + high[0] + 1))
        else:
            part = part + moved(low + 1)
    return part


def swap(value):
    return lax.ppermute(value, "narrow", [(0, 1), (1, 0)])


def dot(left, right, dims=nn):
    return lax.dot_general(
        left, right, dims, precision=highest, preferred_element_type=jnp.float32
    )


def split(value):
    high = value.astype(jnp.bfloat16)
    return high, (value - high.astype(jnp.float32)).astype(jnp.bfloat16)


def dot3(left, right, dims=nn):
    left_high, left_low = left if isinstance(left, tuple) else split(left)
    right_high, right_low = right if isinstance(right, tuple) else split(right)

    def one(a, b):
        return lax.dot_general(a, b, dims, preferred_element_type=jnp.float32)

    return one(left_high, right_high) + (one(left_high, right_low) + one(left_low, right_high))


def eliminate(table, rank):
    width = table.shape[1]
    row = lax.broadcasted_iota(jnp.int32, (8, width), 0)
    tiles = [table[8 * at : 8 * at + 8] for at in range(rank // 8)]
    for at in range(rank // 8):
        live = tiles[at:]
        columns = [
            [jnp.broadcast_to(x[:, 8 * at + k : 8 * at + k + 1], (8, width)) for x in live]
            for k in range(8)
        ]
        for j in range(8):
            heads = [jnp.broadcast_to(columns[k][0][j : j + 1], (8, width)) for k in range(j, 8)]
            inverse = 1.0 / heads[0]
            scale = [x * inverse for x in columns[j]]
            scale[0] = jnp.where(row > j, scale[0], 0.0)
            for k in range(j + 1, 8):
                columns[k] = [x - y * heads[k - j] for x, y in zip(columns[k], scale)]
            lead = jnp.broadcast_to(live[0][j : j + 1], (8, width))
            live = [x - y * lead for x, y in zip(live, scale)]
        tiles[at:] = live
    return jnp.concatenate(tiles, axis=0)


def orthonormal(part):
    rank, size = part.shape
    width = -(-2 * rank // lanes) * lanes
    below = jnp.zeros((width - rank, size), part.dtype)
    gram = dot(part, jnp.concatenate([part, below]), nt)
    row = lax.broadcasted_iota(jnp.int32, (rank, width), 0)
    lane = lax.broadcasted_iota(jnp.int32, (rank, width), 1)
    table = eliminate(jnp.where(lane == row + rank, 1.0, gram), rank)
    pivots = jnp.sum(jnp.where(lane == row, table, 0.0), axis=1, keepdims=True)
    table = jnp.where(lane < rank, 0.0, table * lax.rsqrt(pivots))
    padded = [jnp.zeros((rank, size), part.dtype), part]
    if width > 2 * rank:
        padded.append(jnp.zeros((width - 2 * rank, size), part.dtype))
    return dot(table, jnp.concatenate(padded))


def orthonormal_body(part, out):
    out[...] = orthonormal(part[...])


def near(*shape, dtype=jnp.float32):
    return pltpu.VMEM(shape, dtype)


def far(*shape, dtype=jnp.float32):
    return jax.ShapeDtypeStruct(shape, dtype)


def call(body, shapes, *operands, away=(), away_out=(), **settings):
    inside = pl.BlockSpec(memory_space=pltpu.VMEM)
    outside = pl.BlockSpec(memory_space=pl.ANY)
    placed = [
        x if at in away else pltpu.with_memory_space_constraint(x, pltpu.VMEM)
        for at, x in enumerate(operands)
    ]
    return pl.pallas_call(
        body,
        in_specs=[outside if at in away else inside for at in range(len(operands))],
        out_specs=[outside if at in away_out else inside for at in range(len(shapes))],
        out_shape=shapes,
        **settings,
    )(*placed)


def general(window_data, factor_one, factor_two, factor_three):
    wide = lax.axis_size("wide")
    narrow = lax.axis_size("narrow")
    count = wide * narrow
    depth, rows, cols = window_data.shape
    rank = factor_one.shape[1]
    share = -(-rank // count)
    spare = share * count - rank
    half = depth // narrow
    core_at = lax.axis_index("narrow")

    own = lax.dynamic_slice_in_dim(window_data, core_at * half, half, 0)
    sent = lax.dynamic_slice_in_dim(window_data, (1 - core_at) * half, half, 0)
    other = swap(sent)
    factor_other = swap(factor_one)

    two_t = jnp.pad(factor_two.T, ((0, spare), (0, 0)))
    along = contract("bj,kij->bki", two_t, window_data).reshape(count, share, depth * rows)
    three_own = lax.dynamic_slice_in_dim(factor_three, core_at * half, half, 0)
    three_flat = jnp.broadcast_to(three_own.reshape(1, 1, half * rank), (count, 1, half * rank))
    packed = jnp.concatenate([along.reshape(count, -1), three_flat.reshape(count, -1)], axis=1)
    width = packed.shape[1]
    full = -(-width // 1024) * 1024
    packed = jnp.pad(packed, ((0, 0), (0, full - width))).reshape(count, full // 128, 128)
    got = lax.all_to_all(packed, group, 0, 0, tiled=True).reshape(count, full)
    three = got[:, share * depth * rows : width].reshape(wide, depth, rank)
    got = got[:, : share * depth * rows].reshape(wide, narrow, share, depth, rows)
    first = jnp.where(core_at == 0, factor_one, factor_other)
    second = jnp.where(core_at == 0, factor_other, factor_one)
    one = jnp.stack([first, second])
    unfold = contract("wnbki,wkc->bcni", got, three)
    weights = contract("bcni,nia->bca", unfold, one)
    product = contract("bcni,bca->ani", unfold, weights).reshape(rank, narrow * rows)
    product = total(product)
    one_t = call(orthonormal_body, [near(*product.shape)], product)[0]

    one_pad = jnp.pad(one_t, ((0, spare), (0, 0)))
    one_own = lax.dynamic_slice_in_dim(one_pad, core_at * rows, rows, 1)
    one_other = lax.dynamic_slice_in_dim(one_pad, (1 - core_at) * rows, rows, 1)
    along = contract("ai,kij->akj", one_own, own) + contract("ai,kij->akj", one_other, other)
    got = lax.all_to_all(
        along.reshape(count, share * half * cols // 128, 128), group, 0, 0, tiled=True
    ).reshape(count, share, half, cols)
    three = three.reshape(count, half, rank)
    unfold = contract("dakj,dkc->acj", got, three)
    weights = contract("acj,jb->acb", unfold, factor_two)
    product = contract("acj,acb->bj", unfold, weights)
    product = total(product)
    two_t = call(orthonormal_body, [near(*product.shape)], product)[0]

    unfold = contract("dakj,bj->dakb", got, two_t)
    weights = contract("dakb,dkc->abc", unfold, three)
    product = contract("dakb,abc->cdk", unfold, weights).reshape(rank, count * half)
    product = total(product)
    three_t = call(orthonormal_body, [near(*product.shape)], product)[0]
    core = contract("dakb,cdk->abc", unfold, three_t.reshape(rank, count, half))
    core = core.reshape(share, count, rank * rank // count).transpose(1, 0, 2)
    core = lax.all_to_all(core, group, 0, 0, tiled=True)
    core = core.reshape(count * share, rank * rank // count)[:rank]
    basis_three = lax.dynamic_slice_in_dim(three_t, lax.axis_index("wide") * depth, depth, 1).T
    return (one_own[:rank].T, two_t.T, basis_three, core)


def pack_one(field, two_far, three_far, out, sent, room, flat, two, three, sems, *, share, half, count):
    chunks, _, steps, rows, cols = room.shape
    rank = two.shape[0]
    slots = share + 1
    at_core = lax.axis_index("narrow")
    tall = steps * slots

    def fetch(at, h):
        source = field.at[pl.ds(h * half + at * steps, steps)]
        return pltpu.make_async_copy(source, room.at[at, h], sems.at[2 * at + h])

    def leave(at):
        source = flat.reshape(count, half * slots, lanes).at[:, at * tall : (at + 1) * tall]
        return pltpu.make_async_copy(
            source, out.at[:, at * tall : (at + 1) * tall], sems.at[2 * chunks + at]
        )

    def hand(at):
        target = sent.at[pl.ds(at * steps, steps)]
        return pltpu.make_async_copy(room.at[at, 1 - at_core], target, sems.at[3 * chunks + at])

    copies = [
        pltpu.make_async_copy(three_far, three, sems.at[4 * chunks]),
        pltpu.make_async_copy(two_far, two, sems.at[4 * chunks + 1]),
    ]
    for copy in copies:
        copy.start()
    for at in range(chunks):
        for h in range(2):
            fetch(at, h).start()
    copies[0].wait()
    first = three[:half]
    second = three[half:]
    empty = jnp.zeros((half, lanes // 2 - rank), jnp.float32)
    both = jnp.concatenate([first, empty, second, empty], axis=1)
    for d in range(count):
        flat[pl.ds(d * half * slots + share, half, stride=slots), :] = both
    copies[1].wait()
    two_high, two_low = split(two[...])
    both = jnp.concatenate([two_high, two_low])
    for at in range(chunks):
        for h in range(2):
            fetch(at, h).wait()
        hand(at).start()
        for q in range(steps):
            high, low = split(room[at, :, q].reshape(2 * rows, cols))
            first = lax.dot_general(both, high, nt, preferred_element_type=jnp.float32)
            second = lax.dot_general(two_high, low, nt, preferred_element_type=jnp.float32)
            along = first[:rank] + (first[rank:] + second)
            for s in range(share):
                start = (at * steps + q) * slots + s
                flat[pl.ds(start, count, stride=half * slots), :] = along[
                    s * count : (s + 1) * count
                ]
        leave(at).start()
    for at in range(chunks):
        hand(at).wait()
        leave(at).wait()


def prepare(field, other, high, low, own, sem):
    half, rows, cols = other.shape
    at = lax.axis_index("narrow")
    copy = pltpu.make_async_copy(field.at[pl.ds(at * half, half)], own, sem)
    copy.start()

    def put(value, core):
        top, rest = split(value[...])
        high[:, pl.ds(pl.multiple_of(core * rows, 16), rows), :] = top
        low[:, pl.ds(pl.multiple_of(core * rows, 16), rows), :] = rest

    put(other, 1 - at)
    copy.wait()
    put(own, at)


def work_one(got, own, other, out, three, *, share, half, count):
    rank = own.shape[1]
    slots = share + 1
    size = count * half
    at = lax.axis_index("narrow")
    low = jnp.where(at == 0, own[...], other[...])
    high = jnp.where(at == 0, other[...], own[...])
    one = jnp.concatenate([low, high])
    table = got[pl.ds(share, size, stride=slots), :]
    row = lax.broadcasted_iota(jnp.int32, (size, lanes), 0)
    odd = (row // half) % 2 == 1
    part = lanes // 2
    three[...] = jnp.where(odd, pltpu.roll(table, part, 1), table)[:, :rank]
    table = jnp.concatenate([jnp.where(odd, 0.0, table), jnp.where(odd, table, 0.0)], axis=1)
    table = split(table)
    lane = lax.broadcasted_iota(jnp.int32, (rank, lanes), 1)
    pieces = []
    for s in range(share):
        value = dot3(table, got[pl.ds(s, size, stride=slots), :], tn)
        first = value[:rank] + pltpu.roll(value[part : part + rank], part, 1)
        second = (
            pltpu.roll(value[2 * part : 2 * part + rank], part, 1)
            + value[3 * part : 3 * part + rank]
        )
        pieces.append(jnp.where(lane < part, first, second))
    unfold = split(jnp.concatenate(pieces))
    out[...] = dot3(dot3(unfold, one), unfold, tn)


def pack_two(part, high, low, basis, out, flat, sems, *, share, half, count):
    rank = part.shape[0]
    parts = high.shape[2] // lanes
    slots = share * parts
    chunks = sems.shape[0]
    tall = half // chunks * slots

    def leave(at):
        source = flat.reshape(count, half * slots, lanes).at[:, at * tall : (at + 1) * tall]
        return pltpu.make_async_copy(source, out.at[:, at * tall : (at + 1) * tall], sems.at[at])

    value = orthonormal(part[...])
    basis[...] = value
    value = split(value)
    both = jnp.concatenate(value)
    for at in range(chunks):
        for k in range(at * half // chunks, (at + 1) * half // chunks):
            first = lax.dot_general(both, high[k], nn, preferred_element_type=jnp.float32)
            second = lax.dot_general(value[0], low[k], nn, preferred_element_type=jnp.float32)
            along = first[:rank] + (first[rank:] + second)
            for s in range(share):
                for h in range(parts):
                    start = k * slots + s * parts + h
                    flat[pl.ds(start, count, stride=half * slots), :] = along[
                        s * count : (s + 1) * count, h * lanes : (h + 1) * lanes
                    ]
        leave(at).start()
    for at in range(chunks):
        leave(at).wait()


def taken(got, s, parts, slots, size):
    return jnp.concatenate(
        [got[pl.ds(s * parts + h, size, stride=slots), :] for h in range(parts)], axis=1
    )


def work_two(got, two, three, out, high, low, *, share, half, count):
    parts = two.shape[0] // lanes
    size = count * half
    table = split(three[...])
    pieces = []
    for s in range(share):
        value = split(taken(got, s, parts, share * parts, size))
        high[s], low[s] = value
        pieces.append(dot3(table, value, tn))
    unfold = split(jnp.concatenate(pieces))
    out[...] = dot3(dot3(unfold, two[...]), unfold, tn)


def laid(size):
    return size // lanes, size % lanes != 0


def work_three(
    part, high, low, three, basis, out, sent, room, flat, sem, *, share, half, count
):
    rank, cols = part.shape
    parts = cols // lanes
    size = count * half
    whole, rest = laid(size)
    pitch = flat.shape[0] // count
    value = orthonormal(part[...])
    basis[...] = value
    for h in range(parts):
        room[h * rank : (h + 1) * rank, :] = value[:, h * lanes : (h + 1) * lanes]
    second = split(
        jnp.concatenate(
            [
                jnp.concatenate(
                    [room[pl.ds(h * rank + b, count, stride=share), :] for h in range(parts)],
                    axis=1,
                )
                for b in range(share)
            ]
        )
    )
    pieces = [dot3(second, (high[s], low[s]), nt) for s in range(share)]
    ends = []
    for b in range(share):
        for s in range(share):
            value = pieces[s][b * count : (b + 1) * count]
            for h in range(whole):
                start = (b * share + s) * whole + h
                flat[pl.ds(start, count, stride=pitch), :] = value[:, h * lanes : (h + 1) * lanes]
            if rest:
                ends.append(value[:, whole * lanes :])
    if len(ends) % 2:
        ends.append(ends[-1])
    for at in range(0, len(ends), 2):
        flat[pl.ds(share * share * whole + at // 2, count, stride=pitch), :] = jnp.concatenate(
            ends[at : at + 2], axis=1
        )
    copy = pltpu.make_async_copy(flat, sent, sem)
    copy.start()
    table = split(three[...])
    result = None
    for value in pieces:
        value = split(value)
        term = dot3(dot3(value, table), value, tn)
        result = term if result is None else result + term
    for h in range(whole):
        out[h * rank : (h + 1) * rank, :] = result[:, h * lanes : (h + 1) * lanes]
    if rest:
        end = result[:, whole * lanes :]
        out[whole * rank :, :] = jnp.concatenate([end[: rank // 2], end[rank // 2 :]], axis=1)
    copy.wait()


def finish(part, got, basis, core, room, *, share, half, count):
    size, rank = room.shape
    whole, rest = laid(size)
    pitch = got.shape[0] // count
    value = [part[h * rank : (h + 1) * rank, :] for h in range(whole)]
    if rest:
        end = part[whole * rank :, :]
        value.append(jnp.concatenate([end[:, : lanes // 2], end[:, lanes // 2 :]]))
    value = orthonormal(jnp.concatenate(value, axis=1))
    room[...] = value.T
    depth = basis.shape[0]
    basis[...] = room[pl.ds(pl.multiple_of(lax.axis_index("wide") * depth, 8), depth), :]
    value = split(value)
    for b in range(share):
        rows = []
        for s in range(share):
            at = b * share + s
            pieces = [
                got[pl.ds(at * whole + h, count, stride=pitch), :] for h in range(whole)
            ]
            if rest:
                end = got[pl.ds(share * share * whole + at // 2, count, stride=pitch), :]
                pieces.append(end[:, lanes // 2 :] if at % 2 else end[:, : lanes // 2])
            rows.append(jnp.concatenate(pieces, axis=1))
        core[:, b * rank : (b + 1) * rank] = dot3(jnp.concatenate(rows), value, nt)


def exchange(value):
    count, rows, _ = value.shape
    return lax.all_to_all(value, group, 0, 0, tiled=True).reshape(count * rows, lanes)


def special(window_data, factor_one, factor_two, factor_three):
    wide = lax.axis_size("wide")
    count = wide * lax.axis_size("narrow")
    depth, rows, cols = window_data.shape
    rank = factor_one.shape[1]
    share = rank // count
    half = depth // 2
    size = count * half
    facts = {"share": share, "half": half, "count": count}
    core_at = lax.axis_index("narrow")

    def stage(body):
        def run(*refs):
            body(*refs, **facts)

        run.__name__ = body.__name__
        return run

    slots = share + 1
    parts = cols // lanes
    chunks = max(n for n in (1, 3) if half % n == 0 and half // n * slots % 8 == 0)
    packed, sent = call(
        stage(pack_one),
        [far(count, half * slots, lanes), far(half, rows, cols)],
        window_data,
        factor_two.T,
        factor_three,
        away=(0, 1, 2),
        away_out=(0, 1),
        scratch_shapes=[
            near(chunks, 2, half // chunks, rows, cols),
            near(size * slots, lanes),
            near(rank, cols),
            near(depth, rank),
            pltpu.SemaphoreType.DMA((4 * chunks + 2,)),
        ],
    )
    got = exchange(packed)
    high, low = call(
        prepare,
        [near(half, 2 * rows, cols, dtype=jnp.bfloat16)] * 2,
        window_data,
        swap(sent),
        away=(0,),
        scratch_shapes=[near(half, rows, cols), pltpu.SemaphoreType.DMA],
    )
    one_other = swap(factor_one)
    got, high, low = lax.optimization_barrier((got, high, low))
    product, three = call(
        stage(work_one), [near(rank, 2 * rows), near(size, rank)], got, factor_one, one_other
    )
    product = total(product)

    chunks = 3 if half % 3 == 0 and half // 3 * share * parts % 8 == 0 else 1
    one_t, packed = call(
        stage(pack_two),
        [near(*product.shape), far(count, half * share * parts, lanes)],
        product,
        high,
        low,
        away_out=(1,),
        scratch_shapes=[
            near(size * share * parts, lanes),
            pltpu.SemaphoreType.DMA((chunks,)),
        ],
    )
    got = exchange(packed)
    product, high, low = call(
        stage(work_two),
        [near(rank, cols)] + [near(share, size, cols, dtype=jnp.bfloat16)] * 2,
        got,
        factor_two,
        three,
    )
    product = total(product)

    whole, rest = laid(size)
    pitch = share * share * whole + rest * -(-share * share // 2)
    pitch = -(-pitch // 8) * 8
    two_t, product, sent = call(
        stage(work_three),
        [
            near(*product.shape),
            near(rank * whole + rest * rank // 2, lanes),
            far(count * pitch, lanes),
        ],
        product,
        high,
        low,
        three,
        away_out=(2,),
        scratch_shapes=[
            near(parts * rank, lanes),
            near(count * pitch, lanes),
            pltpu.SemaphoreType.DMA,
        ],
    )
    got = exchange(sent.reshape(count, pitch, lanes))
    product = total(product)
    basis_three, core = call(
        stage(finish),
        [far(depth, rank), far(rank, share * rank)],
        product,
        got,
        scratch_shapes=[near(size, rank)],
    )
    basis_one = lax.dynamic_slice_in_dim(one_t, core_at * rows, rows, 1).T
    return (basis_one, two_t.T, basis_three, core)


def on_device(window_data, factor_one, factor_two, factor_three):
    count = lax.axis_size("wide") * lax.axis_size("narrow")
    depth, rows, cols = window_data.shape
    rank = factor_one.shape[1]
    fits = (
        lax.axis_size("narrow") == 2
        and rank % count == 0
        and count % 8 == 0
        and depth % 8 == 0
        and count * depth // 2 % (lanes // 2) == 0
        and rank % 16 == 0
        and (depth // 2) * (rank // count + 1) % 8 == 0
        and (depth // 2) * (rank // count) * (cols // lanes) % 8 == 0
        and 2 * rows == lanes
        and 2 * rank <= lanes
        and cols % lanes == 0
    )
    return (special if fits else general)(window_data, factor_one, factor_two, factor_three)


def solution(mesh):
    return jax.shard_map(
        on_device,
        mesh=mesh,
        in_specs=(
            P(("win", "wide"), "narrow", None),
            P(("win", "narrow"), None),
            P("win", None),
            P(("win", "wide"), None),
        ),
        out_specs=(
            P(("win", "narrow"), None),
            P("win", None),
            P(("win", "wide"), None),
            P(None, ("win", "wide", "narrow")),
        ),
        check_vma=False,
    )
```

```python
import jax
import jax.numpy as jnp
from jax import lax
from jax.experimental import pallas as pl
from jax.experimental.pallas import tpu as pltpu
from jax.sharding import PartitionSpec as P

highest = lax.Precision.HIGHEST
fine = lax.Precision.HIGH
group = ("wide", "narrow")
lanes = 128
nn = (((1,), (0,)), ((), ()))
nt = (((1,), (1,)), ((), ()))
tn = (((0,), (0,)), ((), ()))


def contract(form, left, right, precision=fine):
    return jnp.einsum(form, left, right, precision=precision)


def total(part):
    narrow = lax.axis_size("narrow")
    count = lax.axis_size("wide") * narrow
    if narrow != 2 or count & (count - 1):
        return lax.psum(part, group)

    def moved(mask):
        return lax.ppermute(part, group, [(at, at ^ mask) for at in range(count)])

    part = part + moved(1)
    bits = []
    while narrow < count:
        bits.append(narrow)
        narrow *= 2
    parts = [bits[-1:]] if len(bits) % 2 else []
    parts += [bits[at : at + 2] for at in range(0, len(bits) - 1, 2)]
    for low, *high in parts:
        if high:
            near_sum, far_sum = moved(low + 1), moved(high[0] + 1)
            part = (part + near_sum) + (far_sum + moved(low + high[0] + 1))
        else:
            part = part + moved(low + 1)
    return part


def swap(value):
    return lax.ppermute(value, "narrow", [(0, 1), (1, 0)])


def dot(left, right, dims=nn):
    return lax.dot_general(
        left, right, dims, precision=highest, preferred_element_type=jnp.float32
    )


def split(value):
    high = value.astype(jnp.bfloat16)
    return high, (value - high.astype(jnp.float32)).astype(jnp.bfloat16)


def dot3(left, right, dims=nn):
    left_high, left_low = left if isinstance(left, tuple) else split(left)
    right_high, right_low = right if isinstance(right, tuple) else split(right)

    def one(a, b):
        return lax.dot_general(a, b, dims, preferred_element_type=jnp.float32)

    return one(left_high, right_high) + (one(left_high, right_low) + one(left_low, right_high))


def eliminate(table, rank):
    width = table.shape[1]
    row = lax.broadcasted_iota(jnp.int32, (8, width), 0)
    tiles = [table[8 * at : 8 * at + 8] for at in range(rank // 8)]
    for at in range(rank // 8):
        live = tiles[at:]
        columns = [
            [jnp.broadcast_to(x[:, 8 * at + k : 8 * at + k + 1], (8, width)) for x in live]
            for k in range(8)
        ]
        for j in range(8):
            heads = [jnp.broadcast_to(columns[k][0][j : j + 1], (8, width)) for k in range(j, 8)]
            inverse = 1.0 / heads[0]
            scale = [x * inverse for x in columns[j]]
            scale[0] = jnp.where(row > j, scale[0], 0.0)
            for k in range(j + 1, 8):
                columns[k] = [x - y * heads[k - j] for x, y in zip(columns[k], scale)]
            lead = jnp.broadcast_to(live[0][j : j + 1], (8, width))
            live = [x - y * lead for x, y in zip(live, scale)]
        tiles[at:] = live
    return jnp.concatenate(tiles, axis=0)


def orthonormal(part):
    rank, size = part.shape
    width = -(-2 * rank // lanes) * lanes
    below = jnp.zeros((width - rank, size), part.dtype)
    gram = dot(part, jnp.concatenate([part, below]), nt)
    row = lax.broadcasted_iota(jnp.int32, (rank, width), 0)
    lane = lax.broadcasted_iota(jnp.int32, (rank, width), 1)
    table = eliminate(jnp.where(lane == row + rank, 1.0, gram), rank)
    pivots = jnp.sum(jnp.where(lane == row, table, 0.0), axis=1, keepdims=True)
    table = jnp.where(lane < rank, 0.0, table * lax.rsqrt(pivots))
    padded = [jnp.zeros((rank, size), part.dtype), part]
    if width > 2 * rank:
        padded.append(jnp.zeros((width - 2 * rank, size), part.dtype))
    return dot(table, jnp.concatenate(padded))


def orthonormal_body(part, out):
    out[...] = orthonormal(part[...])


def near(*shape, dtype=jnp.float32):
    return pltpu.VMEM(shape, dtype)


def far(*shape, dtype=jnp.float32):
    return jax.ShapeDtypeStruct(shape, dtype)


def call(body, shapes, *operands, away=(), away_out=(), **settings):
    inside = pl.BlockSpec(memory_space=pltpu.VMEM)
    outside = pl.BlockSpec(memory_space=pl.ANY)
    placed = [
        x if at in away else pltpu.with_memory_space_constraint(x, pltpu.VMEM)
        for at, x in enumerate(operands)
    ]
    return pl.pallas_call(
        body,
        in_specs=[outside if at in away else inside for at in range(len(operands))],
        out_specs=[outside if at in away_out else inside for at in range(len(shapes))],
        out_shape=shapes,
        **settings,
    )(*placed)


def general(window_data, factor_one, factor_two, factor_three):
    wide = lax.axis_size("wide")
    narrow = lax.axis_size("narrow")
    count = wide * narrow
    depth, rows, cols = window_data.shape
    rank = factor_one.shape[1]
    share = -(-rank // count)
    spare = share * count - rank
    half = depth // narrow
    core_at = lax.axis_index("narrow")

    own = lax.dynamic_slice_in_dim(window_data, core_at * half, half, 0)
    sent = lax.dynamic_slice_in_dim(window_data, (1 - core_at) * half, half, 0)
    other = swap(sent)
    factor_other = swap(factor_one)

    two_t = jnp.pad(factor_two.T, ((0, spare), (0, 0)))
    along = contract("bj,kij->bki", two_t, window_data).reshape(count, share, depth * rows)
    three_own = lax.dynamic_slice_in_dim(factor_three, core_at * half, half, 0)
    three_flat = jnp.broadcast_to(three_own.reshape(1, 1, half * rank), (count, 1, half * rank))
    packed = jnp.concatenate([along.reshape(count, -1), three_flat.reshape(count, -1)], axis=1)
    width = packed.shape[1]
    full = -(-width // 1024) * 1024
    packed = jnp.pad(packed, ((0, 0), (0, full - width))).reshape(count, full // 128, 128)
    got = lax.all_to_all(packed, group, 0, 0, tiled=True).reshape(count, full)
    three = got[:, share * depth * rows : width].reshape(wide, depth, rank)
    got = got[:, : share * depth * rows].reshape(wide, narrow, share, depth, rows)
    first = jnp.where(core_at == 0, factor_one, factor_other)
    second = jnp.where(core_at == 0, factor_other, factor_one)
    one = jnp.stack([first, second])
    unfold = contract("wnbki,wkc->bcni", got, three)
    weights = contract("bcni,nia->bca", unfold, one)
    product = contract("bcni,bca->ani", unfold, weights).reshape(rank, narrow * rows)
    product = total(product)
    one_t = call(orthonormal_body, [near(*product.shape)], product)[0]

    one_pad = jnp.pad(one_t, ((0, spare), (0, 0)))
    one_own = lax.dynamic_slice_in_dim(one_pad, core_at * rows, rows, 1)
    one_other = lax.dynamic_slice_in_dim(one_pad, (1 - core_at) * rows, rows, 1)
    along = contract("ai,kij->akj", one_own, own) + contract("ai,kij->akj", one_other, other)
    got = lax.all_to_all(
        along.reshape(count, share * half * cols // 128, 128), group, 0, 0, tiled=True
    ).reshape(count, share, half, cols)
    three = three.reshape(count, half, rank)
    unfold = contract("dakj,dkc->acj", got, three)
    weights = contract("acj,jb->acb", unfold, factor_two)
    product = contract("acj,acb->bj", unfold, weights)
    product = total(product)
    two_t = call(orthonormal_body, [near(*product.shape)], product)[0]

    unfold = contract("dakj,bj->dakb", got, two_t)
    weights = contract("dakb,dkc->abc", unfold, three)
    product = contract("dakb,abc->cdk", unfold, weights).reshape(rank, count * half)
    product = total(product)
    three_t = call(orthonormal_body, [near(*product.shape)], product)[0]
    core = contract("dakb,cdk->abc", unfold, three_t.reshape(rank, count, half))
    core = core.reshape(share, count, rank * rank // count).transpose(1, 0, 2)
    core = lax.all_to_all(core, group, 0, 0, tiled=True)
    core = core.reshape(count * share, rank * rank // count)[:rank]
    basis_three = lax.dynamic_slice_in_dim(three_t, lax.axis_index("wide") * depth, depth, 1).T
    return (one_own[:rank].T, two_t.T, basis_three, core)


def pack_one(field, two_far, three_far, out, sent, room, flat, two, three, sems, *, share, half, count):
    chunks, _, steps, rows, cols = room.shape
    rank = two.shape[0]
    pitch = flat.shape[0] // count
    at_core = lax.axis_index("narrow")

    def fetch(at, h):
        source = field.at[pl.ds(h * half + at * steps, steps)]
        return pltpu.make_async_copy(source, room.at[at, h], sems.at[2 * at + h])

    def hand(at):
        target = sent.at[pl.ds(at * steps, steps)]
        return pltpu.make_async_copy(room.at[at, 1 - at_core], target, sems.at[2 * chunks + at])

    copies = [
        pltpu.make_async_copy(three_far, three, sems.at[3 * chunks]),
        pltpu.make_async_copy(two_far, two, sems.at[3 * chunks + 1]),
    ]
    leave = pltpu.make_async_copy(flat, out, sems.at[3 * chunks + 2])
    for copy in copies:
        copy.start()
    for at in range(chunks):
        for h in range(2):
            fetch(at, h).start()
    copies[0].wait()
    own = jnp.where(at_core == 0, three[:half], three[half:])
    empty = jnp.zeros((half // 2, lanes // 2 - rank), jnp.float32)
    both = jnp.concatenate([own[: half // 2], empty, own[half // 2 :], empty], axis=1)
    for r in range(half // 2):
        flat[pl.ds(half * share + r, count, stride=pitch), :] = jnp.broadcast_to(
            both[r : r + 1], (count, lanes)
        )
    copies[1].wait()
    two_high, two_low = split(two[...])
    both = jnp.concatenate([two_high, two_low])
    for at in range(chunks):
        for h in range(2):
            fetch(at, h).wait()
        hand(at).start()
        for q in range(steps):
            high, low = split(room[at, :, q].reshape(2 * rows, cols))
            first = lax.dot_general(both, high, nt, preferred_element_type=jnp.float32)
            second = lax.dot_general(two_high, low, nt, preferred_element_type=jnp.float32)
            along = first[:rank] + (first[rank:] + second)
            for s in range(share):
                flat[pl.ds((at * steps + q) * share + s, count, stride=pitch), :] = along[
                    s * count : (s + 1) * count
                ]
    leave.start()
    for at in range(chunks):
        hand(at).wait()
    leave.wait()


def prepare(field, other, high, low, own, sem):
    half, rows, cols = other.shape
    at = lax.axis_index("narrow")
    copy = pltpu.make_async_copy(field.at[pl.ds(at * half, half)], own, sem)
    copy.start()

    def put(value, core):
        top, rest = split(value[...])
        high[:, pl.ds(pl.multiple_of(core * rows, 16), rows), :] = top
        low[:, pl.ds(pl.multiple_of(core * rows, 16), rows), :] = rest

    put(other, 1 - at)
    copy.wait()
    put(own, at)


def work_one(got, own, other, out, three, table, *, share, half, count):
    rank = own.shape[1]
    part = lanes // 2
    pitch = got.shape[0] // count
    each = pitch // share
    size = count * each
    wide = count // 2
    at = lax.axis_index("narrow")
    low = jnp.where(at == 0, own[...], other[...])
    high = jnp.where(at == 0, other[...], own[...])
    one = jnp.concatenate([low, high])
    left = lax.broadcasted_iota(jnp.int32, (wide, lanes), 1) < part
    for r in range(half // 2):
        first, second = [
            got[pl.ds(half * share + r + h * pitch, wide, stride=2 * pitch), :] for h in range(2)
        ]
        first_turned, second_turned = pltpu.roll(first, part, 1), pltpu.roll(second, part, 1)
        for n in range(2):
            start = n * each + r
            table[pl.ds(start, wide, stride=2 * each), :] = jnp.where(left, first, second_turned)
            table[pl.ds(start + half // 2, wide, stride=2 * each), :] = jnp.where(
                left, first_turned, second
            )
        for at, value in enumerate((first, first_turned, second, second_turned)):
            three[pl.ds(at * half // 2 + r, wide, stride=2 * half), :] = value
    for r in range(half, each):
        for n in range(2):
            table[pl.ds(n * each + r, wide, stride=2 * each), :] = jnp.zeros(
                (wide, lanes), jnp.float32
            )
    value = table[...]
    row = lax.broadcasted_iota(jnp.int32, (size, lanes), 0)
    odd = (row // each) % 2 == 1
    value = jnp.concatenate([jnp.where(odd, 0.0, value), jnp.where(odd, value, 0.0)], axis=1)
    mixed = split(value)
    lane = lax.broadcasted_iota(jnp.int32, (rank, lanes), 1)
    pieces = []
    for s in range(share):
        value = dot3(mixed, got[pl.ds(s, size, stride=share), :], tn)
        first = value[:rank] + pltpu.roll(value[part : part + rank], part, 1)
        second = (
            pltpu.roll(value[2 * part : 2 * part + rank], part, 1)
            + value[3 * part : 3 * part + rank]
        )
        pieces.append(jnp.where(lane < part, first, second))
    unfold = split(jnp.concatenate(pieces))
    out[...] = dot3(dot3(unfold, one), unfold, tn)


def pack_two(part, high, low, basis, out, flat, sems, *, share, half, count):
    rank = part.shape[0]
    parts = high.shape[2] // lanes
    slots = share * parts
    chunks = sems.shape[0]
    tall = half // chunks * slots

    def leave(at):
        source = flat.reshape(count, half * slots, lanes).at[:, at * tall : (at + 1) * tall]
        return pltpu.make_async_copy(source, out.at[:, at * tall : (at + 1) * tall], sems.at[at])

    value = orthonormal(part[...])
    basis[...] = value
    value = split(value)
    both = jnp.concatenate(value)
    for at in range(chunks):
        for k in range(at * half // chunks, (at + 1) * half // chunks):
            first = lax.dot_general(both, high[k], nn, preferred_element_type=jnp.float32)
            second = lax.dot_general(value[0], low[k], nn, preferred_element_type=jnp.float32)
            along = first[:rank] + (first[rank:] + second)
            for s in range(share):
                for h in range(parts):
                    start = k * slots + s * parts + h
                    flat[pl.ds(start, count, stride=half * slots), :] = along[
                        s * count : (s + 1) * count, h * lanes : (h + 1) * lanes
                    ]
        leave(at).start()
    for at in range(chunks):
        leave(at).wait()


def taken(got, s, parts, slots, size):
    return jnp.concatenate(
        [got[pl.ds(s * parts + h, size, stride=slots), :] for h in range(parts)], axis=1
    )


def work_two(got, two, three, out, high, low, *, share, half, count):
    parts = two.shape[0] // lanes
    size = count * half
    table = split(three[:, : two.shape[1]])
    pieces = []
    for s in range(share):
        value = split(taken(got, s, parts, share * parts, size))
        high[s], low[s] = value
        pieces.append(dot3(table, value, tn))
    unfold = split(jnp.concatenate(pieces))
    out[...] = dot3(dot3(unfold, two[...]), unfold, tn)


def laid(size):
    return size // lanes, size % lanes != 0


def work_three(
    part, high, low, three, basis, out, sent, room, flat, sem, *, share, half, count
):
    rank, cols = part.shape
    parts = cols // lanes
    size = count * half
    whole, rest = laid(size)
    pitch = flat.shape[0] // count
    value = orthonormal(part[...])
    basis[...] = value
    for h in range(parts):
        room[h * rank : (h + 1) * rank, :] = value[:, h * lanes : (h + 1) * lanes]
    second = split(
        jnp.concatenate(
            [
                jnp.concatenate(
                    [room[pl.ds(h * rank + b, count, stride=share), :] for h in range(parts)],
                    axis=1,
                )
                for b in range(share)
            ]
        )
    )
    pieces = [dot3(second, (high[s], low[s]), nt) for s in range(share)]
    ends = []
    for b in range(share):
        for s in range(share):
            value = pieces[s][b * count : (b + 1) * count]
            for h in range(whole):
                start = (b * share + s) * whole + h
                flat[pl.ds(start, count, stride=pitch), :] = value[:, h * lanes : (h + 1) * lanes]
            if rest:
                ends.append(value[:, whole * lanes :])
    if len(ends) % 2:
        ends.append(ends[-1])
    for at in range(0, len(ends), 2):
        flat[pl.ds(share * share * whole + at // 2, count, stride=pitch), :] = jnp.concatenate(
            ends[at : at + 2], axis=1
        )
    copy = pltpu.make_async_copy(flat, sent, sem)
    copy.start()
    table = split(three[:, :rank])
    result = None
    for value in pieces:
        value = split(value)
        term = dot3(dot3(value, table), value, tn)
        result = term if result is None else result + term
    for h in range(whole):
        out[h * rank : (h + 1) * rank, :] = result[:, h * lanes : (h + 1) * lanes]
    if rest:
        end = result[:, whole * lanes :]
        out[whole * rank :, :] = jnp.concatenate([end[: rank // 2], end[rank // 2 :]], axis=1)
    copy.wait()


def finish(part, got, basis, core, room, *, share, half, count):
    size, rank = room.shape
    whole, rest = laid(size)
    pitch = got.shape[0] // count
    value = [part[h * rank : (h + 1) * rank, :] for h in range(whole)]
    if rest:
        end = part[whole * rank :, :]
        value.append(jnp.concatenate([end[:, : lanes // 2], end[:, lanes // 2 :]]))
    value = orthonormal(jnp.concatenate(value, axis=1))
    room[...] = value.T
    depth = basis.shape[0]
    basis[...] = room[pl.ds(pl.multiple_of(lax.axis_index("wide") * depth, 8), depth), :]
    value = split(value)
    for b in range(share):
        rows = []
        for s in range(share):
            at = b * share + s
            pieces = [
                got[pl.ds(at * whole + h, count, stride=pitch), :] for h in range(whole)
            ]
            if rest:
                end = got[pl.ds(share * share * whole + at // 2, count, stride=pitch), :]
                pieces.append(end[:, lanes // 2 :] if at % 2 else end[:, : lanes // 2])
            rows.append(jnp.concatenate(pieces, axis=1))
        core[:, b * rank : (b + 1) * rank] = dot3(jnp.concatenate(rows), value, nt)


def exchange(value, count):
    rows = value.shape[0]
    flat = value.reshape(count, 1, rows // count * lanes)
    return lax.all_to_all(flat, group, 0, 0, tiled=True).reshape(rows, lanes)


def special(window_data, factor_one, factor_two, factor_three):
    wide = lax.axis_size("wide")
    count = wide * lax.axis_size("narrow")
    depth, rows, cols = window_data.shape
    rank = factor_one.shape[1]
    share = rank // count
    half = depth // 2
    size = count * half
    facts = {"share": share, "half": half, "count": count}
    core_at = lax.axis_index("narrow")

    def stage(body):
        def run(*refs):
            body(*refs, **facts)

        run.__name__ = body.__name__
        return run

    parts = cols // lanes
    chunks = 3 if half % 3 == 0 else 1
    pitch = half * share + half // 2
    packed, sent = call(
        stage(pack_one),
        [far(count * pitch, lanes), far(half, rows, cols)],
        window_data,
        factor_two.T,
        factor_three,
        away=(0, 1, 2),
        away_out=(0, 1),
        scratch_shapes=[
            near(chunks, 2, half // chunks, rows, cols),
            near(count * pitch, lanes),
            near(rank, cols),
            near(depth, rank),
            pltpu.SemaphoreType.DMA((3 * chunks + 3,)),
        ],
    )
    got = exchange(packed, count)
    high, low = call(
        prepare,
        [near(half, 2 * rows, cols, dtype=jnp.bfloat16)] * 2,
        window_data,
        swap(sent),
        away=(0,),
        scratch_shapes=[near(half, rows, cols), pltpu.SemaphoreType.DMA],
    )
    one_other = swap(factor_one)
    got, high, low = lax.optimization_barrier((got, high, low))
    product, three = call(
        stage(work_one),
        [near(rank, 2 * rows), near(size, lanes)],
        got,
        factor_one,
        one_other,
        scratch_shapes=[near(count * pitch // share, lanes)],
    )
    product = total(product)

    chunks = 3 if half % 3 == 0 and half // 3 * share * parts % 8 == 0 else 1
    one_t, packed = call(
        stage(pack_two),
        [near(*product.shape), far(count, half * share * parts, lanes)],
        product,
        high,
        low,
        away_out=(1,),
        scratch_shapes=[
            near(size * share * parts, lanes),
            pltpu.SemaphoreType.DMA((chunks,)),
        ],
    )
    got = exchange(packed.reshape(size * share * parts, lanes), count)
    product, high, low = call(
        stage(work_two),
        [near(rank, cols)] + [near(share, size, cols, dtype=jnp.bfloat16)] * 2,
        got,
        factor_two,
        three,
    )
    product = total(product)

    whole, rest = laid(size)
    pitch = share * share * whole + rest * -(-share * share // 2)
    two_t, product, sent = call(
        stage(work_three),
        [
            near(*product.shape),
            near(rank * whole + rest * rank // 2, lanes),
            far(count * pitch, lanes),
        ],
        product,
        high,
        low,
        three,
        away_out=(2,),
        scratch_shapes=[
            near(parts * rank, lanes),
            near(count * pitch, lanes),
            pltpu.SemaphoreType.DMA,
        ],
    )
    got = exchange(sent, count)
    product = total(product)
    basis_three, core = call(
        stage(finish),
        [far(depth, rank), far(rank, share * rank)],
        product,
        got,
        scratch_shapes=[near(size, rank)],
    )
    basis_one = lax.dynamic_slice_in_dim(one_t, core_at * rows, rows, 1).T
    return (basis_one, two_t.T, basis_three, core)


def on_device(window_data, factor_one, factor_two, factor_three):
    count = lax.axis_size("wide") * lax.axis_size("narrow")
    depth, rows, cols = window_data.shape
    rank = factor_one.shape[1]
    fits = (
        lax.axis_size("narrow") == 2
        and rank % count == 0
        and count % 8 == 0
        and depth % 8 == 0
        and count * depth // 2 % (lanes // 2) == 0
        and rank % 16 == 0
        and depth // 4 % (rank // count) == 0
        and count * depth * (2 * (rank // count) + 1) // 4 % 8 == 0
        and (depth // 2) * (rank // count) * (cols // lanes) % 8 == 0
        and 2 * rows == lanes
        and 2 * rank <= lanes
        and cols % lanes == 0
    )
    return (special if fits else general)(window_data, factor_one, factor_two, factor_three)


def solution(mesh):
    return jax.shard_map(
        on_device,
        mesh=mesh,
        in_specs=(
            P(("win", "wide"), "narrow", None),
            P(("win", "narrow"), None),
            P("win", None),
            P(("win", "wide"), None),
        ),
        out_specs=(
            P(("win", "narrow"), None),
            P("win", None),
            P(("win", "wide"), None),
            P(None, ("win", "wide", "narrow")),
        ),
        check_vma=False,
    )
```

```python
import jax
import jax.numpy as jnp
from jax import lax
from jax.experimental import pallas as pl
from jax.experimental.pallas import tpu as pltpu
from jax.sharding import PartitionSpec as P

highest = lax.Precision.HIGHEST
fine = lax.Precision.HIGH
group = ("wide", "narrow")
lanes = 128
nn = (((1,), (0,)), ((), ()))
nt = (((1,), (1,)), ((), ()))
tn = (((0,), (0,)), ((), ()))


def contract(form, left, right, precision=fine):
    return jnp.einsum(form, left, right, precision=precision)


def total(part):
    narrow = lax.axis_size("narrow")
    count = lax.axis_size("wide") * narrow
    if narrow != 2 or count & (count - 1):
        return lax.psum(part, group)

    def moved(mask):
        return lax.ppermute(part, group, [(at, at ^ mask) for at in range(count)])

    part = part + moved(1)
    bits = []
    while narrow < count:
        bits.append(narrow)
        narrow *= 2
    parts = [bits[-1:]] if len(bits) % 2 else []
    parts += [bits[at : at + 2] for at in range(0, len(bits) - 1, 2)]
    for low, *high in parts:
        if high:
            near_sum, far_sum = moved(low + 1), moved(high[0] + 1)
            part = (part + near_sum) + (far_sum + moved(low + high[0] + 1))
        else:
            part = part + moved(low + 1)
    return part


def swap(value):
    return lax.ppermute(value, "narrow", [(0, 1), (1, 0)])


def dot(left, right, dims=nn):
    return lax.dot_general(
        left, right, dims, precision=highest, preferred_element_type=jnp.float32
    )


def split(value):
    high = value.astype(jnp.bfloat16)
    return high, (value - high.astype(jnp.float32)).astype(jnp.bfloat16)


def dot3(left, right, dims=nn):
    left_high, left_low = left if isinstance(left, tuple) else split(left)
    right_high, right_low = right if isinstance(right, tuple) else split(right)

    def one(a, b):
        return lax.dot_general(a, b, dims, preferred_element_type=jnp.float32)

    return one(left_high, right_high) + (one(left_high, right_low) + one(left_low, right_high))


def eliminate(table, rank):
    width = table.shape[1]
    row = lax.broadcasted_iota(jnp.int32, (8, width), 0)
    tiles = [table[8 * at : 8 * at + 8] for at in range(rank // 8)]
    for at in range(rank // 8):
        live = tiles[at:]
        columns = [
            [jnp.broadcast_to(x[:, 8 * at + k : 8 * at + k + 1], (8, width)) for x in live]
            for k in range(8)
        ]
        root = None
        for j in range(8):
            heads = [jnp.broadcast_to(columns[k][0][j : j + 1], (8, width)) for k in range(j, 8)]
            inverse = 1.0 / heads[0]
            root = jnp.where(row == j, lax.rsqrt(heads[0]), 0.0 if root is None else root)
            scale = [x * inverse for x in columns[j]]
            scale[0] = jnp.where(row > j, scale[0], 0.0)
            for k in range(j + 1, 8):
                columns[k] = [x - y * heads[k - j] for x, y in zip(columns[k], scale)]
            lead = jnp.broadcast_to(live[0][j : j + 1], (8, width))
            live = [x - y * lead for x, y in zip(live, scale)]
        tiles[at:] = live
        tiles[at] = live[0] * root
    return jnp.concatenate(tiles, axis=0)


def orthonormal(part):
    rank, size = part.shape
    width = -(-2 * rank // lanes) * lanes
    below = jnp.zeros((width - rank, size), part.dtype)
    gram = dot(part, jnp.concatenate([part, below]), nt)
    row = lax.broadcasted_iota(jnp.int32, (rank, width), 0)
    lane = lax.broadcasted_iota(jnp.int32, (rank, width), 1)
    table = eliminate(jnp.where(lane == row + rank, 1.0, gram), rank)
    table = jnp.where(lane < rank, 0.0, table)
    padded = [jnp.zeros((rank, size), part.dtype), part]
    if width > 2 * rank:
        padded.append(jnp.zeros((width - 2 * rank, size), part.dtype))
    return dot(table, jnp.concatenate(padded))


def orthonormal_body(part, out):
    out[...] = orthonormal(part[...])


def near(*shape, dtype=jnp.float32):
    return pltpu.VMEM(shape, dtype)


def far(*shape, dtype=jnp.float32):
    return jax.ShapeDtypeStruct(shape, dtype)


def call(body, shapes, *operands, away=(), away_out=(), **settings):
    inside = pl.BlockSpec(memory_space=pltpu.VMEM)
    outside = pl.BlockSpec(memory_space=pl.ANY)
    placed = [
        x if at in away else pltpu.with_memory_space_constraint(x, pltpu.VMEM)
        for at, x in enumerate(operands)
    ]
    return pl.pallas_call(
        body,
        in_specs=[outside if at in away else inside for at in range(len(operands))],
        out_specs=[outside if at in away_out else inside for at in range(len(shapes))],
        out_shape=shapes,
        **settings,
    )(*placed)


def general(window_data, factor_one, factor_two, factor_three):
    wide = lax.axis_size("wide")
    narrow = lax.axis_size("narrow")
    count = wide * narrow
    depth, rows, cols = window_data.shape
    rank = factor_one.shape[1]
    share = -(-rank // count)
    spare = share * count - rank
    half = depth // narrow
    core_at = lax.axis_index("narrow")

    own = lax.dynamic_slice_in_dim(window_data, core_at * half, half, 0)
    sent = lax.dynamic_slice_in_dim(window_data, (1 - core_at) * half, half, 0)
    other = swap(sent)
    factor_other = swap(factor_one)

    two_t = jnp.pad(factor_two.T, ((0, spare), (0, 0)))
    along = contract("bj,kij->bki", two_t, window_data).reshape(count, share, depth * rows)
    three_own = lax.dynamic_slice_in_dim(factor_three, core_at * half, half, 0)
    three_flat = jnp.broadcast_to(three_own.reshape(1, 1, half * rank), (count, 1, half * rank))
    packed = jnp.concatenate([along.reshape(count, -1), three_flat.reshape(count, -1)], axis=1)
    width = packed.shape[1]
    full = -(-width // 1024) * 1024
    packed = jnp.pad(packed, ((0, 0), (0, full - width))).reshape(count, full // 128, 128)
    got = lax.all_to_all(packed, group, 0, 0, tiled=True).reshape(count, full)
    three = got[:, share * depth * rows : width].reshape(wide, depth, rank)
    got = got[:, : share * depth * rows].reshape(wide, narrow, share, depth, rows)
    first = jnp.where(core_at == 0, factor_one, factor_other)
    second = jnp.where(core_at == 0, factor_other, factor_one)
    one = jnp.stack([first, second])
    unfold = contract("wnbki,wkc->bcni", got, three)
    weights = contract("bcni,nia->bca", unfold, one)
    product = contract("bcni,bca->ani", unfold, weights).reshape(rank, narrow * rows)
    product = total(product)
    one_t = call(orthonormal_body, [near(*product.shape)], product)[0]

    one_pad = jnp.pad(one_t, ((0, spare), (0, 0)))
    one_own = lax.dynamic_slice_in_dim(one_pad, core_at * rows, rows, 1)
    one_other = lax.dynamic_slice_in_dim(one_pad, (1 - core_at) * rows, rows, 1)
    along = contract("ai,kij->akj", one_own, own) + contract("ai,kij->akj", one_other, other)
    got = lax.all_to_all(
        along.reshape(count, share * half * cols // 128, 128), group, 0, 0, tiled=True
    ).reshape(count, share, half, cols)
    three = three.reshape(count, half, rank)
    unfold = contract("dakj,dkc->acj", got, three)
    weights = contract("acj,jb->acb", unfold, factor_two)
    product = contract("acj,acb->bj", unfold, weights)
    product = total(product)
    two_t = call(orthonormal_body, [near(*product.shape)], product)[0]

    unfold = contract("dakj,bj->dakb", got, two_t)
    weights = contract("dakb,dkc->abc", unfold, three)
    product = contract("dakb,abc->cdk", unfold, weights).reshape(rank, count * half)
    product = total(product)
    three_t = call(orthonormal_body, [near(*product.shape)], product)[0]
    core = contract("dakb,cdk->abc", unfold, three_t.reshape(rank, count, half))
    core = core.reshape(share, count, rank * rank // count).transpose(1, 0, 2)
    core = lax.all_to_all(core, group, 0, 0, tiled=True)
    core = core.reshape(count * share, rank * rank // count)[:rank]
    basis_three = lax.dynamic_slice_in_dim(three_t, lax.axis_index("wide") * depth, depth, 1).T
    return (one_own[:rank].T, two_t.T, basis_three, core)


def pack_one(field, two_far, three_far, out, sent, room, flat, two, three, sems, *, share, half, count):
    chunks, _, steps, rows, cols = room.shape
    rank = two.shape[0]
    pitch = flat.shape[0] // count
    at_core = lax.axis_index("narrow")

    def fetch(at, h):
        source = field.at[pl.ds(h * half + at * steps, steps)]
        return pltpu.make_async_copy(source, room.at[at, h], sems.at[2 * at + h])

    def hand(at):
        target = sent.at[pl.ds(at * steps, steps)]
        return pltpu.make_async_copy(room.at[at, 1 - at_core], target, sems.at[2 * chunks + at])

    copies = [
        pltpu.make_async_copy(three_far, three, sems.at[3 * chunks]),
        pltpu.make_async_copy(two_far, two, sems.at[3 * chunks + 1]),
    ]
    leave = pltpu.make_async_copy(flat, out, sems.at[3 * chunks + 2])
    for copy in copies:
        copy.start()
    for at in range(chunks):
        for h in range(2):
            fetch(at, h).start()
    copies[0].wait()
    own = jnp.where(at_core == 0, three[:half], three[half:])
    empty = jnp.zeros((half // 2, lanes // 2 - rank), jnp.float32)
    both = jnp.concatenate([own[: half // 2], empty, own[half // 2 :], empty], axis=1)
    for r in range(half // 2):
        flat[pl.ds(half * share + r, count, stride=pitch), :] = jnp.broadcast_to(
            both[r : r + 1], (count, lanes)
        )
    copies[1].wait()
    two_high, two_low = split(two[...])
    both = jnp.concatenate([two_high, two_low])
    for at in range(chunks):
        for h in range(2):
            fetch(at, h).wait()
        hand(at).start()
        for q in range(steps):
            high, low = split(room[at, :, q].reshape(2 * rows, cols))
            first = lax.dot_general(both, high, nt, preferred_element_type=jnp.float32)
            second = lax.dot_general(two_high, low, nt, preferred_element_type=jnp.float32)
            along = first[:rank] + (first[rank:] + second)
            for s in range(share):
                flat[pl.ds((at * steps + q) * share + s, count, stride=pitch), :] = along[
                    s * count : (s + 1) * count
                ]
    leave.start()
    for at in range(chunks):
        hand(at).wait()
    leave.wait()


def prepare(field, other, high, low, own, sem):
    half, rows, cols = other.shape
    at = lax.axis_index("narrow")
    copy = pltpu.make_async_copy(field.at[pl.ds(at * half, half)], own, sem)
    copy.start()

    def put(value, core):
        top, rest = split(value[...])
        high[:, pl.ds(pl.multiple_of(core * rows, 16), rows), :] = top
        low[:, pl.ds(pl.multiple_of(core * rows, 16), rows), :] = rest

    put(other, 1 - at)
    copy.wait()
    put(own, at)


def work_one(got, own, other, out, three, table, *, share, half, count):
    rank = own.shape[1]
    part = lanes // 2
    pitch = got.shape[0] // count
    each = pitch // share
    size = count * each
    wide = count // 2
    at = lax.axis_index("narrow")
    low = jnp.where(at == 0, own[...], other[...])
    high = jnp.where(at == 0, other[...], own[...])
    one = jnp.concatenate([low, high])
    left = lax.broadcasted_iota(jnp.int32, (wide, lanes), 1) < part
    for r in range(half // 2):
        first, second = [
            got[pl.ds(half * share + r + h * pitch, wide, stride=2 * pitch), :] for h in range(2)
        ]
        first_turned, second_turned = pltpu.roll(first, part, 1), pltpu.roll(second, part, 1)
        for n in range(2):
            start = n * each + r
            table[pl.ds(start, wide, stride=2 * each), :] = jnp.where(left, first, second_turned)
            table[pl.ds(start + half // 2, wide, stride=2 * each), :] = jnp.where(
                left, first_turned, second
            )
        for at, value in enumerate((first, first_turned, second, second_turned)):
            three[pl.ds(at * half // 2 + r, wide, stride=2 * half), :] = value
    for r in range(half, each):
        for n in range(2):
            table[pl.ds(n * each + r, wide, stride=2 * each), :] = jnp.zeros(
                (wide, lanes), jnp.float32
            )
    value = table[...]
    row = lax.broadcasted_iota(jnp.int32, (size, lanes), 0)
    odd = (row // each) % 2 == 1
    value = jnp.concatenate([jnp.where(odd, 0.0, value), jnp.where(odd, value, 0.0)], axis=1)
    mixed = split(value)
    lane = lax.broadcasted_iota(jnp.int32, (rank, lanes), 1)
    pieces = []
    for s in range(share):
        value = dot3(mixed, got[pl.ds(s, size, stride=share), :], tn)
        first = value[:rank] + pltpu.roll(value[part : part + rank], part, 1)
        second = (
            pltpu.roll(value[2 * part : 2 * part + rank], part, 1)
            + value[3 * part : 3 * part + rank]
        )
        pieces.append(jnp.where(lane < part, first, second))
    unfold = split(jnp.concatenate(pieces))
    out[...] = dot3(dot3(unfold, one), unfold, tn)


def pack_two(part, high, low, basis, out, flat, sems, *, share, half, count):
    rank = part.shape[0]
    parts = high.shape[2] // lanes
    slots = share * parts
    chunks = sems.shape[0]
    tall = half // chunks * slots

    def leave(at):
        source = flat.reshape(count, half * slots, lanes).at[:, at * tall : (at + 1) * tall]
        return pltpu.make_async_copy(source, out.at[:, at * tall : (at + 1) * tall], sems.at[at])

    value = orthonormal(part[...])
    basis[...] = value
    value = split(value)
    both = jnp.concatenate(value)
    for at in range(chunks):
        for k in range(at * half // chunks, (at + 1) * half // chunks):
            first = lax.dot_general(both, high[k], nn, preferred_element_type=jnp.float32)
            second = lax.dot_general(value[0], low[k], nn, preferred_element_type=jnp.float32)
            along = first[:rank] + (first[rank:] + second)
            for s in range(share):
                for h in range(parts):
                    start = k * slots + s * parts + h
                    flat[pl.ds(start, count, stride=half * slots), :] = along[
                        s * count : (s + 1) * count, h * lanes : (h + 1) * lanes
                    ]
        leave(at).start()
    for at in range(chunks):
        leave(at).wait()


def taken(got, s, parts, slots, size):
    return jnp.concatenate(
        [got[pl.ds(s * parts + h, size, stride=slots), :] for h in range(parts)], axis=1
    )


def work_two(got, two, three, out, high, low, *, share, half, count):
    parts = two.shape[0] // lanes
    size = count * half
    table = split(three[:, : two.shape[1]])
    pieces = []
    for s in range(share):
        value = split(taken(got, s, parts, share * parts, size))
        high[s], low[s] = value
        pieces.append(dot3(table, value, tn))
    unfold = split(jnp.concatenate(pieces))
    out[...] = dot3(dot3(unfold, two[...]), unfold, tn)


def laid(size):
    return size // lanes, size % lanes != 0


def work_three(
    part, high, low, three, basis, out, sent, room, flat, sem, *, share, half, count
):
    rank, cols = part.shape
    parts = cols // lanes
    size = count * half
    whole, rest = laid(size)
    pitch = flat.shape[0] // count
    value = orthonormal(part[...])
    basis[...] = value
    for h in range(parts):
        room[h * rank : (h + 1) * rank, :] = value[:, h * lanes : (h + 1) * lanes]
    second = split(
        jnp.concatenate(
            [
                jnp.concatenate(
                    [room[pl.ds(h * rank + b, count, stride=share), :] for h in range(parts)],
                    axis=1,
                )
                for b in range(share)
            ]
        )
    )
    pieces = [dot3(second, (high[s], low[s]), nt) for s in range(share)]
    ends = []
    for b in range(share):
        for s in range(share):
            value = pieces[s][b * count : (b + 1) * count]
            for h in range(whole):
                start = (b * share + s) * whole + h
                flat[pl.ds(start, count, stride=pitch), :] = value[:, h * lanes : (h + 1) * lanes]
            if rest:
                ends.append(value[:, whole * lanes :])
    if len(ends) % 2:
        ends.append(ends[-1])
    for at in range(0, len(ends), 2):
        flat[pl.ds(share * share * whole + at // 2, count, stride=pitch), :] = jnp.concatenate(
            ends[at : at + 2], axis=1
        )
    copy = pltpu.make_async_copy(flat, sent, sem)
    copy.start()
    table = split(three[:, :rank])
    result = None
    for value in pieces:
        value = split(value)
        term = dot3(dot3(value, table), value, tn)
        result = term if result is None else result + term
    for h in range(whole):
        out[h * rank : (h + 1) * rank, :] = result[:, h * lanes : (h + 1) * lanes]
    if rest:
        end = result[:, whole * lanes :]
        out[whole * rank :, :] = jnp.concatenate([end[: rank // 2], end[rank // 2 :]], axis=1)
    copy.wait()


def finish(part, got, basis, core, room, *, share, half, count):
    size, rank = room.shape
    whole, rest = laid(size)
    pitch = got.shape[0] // count
    value = [part[h * rank : (h + 1) * rank, :] for h in range(whole)]
    if rest:
        end = part[whole * rank :, :]
        value.append(jnp.concatenate([end[:, : lanes // 2], end[:, lanes // 2 :]]))
    value = orthonormal(jnp.concatenate(value, axis=1))
    room[...] = value.T
    depth = basis.shape[0]
    basis[...] = room[pl.ds(pl.multiple_of(lax.axis_index("wide") * depth, 8), depth), :]
    value = split(value)
    for b in range(share):
        rows = []
        for s in range(share):
            at = b * share + s
            pieces = [
                got[pl.ds(at * whole + h, count, stride=pitch), :] for h in range(whole)
            ]
            if rest:
                end = got[pl.ds(share * share * whole + at // 2, count, stride=pitch), :]
                pieces.append(end[:, lanes // 2 :] if at % 2 else end[:, : lanes // 2])
            rows.append(jnp.concatenate(pieces, axis=1))
        core[:, b * rank : (b + 1) * rank] = dot3(jnp.concatenate(rows), value, nt)


def exchange(value, count):
    rows = value.shape[0]
    flat = value.reshape(count, 1, rows // count * lanes)
    return lax.all_to_all(flat, group, 0, 0, tiled=True).reshape(rows, lanes)


def special(window_data, factor_one, factor_two, factor_three):
    wide = lax.axis_size("wide")
    count = wide * lax.axis_size("narrow")
    depth, rows, cols = window_data.shape
    rank = factor_one.shape[1]
    share = rank // count
    half = depth // 2
    size = count * half
    facts = {"share": share, "half": half, "count": count}
    core_at = lax.axis_index("narrow")

    def stage(body):
        def run(*refs):
            body(*refs, **facts)

        run.__name__ = body.__name__
        return run

    parts = cols // lanes
    chunks = 3 if half % 3 == 0 else 1
    pitch = half * share + half // 2
    packed, sent = call(
        stage(pack_one),
        [far(count * pitch, lanes), far(half, rows, cols)],
        window_data,
        factor_two.T,
        factor_three,
        away=(0, 1, 2),
        away_out=(0, 1),
        scratch_shapes=[
            near(chunks, 2, half // chunks, rows, cols),
            near(count * pitch, lanes),
            near(rank, cols),
            near(depth, rank),
            pltpu.SemaphoreType.DMA((3 * chunks + 3,)),
        ],
    )
    got = exchange(packed, count)
    high, low = call(
        prepare,
        [near(half, 2 * rows, cols, dtype=jnp.bfloat16)] * 2,
        window_data,
        swap(sent),
        away=(0,),
        scratch_shapes=[near(half, rows, cols), pltpu.SemaphoreType.DMA],
    )
    one_other = swap(factor_one)
    got, high, low = lax.optimization_barrier((got, high, low))
    product, three = call(
        stage(work_one),
        [near(rank, 2 * rows), near(size, lanes)],
        got,
        factor_one,
        one_other,
        scratch_shapes=[near(count * pitch // share, lanes)],
    )
    product = total(product)

    chunks = 3 if half % 3 == 0 and half // 3 * share * parts % 8 == 0 else 1
    one_t, packed = call(
        stage(pack_two),
        [near(*product.shape), far(count, half * share * parts, lanes)],
        product,
        high,
        low,
        away_out=(1,),
        scratch_shapes=[
            near(size * share * parts, lanes),
            pltpu.SemaphoreType.DMA((chunks,)),
        ],
    )
    got = exchange(packed.reshape(size * share * parts, lanes), count)
    product, high, low = call(
        stage(work_two),
        [near(rank, cols)] + [near(share, size, cols, dtype=jnp.bfloat16)] * 2,
        got,
        factor_two,
        three,
    )
    product = total(product)

    whole, rest = laid(size)
    pitch = share * share * whole + rest * -(-share * share // 2)
    pitch = -(-pitch // 8) * 8
    two_t, product, sent = call(
        stage(work_three),
        [
            near(*product.shape),
            near(rank * whole + rest * rank // 2, lanes),
            far(count * pitch, lanes),
        ],
        product,
        high,
        low,
        three,
        away_out=(2,),
        scratch_shapes=[
            near(parts * rank, lanes),
            near(count * pitch, lanes),
            pltpu.SemaphoreType.DMA,
        ],
    )
    got = exchange(sent, count)
    product = total(product)
    basis_three, core = call(
        stage(finish),
        [far(depth, rank), far(rank, share * rank)],
        product,
        got,
        scratch_shapes=[near(size, rank)],
    )
    basis_one = lax.dynamic_slice_in_dim(one_t, core_at * rows, rows, 1).T
    return (basis_one, two_t.T, basis_three, core)


def on_device(window_data, factor_one, factor_two, factor_three):
    count = lax.axis_size("wide") * lax.axis_size("narrow")
    depth, rows, cols = window_data.shape
    rank = factor_one.shape[1]
    fits = (
        lax.axis_size("narrow") == 2
        and rank % count == 0
        and count % 8 == 0
        and depth % 8 == 0
        and count * depth // 2 % (lanes // 2) == 0
        and rank % 16 == 0
        and depth // 4 % (rank // count) == 0
        and count * depth * (2 * (rank // count) + 1) // 4 % 8 == 0
        and (depth // 2) * (rank // count) * (cols // lanes) % 8 == 0
        and 2 * rows == lanes
        and 2 * rank <= lanes
        and cols % lanes == 0
    )
    return (special if fits else general)(window_data, factor_one, factor_two, factor_three)


def solution(mesh):
    return jax.shard_map(
        on_device,
        mesh=mesh,
        in_specs=(
            P(("win", "wide"), "narrow", None),
            P(("win", "narrow"), None),
            P("win", None),
            P(("win", "wide"), None),
        ),
        out_specs=(
            P(("win", "narrow"), None),
            P("win", None),
            P(("win", "wide"), None),
            P(None, ("win", "wide", "narrow")),
        ),
        check_vma=False,
    )
```

```python
import jax
import jax.numpy as jnp
from jax import lax
from jax.experimental import pallas as pl
from jax.experimental.pallas import tpu as pltpu
from jax.sharding import PartitionSpec as P

highest = lax.Precision.HIGHEST
fine = lax.Precision.HIGH
group = ("wide", "narrow")
lanes = 128
nn = (((1,), (0,)), ((), ()))
nt = (((1,), (1,)), ((), ()))
tn = (((0,), (0,)), ((), ()))


def contract(form, left, right, precision=fine):
    return jnp.einsum(form, left, right, precision=precision)


def total(part):
    narrow = lax.axis_size("narrow")
    count = lax.axis_size("wide") * narrow
    if narrow != 2 or count & (count - 1):
        return lax.psum(part, group)

    def moved(mask):
        return lax.ppermute(part, group, [(at, at ^ mask) for at in range(count)])

    part = part + moved(1)
    bits = []
    while narrow < count:
        bits.append(narrow)
        narrow *= 2
    parts = [bits[-1:]] if len(bits) % 2 else []
    parts += [bits[at : at + 2] for at in range(0, len(bits) - 1, 2)]
    for low, *high in parts:
        if high:
            near_sum, far_sum = moved(low + 1), moved(high[0] + 1)
            part = (part + near_sum) + (far_sum + moved(low + high[0] + 1))
        else:
            part = part + moved(low + 1)
    return part


def swap(value):
    return lax.ppermute(value, "narrow", [(0, 1), (1, 0)])


def dot(left, right, dims=nn):
    return lax.dot_general(
        left, right, dims, precision=highest, preferred_element_type=jnp.float32
    )


def split(value):
    high = value.astype(jnp.bfloat16)
    return high, (value - high.astype(jnp.float32)).astype(jnp.bfloat16)


def dot3(left, right, dims=nn):
    left_high, left_low = left if isinstance(left, tuple) else split(left)
    right_high, right_low = right if isinstance(right, tuple) else split(right)

    def one(a, b):
        return lax.dot_general(a, b, dims, preferred_element_type=jnp.float32)

    return one(left_high, right_high) + (one(left_high, right_low) + one(left_low, right_high))


def eliminate(table, rank):
    width = table.shape[1]
    row = lax.broadcasted_iota(jnp.int32, (8, width), 0)
    tiles = [table[8 * at : 8 * at + 8] for at in range(rank // 8)]
    for at in range(rank // 8):
        live = tiles[at:]
        columns = [
            [jnp.broadcast_to(x[:, 8 * at + k : 8 * at + k + 1], (8, width)) for x in live]
            for k in range(8)
        ]
        root = None
        for j in range(8):
            heads = [jnp.broadcast_to(columns[k][0][j : j + 1], (8, width)) for k in range(j, 8)]
            inverse = 1.0 / heads[0]
            root = jnp.where(row == j, lax.rsqrt(heads[0]), 0.0 if root is None else root)
            scale = [x * inverse for x in columns[j]]
            scale[0] = jnp.where(row > j, scale[0], 0.0)
            for k in range(j + 1, 8):
                columns[k] = [x - y * heads[k - j] for x, y in zip(columns[k], scale)]
            lead = jnp.broadcast_to(live[0][j : j + 1], (8, width))
            live = [x - y * lead for x, y in zip(live, scale)]
        tiles[at:] = live
        tiles[at] = live[0] * root
    return jnp.concatenate(tiles, axis=0)


def orthonormal(part):
    rank, size = part.shape
    width = -(-2 * rank // lanes) * lanes
    below = jnp.zeros((width - rank, size), part.dtype)
    gram = dot(part, jnp.concatenate([part, below]), nt)
    row = lax.broadcasted_iota(jnp.int32, (rank, width), 0)
    lane = lax.broadcasted_iota(jnp.int32, (rank, width), 1)
    table = eliminate(jnp.where(lane == row + rank, 1.0, gram), rank)
    table = jnp.where(lane < rank, 0.0, table)
    padded = [jnp.zeros((rank, size), part.dtype), part]
    if width > 2 * rank:
        padded.append(jnp.zeros((width - 2 * rank, size), part.dtype))
    return dot(table, jnp.concatenate(padded))


def orthonormal_body(part, out):
    out[...] = orthonormal(part[...])


def near(*shape, dtype=jnp.float32):
    return pltpu.VMEM(shape, dtype)


def far(*shape, dtype=jnp.float32):
    return jax.ShapeDtypeStruct(shape, dtype)


def call(body, shapes, *operands, away=(), away_out=(), **settings):
    inside = pl.BlockSpec(memory_space=pltpu.VMEM)
    outside = pl.BlockSpec(memory_space=pl.ANY)
    placed = [
        x if at in away else pltpu.with_memory_space_constraint(x, pltpu.VMEM)
        for at, x in enumerate(operands)
    ]
    return pl.pallas_call(
        body,
        in_specs=[outside if at in away else inside for at in range(len(operands))],
        out_specs=[outside if at in away_out else inside for at in range(len(shapes))],
        out_shape=shapes,
        **settings,
    )(*placed)


def general(window_data, factor_one, factor_two, factor_three):
    wide = lax.axis_size("wide")
    narrow = lax.axis_size("narrow")
    count = wide * narrow
    depth, rows, cols = window_data.shape
    rank = factor_one.shape[1]
    share = -(-rank // count)
    spare = share * count - rank
    half = depth // narrow
    core_at = lax.axis_index("narrow")

    own = lax.dynamic_slice_in_dim(window_data, core_at * half, half, 0)
    sent = lax.dynamic_slice_in_dim(window_data, (1 - core_at) * half, half, 0)
    other = swap(sent)
    factor_other = swap(factor_one)

    two_t = jnp.pad(factor_two.T, ((0, spare), (0, 0)))
    along = contract("bj,kij->bki", two_t, window_data).reshape(count, share, depth * rows)
    three_own = lax.dynamic_slice_in_dim(factor_three, core_at * half, half, 0)
    three_flat = jnp.broadcast_to(three_own.reshape(1, 1, half * rank), (count, 1, half * rank))
    packed = jnp.concatenate([along.reshape(count, -1), three_flat.reshape(count, -1)], axis=1)
    width = packed.shape[1]
    full = -(-width // 1024) * 1024
    packed = jnp.pad(packed, ((0, 0), (0, full - width))).reshape(count, full // 128, 128)
    got = lax.all_to_all(packed, group, 0, 0, tiled=True).reshape(count, full)
    three = got[:, share * depth * rows : width].reshape(wide, depth, rank)
    got = got[:, : share * depth * rows].reshape(wide, narrow, share, depth, rows)
    first = jnp.where(core_at == 0, factor_one, factor_other)
    second = jnp.where(core_at == 0, factor_other, factor_one)
    one = jnp.stack([first, second])
    unfold = contract("wnbki,wkc->bcni", got, three)
    weights = contract("bcni,nia->bca", unfold, one)
    product = contract("bcni,bca->ani", unfold, weights).reshape(rank, narrow * rows)
    product = total(product)
    one_t = call(orthonormal_body, [near(*product.shape)], product)[0]

    one_pad = jnp.pad(one_t, ((0, spare), (0, 0)))
    one_own = lax.dynamic_slice_in_dim(one_pad, core_at * rows, rows, 1)
    one_other = lax.dynamic_slice_in_dim(one_pad, (1 - core_at) * rows, rows, 1)
    along = contract("ai,kij->akj", one_own, own) + contract("ai,kij->akj", one_other, other)
    got = lax.all_to_all(
        along.reshape(count, share * half * cols // 128, 128), group, 0, 0, tiled=True
    ).reshape(count, share, half, cols)
    three = three.reshape(count, half, rank)
    unfold = contract("dakj,dkc->acj", got, three)
    weights = contract("acj,jb->acb", unfold, factor_two)
    product = contract("acj,acb->bj", unfold, weights)
    product = total(product)
    two_t = call(orthonormal_body, [near(*product.shape)], product)[0]

    unfold = contract("dakj,bj->dakb", got, two_t)
    weights = contract("dakb,dkc->abc", unfold, three)
    product = contract("dakb,abc->cdk", unfold, weights).reshape(rank, count * half)
    product = total(product)
    three_t = call(orthonormal_body, [near(*product.shape)], product)[0]
    core = contract("dakb,cdk->abc", unfold, three_t.reshape(rank, count, half))
    core = core.reshape(share, count, rank * rank // count).transpose(1, 0, 2)
    core = lax.all_to_all(core, group, 0, 0, tiled=True)
    core = core.reshape(count * share, rank * rank // count)[:rank]
    basis_three = lax.dynamic_slice_in_dim(three_t, lax.axis_index("wide") * depth, depth, 1).T
    return (one_own[:rank].T, two_t.T, basis_three, core)


def pack_one(field, two_far, three_far, out, sent, room, flat, two, three, sems, *, share, half, count):
    chunks, _, steps, rows, cols = room.shape
    rank = two.shape[0]
    pitch = flat.shape[0] // count
    at_core = lax.axis_index("narrow")

    def fetch(at, h):
        source = field.at[pl.ds(h * half + at * steps, steps)]
        return pltpu.make_async_copy(source, room.at[at, h], sems.at[2 * at + h])

    def hand(at):
        target = sent.at[pl.ds(at * steps, steps)]
        return pltpu.make_async_copy(room.at[at, 1 - at_core], target, sems.at[2 * chunks + at])

    copies = [
        pltpu.make_async_copy(three_far, three, sems.at[3 * chunks]),
        pltpu.make_async_copy(two_far, two, sems.at[3 * chunks + 1]),
    ]
    leave = pltpu.make_async_copy(flat, out, sems.at[3 * chunks + 2])
    for copy in copies:
        copy.start()
    for at in range(chunks):
        for h in range(2):
            fetch(at, h).start()
    copies[0].wait()
    own = jnp.where(at_core == 0, three[:half], three[half:])
    empty = jnp.zeros((half // 2, lanes // 2 - rank), jnp.float32)
    both = jnp.concatenate([own[: half // 2], empty, own[half // 2 :], empty], axis=1)
    for r in range(half // 2):
        flat[pl.ds(half * share + r, count, stride=pitch), :] = jnp.broadcast_to(
            both[r : r + 1], (count, lanes)
        )
    copies[1].wait()
    two_high, two_low = split(two[...])
    both = jnp.concatenate([two_high, two_low])
    for at in range(chunks):
        for h in range(2):
            fetch(at, h).wait()
        hand(at).start()
        value = [room[at, h, q] for q in range(steps) for h in range(2)]
        high, low = split(jnp.concatenate(value))
        first = lax.dot_general(both, high, nt, preferred_element_type=jnp.float32)
        second = lax.dot_general(two_high, low, nt, preferred_element_type=jnp.float32)
        along = first[:rank] + (first[rank:] + second)
        for q in range(steps):
            for s in range(share):
                flat[pl.ds((at * steps + q) * share + s, count, stride=pitch), :] = along[
                    s * count : (s + 1) * count, q * lanes : (q + 1) * lanes
                ]
    leave.start()
    for at in range(chunks):
        hand(at).wait()
    leave.wait()


def prepare(field, other, high, low, own, sem):
    half, rows, cols = other.shape
    at = lax.axis_index("narrow")
    copy = pltpu.make_async_copy(field.at[pl.ds(at * half, half)], own, sem)
    copy.start()

    def put(value, core):
        top, rest = split(value[...])
        high[:, pl.ds(pl.multiple_of(core * rows, 16), rows), :] = top
        low[:, pl.ds(pl.multiple_of(core * rows, 16), rows), :] = rest

    put(other, 1 - at)
    copy.wait()
    put(own, at)


def work_one(got, own, other, out, three, table, *, share, half, count):
    rank = own.shape[1]
    part = lanes // 2
    pitch = got.shape[0] // count
    each = pitch // share
    size = count * each
    wide = count // 2
    at = lax.axis_index("narrow")
    low = jnp.where(at == 0, own[...], other[...])
    high = jnp.where(at == 0, other[...], own[...])
    one = jnp.concatenate([low, high])
    left = lax.broadcasted_iota(jnp.int32, (wide, lanes), 1) < part
    for r in range(half // 2):
        first, second = [
            got[pl.ds(half * share + r + h * pitch, wide, stride=2 * pitch), :] for h in range(2)
        ]
        first_turned, second_turned = pltpu.roll(first, part, 1), pltpu.roll(second, part, 1)
        for n in range(2):
            start = n * each + r
            table[pl.ds(start, wide, stride=2 * each), :] = jnp.where(left, first, second_turned)
            table[pl.ds(start + half // 2, wide, stride=2 * each), :] = jnp.where(
                left, first_turned, second
            )
        for at, value in enumerate((first, first_turned, second, second_turned)):
            three[pl.ds(at * half // 2 + r, wide, stride=2 * half), :] = value
    for r in range(half, each):
        for n in range(2):
            table[pl.ds(n * each + r, wide, stride=2 * each), :] = jnp.zeros(
                (wide, lanes), jnp.float32
            )
    value = table[...]
    row = lax.broadcasted_iota(jnp.int32, (size, lanes), 0)
    odd = (row // each) % 2 == 1
    value = jnp.concatenate([jnp.where(odd, 0.0, value), jnp.where(odd, value, 0.0)], axis=1)
    mixed = split(value)
    lane = lax.broadcasted_iota(jnp.int32, (rank, lanes), 1)
    pieces = []
    field = jnp.concatenate([got[pl.ds(s, size, stride=share), :] for s in range(share)], axis=1)
    field = dot3(mixed, field, tn)
    for s in range(share):
        value = field[:, s * lanes : (s + 1) * lanes]
        first = value[:rank] + pltpu.roll(value[part : part + rank], part, 1)
        second = (
            pltpu.roll(value[2 * part : 2 * part + rank], part, 1)
            + value[3 * part : 3 * part + rank]
        )
        pieces.append(jnp.where(lane < part, first, second))
    unfold = split(jnp.concatenate(pieces))
    out[...] = dot3(dot3(unfold, one), unfold, tn)


def pack_two(part, high, low, basis, out, flat, sems, *, share, half, count):
    rank = part.shape[0]
    parts = high.shape[2] // lanes
    slots = share * parts
    chunks = sems.shape[0]
    tall = half // chunks * slots

    def leave(at):
        source = flat.reshape(count, half * slots, lanes).at[:, at * tall : (at + 1) * tall]
        return pltpu.make_async_copy(source, out.at[:, at * tall : (at + 1) * tall], sems.at[at])

    value = orthonormal(part[...])
    basis[...] = value
    value = split(value)
    both = jnp.concatenate(value)
    for at in range(chunks):
        for k in range(at * half // chunks, (at + 1) * half // chunks):
            first = lax.dot_general(both, high[k], nn, preferred_element_type=jnp.float32)
            second = lax.dot_general(value[0], low[k], nn, preferred_element_type=jnp.float32)
            along = first[:rank] + (first[rank:] + second)
            for s in range(share):
                for h in range(parts):
                    start = k * slots + s * parts + h
                    flat[pl.ds(start, count, stride=half * slots), :] = along[
                        s * count : (s + 1) * count, h * lanes : (h + 1) * lanes
                    ]
        leave(at).start()
    for at in range(chunks):
        leave(at).wait()


def taken(got, s, parts, slots, size):
    return jnp.concatenate(
        [got[pl.ds(s * parts + h, size, stride=slots), :] for h in range(parts)], axis=1
    )


def work_two(got, two, three, out, high, low, *, share, half, count):
    parts = two.shape[0] // lanes
    size = count * half
    table = split(three[:, : two.shape[1]])
    field = []
    for s in range(share):
        value = split(taken(got, s, parts, share * parts, size))
        high[s], low[s] = value
        field.append(value)
    field = [jnp.concatenate(value, axis=1) for value in zip(*field)]
    field = dot3(table, tuple(field), tn)
    cols = parts * lanes
    unfold = split(jnp.concatenate([field[:, s * cols : (s + 1) * cols] for s in range(share)]))
    out[...] = dot3(dot3(unfold, two[...]), unfold, tn)


def laid(size):
    return size // lanes, size % lanes != 0


def work_three(
    part, high, low, three, basis, out, sent, room, flat, sem, *, share, half, count
):
    rank, cols = part.shape
    parts = cols // lanes
    size = count * half
    whole, rest = laid(size)
    pitch = flat.shape[0] // count
    value = orthonormal(part[...])
    basis[...] = value
    for h in range(parts):
        room[h * rank : (h + 1) * rank, :] = value[:, h * lanes : (h + 1) * lanes]
    second = split(
        jnp.concatenate(
            [
                jnp.concatenate(
                    [room[pl.ds(h * rank + b, count, stride=share), :] for h in range(parts)],
                    axis=1,
                )
                for b in range(share)
            ]
        )
    )
    pieces = [dot3(second, (high[s], low[s]), nt) for s in range(share)]
    ends = []
    for b in range(share):
        for s in range(share):
            value = pieces[s][b * count : (b + 1) * count]
            for h in range(whole):
                start = (b * share + s) * whole + h
                flat[pl.ds(start, count, stride=pitch), :] = value[:, h * lanes : (h + 1) * lanes]
            if rest:
                ends.append(value[:, whole * lanes :])
    if len(ends) % 2:
        ends.append(ends[-1])
    for at in range(0, len(ends), 2):
        flat[pl.ds(share * share * whole + at // 2, count, stride=pitch), :] = jnp.concatenate(
            ends[at : at + 2], axis=1
        )
    copy = pltpu.make_async_copy(flat, sent, sem)
    copy.start()
    value = split(jnp.concatenate(pieces))
    result = dot3(dot3(value, three[:, :rank]), value, tn)
    for h in range(whole):
        out[h * rank : (h + 1) * rank, :] = result[:, h * lanes : (h + 1) * lanes]
    if rest:
        end = result[:, whole * lanes :]
        out[whole * rank :, :] = jnp.concatenate([end[: rank // 2], end[rank // 2 :]], axis=1)
    copy.wait()


def finish(part, got, basis, core, room, *, share, half, count):
    size, rank = room.shape
    whole, rest = laid(size)
    pitch = got.shape[0] // count
    value = [part[h * rank : (h + 1) * rank, :] for h in range(whole)]
    if rest:
        end = part[whole * rank :, :]
        value.append(jnp.concatenate([end[:, : lanes // 2], end[:, lanes // 2 :]]))
    value = orthonormal(jnp.concatenate(value, axis=1))
    room[...] = value.T
    depth = basis.shape[0]
    basis[...] = room[pl.ds(pl.multiple_of(lax.axis_index("wide") * depth, 8), depth), :]
    rows = []
    for b in range(share):
        for s in range(share):
            at = b * share + s
            pieces = [
                got[pl.ds(at * whole + h, count, stride=pitch), :] for h in range(whole)
            ]
            if rest:
                end = got[pl.ds(share * share * whole + at // 2, count, stride=pitch), :]
                pieces.append(end[:, lanes // 2 :] if at % 2 else end[:, : lanes // 2])
            rows.append(jnp.concatenate(pieces, axis=1))
    value = dot3(jnp.concatenate(rows), value, nt)
    for b in range(share):
        core[:, b * rank : (b + 1) * rank] = value[b * rank : (b + 1) * rank]


def exchange(value, count):
    rows = value.shape[0]
    flat = value.reshape(count, 1, rows // count * lanes)
    return lax.all_to_all(flat, group, 0, 0, tiled=True).reshape(rows, lanes)


def special(window_data, factor_one, factor_two, factor_three):
    wide = lax.axis_size("wide")
    count = wide * lax.axis_size("narrow")
    depth, rows, cols = window_data.shape
    rank = factor_one.shape[1]
    share = rank // count
    half = depth // 2
    size = count * half
    facts = {"share": share, "half": half, "count": count}
    core_at = lax.axis_index("narrow")

    def stage(body):
        def run(*refs):
            body(*refs, **facts)

        run.__name__ = body.__name__
        return run

    parts = cols // lanes
    chunks = 3 if half % 3 == 0 else 1
    pitch = half * share + half // 2
    packed, sent = call(
        stage(pack_one),
        [far(count * pitch, lanes), far(half, rows, cols)],
        window_data,
        factor_two.T,
        factor_three,
        away=(0, 1, 2),
        away_out=(0, 1),
        scratch_shapes=[
            near(chunks, 2, half // chunks, rows, cols),
            near(count * pitch, lanes),
            near(rank, cols),
            near(depth, rank),
            pltpu.SemaphoreType.DMA((3 * chunks + 3,)),
        ],
    )
    got = exchange(packed, count)
    high, low = call(
        prepare,
        [near(half, 2 * rows, cols, dtype=jnp.bfloat16)] * 2,
        window_data,
        swap(sent),
        away=(0,),
        scratch_shapes=[near(half, rows, cols), pltpu.SemaphoreType.DMA],
    )
    one_other = swap(factor_one)
    got, high, low = lax.optimization_barrier((got, high, low))
    product, three = call(
        stage(work_one),
        [near(rank, 2 * rows), near(size, lanes)],
        got,
        factor_one,
        one_other,
        scratch_shapes=[near(count * pitch // share, lanes)],
    )
    product = total(product)

    chunks = 3 if half % 3 == 0 and half // 3 * share * parts % 8 == 0 else 1
    one_t, packed = call(
        stage(pack_two),
        [near(*product.shape), far(count, half * share * parts, lanes)],
        product,
        high,
        low,
        away_out=(1,),
        scratch_shapes=[
            near(size * share * parts, lanes),
            pltpu.SemaphoreType.DMA((chunks,)),
        ],
    )
    got = exchange(packed.reshape(size * share * parts, lanes), count)
    product, high, low = call(
        stage(work_two),
        [near(rank, cols)] + [near(share, size, cols, dtype=jnp.bfloat16)] * 2,
        got,
        factor_two,
        three,
    )
    product = total(product)

    whole, rest = laid(size)
    pitch = share * share * whole + rest * -(-share * share // 2)
    pitch = -(-pitch // 8) * 8
    two_t, product, sent = call(
        stage(work_three),
        [
            near(*product.shape),
            near(rank * whole + rest * rank // 2, lanes),
            far(count * pitch, lanes),
        ],
        product,
        high,
        low,
        three,
        away_out=(2,),
        scratch_shapes=[
            near(parts * rank, lanes),
            near(count * pitch, lanes),
            pltpu.SemaphoreType.DMA,
        ],
    )
    got = exchange(sent, count)
    product = total(product)
    basis_three, core = call(
        stage(finish),
        [far(depth, rank), far(rank, share * rank)],
        product,
        got,
        scratch_shapes=[near(size, rank)],
    )
    basis_one = lax.dynamic_slice_in_dim(one_t, core_at * rows, rows, 1).T
    return (basis_one, two_t.T, basis_three, core)


def on_device(window_data, factor_one, factor_two, factor_three):
    count = lax.axis_size("wide") * lax.axis_size("narrow")
    depth, rows, cols = window_data.shape
    rank = factor_one.shape[1]
    fits = (
        lax.axis_size("narrow") == 2
        and rank % count == 0
        and count % 8 == 0
        and depth % 8 == 0
        and count * depth // 2 % (lanes // 2) == 0
        and rank % 16 == 0
        and depth // 4 % (rank // count) == 0
        and count * depth * (2 * (rank // count) + 1) // 4 % 8 == 0
        and (depth // 2) * (rank // count) * (cols // lanes) % 8 == 0
        and 2 * rows == lanes
        and 2 * rank <= lanes
        and cols % lanes == 0
    )
    return (special if fits else general)(window_data, factor_one, factor_two, factor_three)


def solution(mesh):
    return jax.shard_map(
        on_device,
        mesh=mesh,
        in_specs=(
            P(("win", "wide"), "narrow", None),
            P(("win", "narrow"), None),
            P("win", None),
            P(("win", "wide"), None),
        ),
        out_specs=(
            P(("win", "narrow"), None),
            P("win", None),
            P(("win", "wide"), None),
            P(None, ("win", "wide", "narrow")),
        ),
        check_vma=False,
    )
```

```python
import jax
import jax.numpy as jnp
from jax import lax
from jax.experimental import pallas as pl
from jax.experimental.pallas import tpu as pltpu
from jax.sharding import PartitionSpec as P

highest = lax.Precision.HIGHEST
fine = lax.Precision.HIGH
group = ("wide", "narrow")
lanes = 128
nn = (((1,), (0,)), ((), ()))
nt = (((1,), (1,)), ((), ()))
tn = (((0,), (0,)), ((), ()))


def contract(form, left, right, precision=fine):
    return jnp.einsum(form, left, right, precision=precision)


def total(part, far_first=True):
    narrow = lax.axis_size("narrow")
    count = lax.axis_size("wide") * narrow
    if narrow != 2 or count & (count - 1):
        return lax.psum(part, group)

    def moved(mask):
        return lax.ppermute(part, group, [(at, at ^ mask) for at in range(count)])

    part = part + moved(1)
    bits = []
    while narrow < count:
        bits.append(narrow)
        narrow *= 2
    parts = []
    if len(bits) % 2:
        parts = [bits[-1:]] if far_first else [bits[:1]]
        bits = bits[:-1] if far_first else bits[1:]
    parts += [bits[at : at + 2] for at in range(0, len(bits), 2)]
    for low, *high in parts:
        if high:
            near_sum, far_sum = moved(low + 1), moved(high[0] + 1)
            part = (part + near_sum) + (far_sum + moved(low + high[0] + 1))
        else:
            part = part + moved(low + 1)
    return part


def swap(value):
    return lax.ppermute(value, "narrow", [(0, 1), (1, 0)])


def dot(left, right, dims=nn):
    return lax.dot_general(
        left, right, dims, precision=highest, preferred_element_type=jnp.float32
    )


def split(value):
    high = value.astype(jnp.bfloat16)
    return high, (value - high.astype(jnp.float32)).astype(jnp.bfloat16)


def dot3(left, right, dims=nn):
    left_high, left_low = left if isinstance(left, tuple) else split(left)
    right_high, right_low = right if isinstance(right, tuple) else split(right)

    def one(a, b):
        return lax.dot_general(a, b, dims, preferred_element_type=jnp.float32)

    return one(left_high, right_high) + (one(left_high, right_low) + one(left_low, right_high))


def eliminate(table, rank):
    width = table.shape[1]
    row = lax.broadcasted_iota(jnp.int32, (8, width), 0)
    tiles = [table[8 * at : 8 * at + 8] for at in range(rank // 8)]
    for at in range(rank // 8):
        live = tiles[at:]
        columns = [
            [jnp.broadcast_to(x[:, 8 * at + k : 8 * at + k + 1], (8, width)) for x in live]
            for k in range(8)
        ]
        root = None
        for j in range(8):
            heads = [jnp.broadcast_to(columns[k][0][j : j + 1], (8, width)) for k in range(j, 8)]
            inverse = 1.0 / heads[0]
            root = jnp.where(row == j, lax.rsqrt(heads[0]), 0.0 if root is None else root)
            scale = [x * inverse for x in columns[j]]
            scale[0] = jnp.where(row > j, scale[0], 0.0)
            for k in range(j + 1, 8):
                columns[k] = [x - y * heads[k - j] for x, y in zip(columns[k], scale)]
            lead = jnp.broadcast_to(live[0][j : j + 1], (8, width))
            live = [x - y * lead for x, y in zip(live, scale)]
        tiles[at:] = live
        tiles[at] = live[0] * root
    return jnp.concatenate(tiles, axis=0)


def orthonormal(part):
    rank, size = part.shape
    width = -(-2 * rank // lanes) * lanes
    below = jnp.zeros((width - rank, size), part.dtype)
    gram = dot(part, jnp.concatenate([part, below]), nt)
    row = lax.broadcasted_iota(jnp.int32, (rank, width), 0)
    lane = lax.broadcasted_iota(jnp.int32, (rank, width), 1)
    table = eliminate(jnp.where(lane == row + rank, 1.0, gram), rank)
    table = jnp.where(lane < rank, 0.0, table)
    padded = [jnp.zeros((rank, size), part.dtype), part]
    if width > 2 * rank:
        padded.append(jnp.zeros((width - 2 * rank, size), part.dtype))
    return dot(table, jnp.concatenate(padded))


def orthonormal_body(part, out):
    out[...] = orthonormal(part[...])


def near(*shape, dtype=jnp.float32):
    return pltpu.VMEM(shape, dtype)


def far(*shape, dtype=jnp.float32):
    return jax.ShapeDtypeStruct(shape, dtype)


def call(body, shapes, *operands, away=(), away_out=(), **settings):
    inside = pl.BlockSpec(memory_space=pltpu.VMEM)
    outside = pl.BlockSpec(memory_space=pl.ANY)
    placed = [
        x if at in away else pltpu.with_memory_space_constraint(x, pltpu.VMEM)
        for at, x in enumerate(operands)
    ]
    return pl.pallas_call(
        body,
        in_specs=[outside if at in away else inside for at in range(len(operands))],
        out_specs=[outside if at in away_out else inside for at in range(len(shapes))],
        out_shape=shapes,
        **settings,
    )(*placed)


def general(window_data, factor_one, factor_two, factor_three):
    wide = lax.axis_size("wide")
    narrow = lax.axis_size("narrow")
    count = wide * narrow
    depth, rows, cols = window_data.shape
    rank = factor_one.shape[1]
    share = -(-rank // count)
    spare = share * count - rank
    half = depth // narrow
    core_at = lax.axis_index("narrow")

    own = lax.dynamic_slice_in_dim(window_data, core_at * half, half, 0)
    sent = lax.dynamic_slice_in_dim(window_data, (1 - core_at) * half, half, 0)
    other = swap(sent)
    factor_other = swap(factor_one)

    two_t = jnp.pad(factor_two.T, ((0, spare), (0, 0)))
    along = contract("bj,kij->bki", two_t, window_data).reshape(count, share, depth * rows)
    three_own = lax.dynamic_slice_in_dim(factor_three, core_at * half, half, 0)
    three_flat = jnp.broadcast_to(three_own.reshape(1, 1, half * rank), (count, 1, half * rank))
    packed = jnp.concatenate([along.reshape(count, -1), three_flat.reshape(count, -1)], axis=1)
    width = packed.shape[1]
    full = -(-width // 1024) * 1024
    packed = jnp.pad(packed, ((0, 0), (0, full - width))).reshape(count, full // 128, 128)
    got = lax.all_to_all(packed, group, 0, 0, tiled=True).reshape(count, full)
    three = got[:, share * depth * rows : width].reshape(wide, depth, rank)
    got = got[:, : share * depth * rows].reshape(wide, narrow, share, depth, rows)
    first = jnp.where(core_at == 0, factor_one, factor_other)
    second = jnp.where(core_at == 0, factor_other, factor_one)
    one = jnp.stack([first, second])
    unfold = contract("wnbki,wkc->bcni", got, three)
    weights = contract("bcni,nia->bca", unfold, one)
    product = contract("bcni,bca->ani", unfold, weights).reshape(rank, narrow * rows)
    product = total(product)
    one_t = call(orthonormal_body, [near(*product.shape)], product)[0]

    one_pad = jnp.pad(one_t, ((0, spare), (0, 0)))
    one_own = lax.dynamic_slice_in_dim(one_pad, core_at * rows, rows, 1)
    one_other = lax.dynamic_slice_in_dim(one_pad, (1 - core_at) * rows, rows, 1)
    along = contract("ai,kij->akj", one_own, own) + contract("ai,kij->akj", one_other, other)
    got = lax.all_to_all(
        along.reshape(count, share * half * cols // 128, 128), group, 0, 0, tiled=True
    ).reshape(count, share, half, cols)
    three = three.reshape(count, half, rank)
    unfold = contract("dakj,dkc->acj", got, three)
    weights = contract("acj,jb->acb", unfold, factor_two)
    product = contract("acj,acb->bj", unfold, weights)
    product = total(product)
    two_t = call(orthonormal_body, [near(*product.shape)], product)[0]

    unfold = contract("dakj,bj->dakb", got, two_t)
    weights = contract("dakb,dkc->abc", unfold, three)
    product = contract("dakb,abc->cdk", unfold, weights).reshape(rank, count * half)
    product = total(product)
    three_t = call(orthonormal_body, [near(*product.shape)], product)[0]
    core = contract("dakb,cdk->abc", unfold, three_t.reshape(rank, count, half))
    core = core.reshape(share, count, rank * rank // count).transpose(1, 0, 2)
    core = lax.all_to_all(core, group, 0, 0, tiled=True)
    core = core.reshape(count * share, rank * rank // count)[:rank]
    basis_three = lax.dynamic_slice_in_dim(three_t, lax.axis_index("wide") * depth, depth, 1).T
    return (one_own[:rank].T, two_t.T, basis_three, core)


def pack_one(field, two_far, three_far, out, sent, room, flat, two, three, sems, *, share, half, count):
    chunks, _, steps, rows, cols = room.shape
    rank = two.shape[0]
    pitch = flat.shape[0] // count
    at_core = lax.axis_index("narrow")

    def fetch(at, h):
        source = field.at[pl.ds(h * half + at * steps, steps)]
        return pltpu.make_async_copy(source, room.at[at, h], sems.at[2 * at + h])

    def hand(at):
        target = sent.at[pl.ds(at * steps, steps)]
        return pltpu.make_async_copy(room.at[at, 1 - at_core], target, sems.at[2 * chunks + at])

    copies = [
        pltpu.make_async_copy(three_far, three, sems.at[3 * chunks]),
        pltpu.make_async_copy(two_far, two, sems.at[3 * chunks + 1]),
    ]
    leave = pltpu.make_async_copy(flat, out, sems.at[3 * chunks + 2])
    for h in range(2):
        fetch(0, h).start()
    for copy in copies:
        copy.start()
    for at in range(1, chunks):
        for h in range(2):
            fetch(at, h).start()
    copies[0].wait()
    own = jnp.where(at_core == 0, three[:half], three[half:])
    empty = jnp.zeros((half // 2, lanes // 2 - rank), jnp.float32)
    both = jnp.concatenate([own[: half // 2], empty, own[half // 2 :], empty], axis=1)
    for r in range(half // 2):
        flat[pl.ds(half * share + r, count, stride=pitch), :] = jnp.broadcast_to(
            both[r : r + 1], (count, lanes)
        )
    copies[1].wait()
    two_high, two_low = split(two[...])
    both = jnp.concatenate([two_high, two_low])
    for at in range(chunks):
        for h in range(2):
            fetch(at, h).wait()
        hand(at).start()
        value = [room[at, h, q] for q in range(steps) for h in range(2)]
        high, low = split(jnp.concatenate(value))
        first = lax.dot_general(both, high, nt, preferred_element_type=jnp.float32)
        second = lax.dot_general(two_high, low, nt, preferred_element_type=jnp.float32)
        along = first[:rank] + (first[rank:] + second)
        for q in range(steps):
            for s in range(share):
                flat[pl.ds((at * steps + q) * share + s, count, stride=pitch), :] = along[
                    s * count : (s + 1) * count, q * lanes : (q + 1) * lanes
                ]
    leave.start()
    for at in range(chunks):
        hand(at).wait()
    leave.wait()


def prepare(field, other, high, low, own, sem):
    half, rows, cols = other.shape
    at = lax.axis_index("narrow")
    copy = pltpu.make_async_copy(field.at[pl.ds(at * half, half)], own, sem)
    copy.start()

    def put(value, core):
        top, rest = split(value[...])
        high[:, pl.ds(pl.multiple_of(core * rows, 16), rows), :] = top
        low[:, pl.ds(pl.multiple_of(core * rows, 16), rows), :] = rest

    put(other, 1 - at)
    copy.wait()
    put(own, at)


def work_one(got, own, other, out, three, table, *, share, half, count):
    rank = own.shape[1]
    part = lanes // 2
    pitch = got.shape[0] // count
    each = pitch // share
    size = count * each
    wide = count // 2
    at = lax.axis_index("narrow")
    low = jnp.where(at == 0, own[...], other[...])
    high = jnp.where(at == 0, other[...], own[...])
    one = jnp.concatenate([low, high])
    left = lax.broadcasted_iota(jnp.int32, (wide, lanes), 1) < part
    for r in range(half // 2):
        first, second = [
            got[pl.ds(half * share + r + h * pitch, wide, stride=2 * pitch), :] for h in range(2)
        ]
        first_turned, second_turned = pltpu.roll(first, part, 1), pltpu.roll(second, part, 1)
        for n in range(2):
            start = n * each + r
            table[pl.ds(start, wide, stride=2 * each), :] = jnp.where(left, first, second_turned)
            table[pl.ds(start + half // 2, wide, stride=2 * each), :] = jnp.where(
                left, first_turned, second
            )
        for at, value in enumerate((first, first_turned, second, second_turned)):
            three[pl.ds(at * half // 2 + r, wide, stride=2 * half), :] = value
    for r in range(half, each):
        for n in range(2):
            table[pl.ds(n * each + r, wide, stride=2 * each), :] = jnp.zeros(
                (wide, lanes), jnp.float32
            )
    value = table[...]
    row = lax.broadcasted_iota(jnp.int32, (size, lanes), 0)
    odd = (row // each) % 2 == 1
    value = jnp.concatenate([jnp.where(odd, 0.0, value), jnp.where(odd, value, 0.0)], axis=1)
    mixed = split(value)
    lane = lax.broadcasted_iota(jnp.int32, (rank, lanes), 1)
    pieces = []
    field = jnp.concatenate([got[pl.ds(s, size, stride=share), :] for s in range(share)], axis=1)
    field = dot3(mixed, field, tn)
    for s in range(share):
        value = field[:, s * lanes : (s + 1) * lanes]
        first = value[:rank] + pltpu.roll(value[part : part + rank], part, 1)
        second = (
            pltpu.roll(value[2 * part : 2 * part + rank], part, 1)
            + value[3 * part : 3 * part + rank]
        )
        pieces.append(jnp.where(lane < part, first, second))
    unfold = split(jnp.concatenate(pieces))
    out[...] = dot3(dot3(unfold, one), unfold, tn)


def pack_two(part, high, low, basis, out, flat, sems, *, share, half, count):
    rank = part.shape[0]
    parts = high.shape[2] // lanes
    slots = share * parts
    chunks = sems.shape[0]
    tall = half // chunks * slots

    def leave(at):
        source = flat.reshape(count, half * slots, lanes).at[:, at * tall : (at + 1) * tall]
        return pltpu.make_async_copy(source, out.at[:, at * tall : (at + 1) * tall], sems.at[at])

    value = orthonormal(part[...])
    basis[...] = value
    value = split(value)
    both = jnp.concatenate(value)
    for at in range(chunks):
        for k in range(at * half // chunks, (at + 1) * half // chunks):
            first = lax.dot_general(both, high[k], nn, preferred_element_type=jnp.float32)
            second = lax.dot_general(value[0], low[k], nn, preferred_element_type=jnp.float32)
            along = first[:rank] + (first[rank:] + second)
            for s in range(share):
                for h in range(parts):
                    start = k * slots + s * parts + h
                    flat[pl.ds(start, count, stride=half * slots), :] = along[
                        s * count : (s + 1) * count, h * lanes : (h + 1) * lanes
                    ]
        leave(at).start()
    for at in range(chunks):
        leave(at).wait()


def taken(got, s, parts, slots, size):
    return jnp.concatenate(
        [got[pl.ds(s * parts + h, size, stride=slots), :] for h in range(parts)], axis=1
    )


def work_two(got, two, three, out, high, low, *, share, half, count):
    parts = two.shape[0] // lanes
    size = count * half
    table = split(three[:, : two.shape[1]])
    field = []
    for s in range(share):
        value = split(taken(got, s, parts, share * parts, size))
        high[s], low[s] = value
        field.append(value)
    field = [jnp.concatenate(value, axis=1) for value in zip(*field)]
    field = dot3(table, tuple(field), tn)
    cols = parts * lanes
    unfold = split(jnp.concatenate([field[:, s * cols : (s + 1) * cols] for s in range(share)]))
    out[...] = dot3(dot3(unfold, two[...]), unfold, tn)


def laid(size):
    return size // lanes, size % lanes != 0


def work_three(
    part, high, low, three, basis, out, sent, room, flat, sem, *, share, half, count
):
    rank, cols = part.shape
    parts = cols // lanes
    size = count * half
    whole, rest = laid(size)
    pitch = flat.shape[0] // count
    value = orthonormal(part[...])
    basis[...] = value
    for h in range(parts):
        room[h * rank : (h + 1) * rank, :] = value[:, h * lanes : (h + 1) * lanes]
    second = split(
        jnp.concatenate(
            [
                jnp.concatenate(
                    [room[pl.ds(h * rank + b, count, stride=share), :] for h in range(parts)],
                    axis=1,
                )
                for b in range(share)
            ]
        )
    )
    pieces = [dot3(second, (high[s], low[s]), nt) for s in range(share)]
    ends = []
    for b in range(share):
        for s in range(share):
            value = pieces[s][b * count : (b + 1) * count]
            for h in range(whole):
                start = (b * share + s) * whole + h
                flat[pl.ds(start, count, stride=pitch), :] = value[:, h * lanes : (h + 1) * lanes]
            if rest:
                ends.append(value[:, whole * lanes :])
    if len(ends) % 2:
        ends.append(ends[-1])
    for at in range(0, len(ends), 2):
        flat[pl.ds(share * share * whole + at // 2, count, stride=pitch), :] = jnp.concatenate(
            ends[at : at + 2], axis=1
        )
    copy = pltpu.make_async_copy(flat, sent, sem)
    copy.start()
    value = split(jnp.concatenate(pieces))
    result = dot3(dot3(value, three[:, :rank]), value, tn)
    for h in range(whole):
        out[h * rank : (h + 1) * rank, :] = result[:, h * lanes : (h + 1) * lanes]
    if rest:
        end = result[:, whole * lanes :]
        out[whole * rank :, :] = jnp.concatenate([end[: rank // 2], end[rank // 2 :]], axis=1)
    copy.wait()


def finish(part, got, basis, core, room, *, share, half, count):
    size, rank = room.shape
    whole, rest = laid(size)
    pitch = got.shape[0] // count
    value = [part[h * rank : (h + 1) * rank, :] for h in range(whole)]
    if rest:
        end = part[whole * rank :, :]
        value.append(jnp.concatenate([end[:, : lanes // 2], end[:, lanes // 2 :]]))
    value = orthonormal(jnp.concatenate(value, axis=1))
    room[...] = value.T
    depth = basis.shape[0]
    basis[...] = room[pl.ds(pl.multiple_of(lax.axis_index("wide") * depth, 8), depth), :]
    rows = []
    for b in range(share):
        for s in range(share):
            at = b * share + s
            pieces = [
                got[pl.ds(at * whole + h, count, stride=pitch), :] for h in range(whole)
            ]
            if rest:
                end = got[pl.ds(share * share * whole + at // 2, count, stride=pitch), :]
                pieces.append(end[:, lanes // 2 :] if at % 2 else end[:, : lanes // 2])
            rows.append(jnp.concatenate(pieces, axis=1))
    value = dot3(jnp.concatenate(rows), value, nt)
    for b in range(share):
        core[:, b * rank : (b + 1) * rank] = value[b * rank : (b + 1) * rank]


def exchange(value, count):
    rows = value.shape[0]
    flat = value.reshape(count, 1, rows // count * lanes)
    return lax.all_to_all(flat, group, 0, 0, tiled=True).reshape(rows, lanes)


def special(window_data, factor_one, factor_two, factor_three):
    wide = lax.axis_size("wide")
    count = wide * lax.axis_size("narrow")
    depth, rows, cols = window_data.shape
    rank = factor_one.shape[1]
    share = rank // count
    half = depth // 2
    size = count * half
    facts = {"share": share, "half": half, "count": count}
    core_at = lax.axis_index("narrow")

    def stage(body):
        def run(*refs):
            body(*refs, **facts)

        run.__name__ = body.__name__
        return run

    parts = cols // lanes
    chunks = 3 if half % 3 == 0 else 1
    pitch = half * share + half // 2
    packed, sent = call(
        stage(pack_one),
        [far(count * pitch, lanes), far(half, rows, cols)],
        window_data,
        factor_two.T,
        factor_three,
        away=(0, 1, 2),
        away_out=(0, 1),
        scratch_shapes=[
            near(chunks, 2, half // chunks, rows, cols),
            near(count * pitch, lanes),
            near(rank, cols),
            near(depth, rank),
            pltpu.SemaphoreType.DMA((3 * chunks + 3,)),
        ],
    )
    got = exchange(packed, count)
    high, low = call(
        prepare,
        [near(half, 2 * rows, cols, dtype=jnp.bfloat16)] * 2,
        window_data,
        swap(sent),
        away=(0,),
        scratch_shapes=[near(half, rows, cols), pltpu.SemaphoreType.DMA],
    )
    one_other = swap(factor_one)
    got, high, low = lax.optimization_barrier((got, high, low))
    product, three = call(
        stage(work_one),
        [near(rank, 2 * rows), near(size, lanes)],
        got,
        factor_one,
        one_other,
        scratch_shapes=[near(count * pitch // share, lanes)],
    )
    product = total(product)

    chunks = 3 if half % 3 == 0 and half // 3 * share * parts % 8 == 0 else 1
    one_t, packed = call(
        stage(pack_two),
        [near(*product.shape), far(count, half * share * parts, lanes)],
        product,
        high,
        low,
        away_out=(1,),
        scratch_shapes=[
            near(size * share * parts, lanes),
            pltpu.SemaphoreType.DMA((chunks,)),
        ],
    )
    got = exchange(packed.reshape(size * share * parts, lanes), count)
    product, high, low = call(
        stage(work_two),
        [near(rank, cols)] + [near(share, size, cols, dtype=jnp.bfloat16)] * 2,
        got,
        factor_two,
        three,
    )
    product = total(product, far_first=False)

    whole, rest = laid(size)
    pitch = share * share * whole + rest * -(-share * share // 2)
    pitch = -(-pitch // 8) * 8
    two_t, product, sent = call(
        stage(work_three),
        [
            near(*product.shape),
            near(rank * whole + rest * rank // 2, lanes),
            far(count * pitch, lanes),
        ],
        product,
        high,
        low,
        three,
        away_out=(2,),
        scratch_shapes=[
            near(parts * rank, lanes),
            near(count * pitch, lanes),
            pltpu.SemaphoreType.DMA,
        ],
    )
    got = exchange(sent, count)
    product = total(product)
    basis_three, core = call(
        stage(finish),
        [far(depth, rank), far(rank, share * rank)],
        product,
        got,
        scratch_shapes=[near(size, rank)],
    )
    basis_one = lax.dynamic_slice_in_dim(one_t, core_at * rows, rows, 1).T
    return (basis_one, two_t.T, basis_three, core)


def on_device(window_data, factor_one, factor_two, factor_three):
    count = lax.axis_size("wide") * lax.axis_size("narrow")
    depth, rows, cols = window_data.shape
    rank = factor_one.shape[1]
    fits = (
        lax.axis_size("narrow") == 2
        and rank % count == 0
        and count % 8 == 0
        and depth % 8 == 0
        and count * depth // 2 % (lanes // 2) == 0
        and rank % 16 == 0
        and depth // 4 % (rank // count) == 0
        and count * depth * (2 * (rank // count) + 1) // 4 % 8 == 0
        and (depth // 2) * (rank // count) * (cols // lanes) % 8 == 0
        and 2 * rows == lanes
        and 2 * rank <= lanes
        and cols % lanes == 0
    )
    return (special if fits else general)(window_data, factor_one, factor_two, factor_three)


def solution(mesh):
    return jax.shard_map(
        on_device,
        mesh=mesh,
        in_specs=(
            P(("win", "wide"), "narrow", None),
            P(("win", "narrow"), None),
            P("win", None),
            P(("win", "wide"), None),
        ),
        out_specs=(
            P(("win", "narrow"), None),
            P("win", None),
            P(("win", "wide"), None),
            P(None, ("win", "wide", "narrow")),
        ),
        check_vma=False,
    )
```

```python
import jax
import jax.numpy as jnp
from jax import lax
from jax.experimental import pallas as pl
from jax.experimental.pallas import tpu as pltpu
from jax.sharding import PartitionSpec as P

highest = lax.Precision.HIGHEST
fine = lax.Precision.HIGH
group = ("wide", "narrow")
lanes = 128
nn = (((1,), (0,)), ((), ()))
nt = (((1,), (1,)), ((), ()))
tn = (((0,), (0,)), ((), ()))


def contract(form, left, right, precision=fine):
    return jnp.einsum(form, left, right, precision=precision)


def total(part, far_first=True):
    narrow = lax.axis_size("narrow")
    count = lax.axis_size("wide") * narrow
    if narrow != 2 or count & (count - 1):
        return lax.psum(part, group)

    def moved(mask):
        return lax.ppermute(part, group, [(at, at ^ mask) for at in range(count)])

    part = part + moved(1)
    bits = []
    while narrow < count:
        bits.append(narrow)
        narrow *= 2
    parts = []
    if len(bits) % 2:
        parts = [bits[-1:]] if far_first else [bits[:1]]
        bits = bits[:-1] if far_first else bits[1:]
    parts += [bits[at : at + 2] for at in range(0, len(bits), 2)]
    for low, *high in parts:
        if high:
            near_sum, far_sum = moved(low + 1), moved(high[0] + 1)
            part = (part + near_sum) + (far_sum + moved(low + high[0] + 1))
        else:
            part = part + moved(low + 1)
    return part


def swap(value):
    return lax.ppermute(value, "narrow", [(0, 1), (1, 0)])


def dot(left, right, dims=nn):
    return lax.dot_general(
        left, right, dims, precision=highest, preferred_element_type=jnp.float32
    )


def split(value):
    high = value.astype(jnp.bfloat16)
    return high, (value - high.astype(jnp.float32)).astype(jnp.bfloat16)


def dot3(left, right, dims=nn):
    left_high, left_low = left if isinstance(left, tuple) else split(left)
    right_high, right_low = right if isinstance(right, tuple) else split(right)

    def one(a, b):
        return lax.dot_general(a, b, dims, preferred_element_type=jnp.float32)

    return one(left_high, right_high) + (one(left_high, right_low) + one(left_low, right_high))


def eliminate(table, rank):
    width = table.shape[1]
    row = lax.broadcasted_iota(jnp.int32, (8, width), 0)
    tiles = [table[8 * at : 8 * at + 8] for at in range(rank // 8)]
    for at in range(rank // 8):
        live = tiles[at:]
        columns = [
            [jnp.broadcast_to(x[:, 8 * at + k : 8 * at + k + 1], (8, width)) for x in live]
            for k in range(8)
        ]
        root = None
        for j in range(8):
            heads = [jnp.broadcast_to(columns[k][0][j : j + 1], (8, width)) for k in range(j, 8)]
            inverse = 1.0 / heads[0]
            root = jnp.where(row == j, lax.rsqrt(heads[0]), 0.0 if root is None else root)
            scale = [x * inverse for x in columns[j]]
            scale[0] = jnp.where(row > j, scale[0], 0.0)
            for k in range(j + 1, 8):
                columns[k] = [x - y * heads[k - j] for x, y in zip(columns[k], scale)]
            lead = jnp.broadcast_to(live[0][j : j + 1], (8, width))
            live = [x - y * lead for x, y in zip(live, scale)]
        tiles[at:] = live
        tiles[at] = live[0] * root
    return jnp.concatenate(tiles, axis=0)


def orthonormal(part):
    rank, size = part.shape
    width = -(-2 * rank // lanes) * lanes
    below = jnp.zeros((width - rank, size), part.dtype)
    gram = dot(part, jnp.concatenate([part, below]), nt)
    row = lax.broadcasted_iota(jnp.int32, (rank, width), 0)
    lane = lax.broadcasted_iota(jnp.int32, (rank, width), 1)
    table = eliminate(jnp.where(lane == row + rank, 1.0, gram), rank)
    table = jnp.where(lane < rank, 0.0, table)
    padded = [jnp.zeros((rank, size), part.dtype), part]
    if width > 2 * rank:
        padded.append(jnp.zeros((width - 2 * rank, size), part.dtype))
    return dot(table, jnp.concatenate(padded))


def orthonormal_body(part, out):
    out[...] = orthonormal(part[...])


def near(*shape, dtype=jnp.float32):
    return pltpu.VMEM(shape, dtype)


def far(*shape, dtype=jnp.float32):
    return jax.ShapeDtypeStruct(shape, dtype)


def call(body, shapes, *operands, away=(), away_out=(), **settings):
    inside = pl.BlockSpec(memory_space=pltpu.VMEM)
    outside = pl.BlockSpec(memory_space=pl.ANY)
    placed = [
        x if at in away else pltpu.with_memory_space_constraint(x, pltpu.VMEM)
        for at, x in enumerate(operands)
    ]
    return pl.pallas_call(
        body,
        in_specs=[outside if at in away else inside for at in range(len(operands))],
        out_specs=[outside if at in away_out else inside for at in range(len(shapes))],
        out_shape=shapes,
        **settings,
    )(*placed)


def general(window_data, factor_one, factor_two, factor_three):
    wide = lax.axis_size("wide")
    narrow = lax.axis_size("narrow")
    count = wide * narrow
    depth, rows, cols = window_data.shape
    rank = factor_one.shape[1]
    share = -(-rank // count)
    spare = share * count - rank
    half = depth // narrow
    core_at = lax.axis_index("narrow")

    own = lax.dynamic_slice_in_dim(window_data, core_at * half, half, 0)
    sent = lax.dynamic_slice_in_dim(window_data, (1 - core_at) * half, half, 0)
    other = swap(sent)
    factor_other = swap(factor_one)

    two_t = jnp.pad(factor_two.T, ((0, spare), (0, 0)))
    along = contract("bj,kij->bki", two_t, window_data).reshape(count, share, depth * rows)
    three_own = lax.dynamic_slice_in_dim(factor_three, core_at * half, half, 0)
    three_flat = jnp.broadcast_to(three_own.reshape(1, 1, half * rank), (count, 1, half * rank))
    packed = jnp.concatenate([along.reshape(count, -1), three_flat.reshape(count, -1)], axis=1)
    width = packed.shape[1]
    full = -(-width // 1024) * 1024
    packed = jnp.pad(packed, ((0, 0), (0, full - width))).reshape(count, full // 128, 128)
    got = lax.all_to_all(packed, group, 0, 0, tiled=True).reshape(count, full)
    three = got[:, share * depth * rows : width].reshape(wide, depth, rank)
    got = got[:, : share * depth * rows].reshape(wide, narrow, share, depth, rows)
    first = jnp.where(core_at == 0, factor_one, factor_other)
    second = jnp.where(core_at == 0, factor_other, factor_one)
    one = jnp.stack([first, second])
    unfold = contract("wnbki,wkc->bcni", got, three)
    weights = contract("bcni,nia->bca", unfold, one)
    product = contract("bcni,bca->ani", unfold, weights).reshape(rank, narrow * rows)
    product = total(product)
    one_t = call(orthonormal_body, [near(*product.shape)], product)[0]

    one_pad = jnp.pad(one_t, ((0, spare), (0, 0)))
    one_own = lax.dynamic_slice_in_dim(one_pad, core_at * rows, rows, 1)
    one_other = lax.dynamic_slice_in_dim(one_pad, (1 - core_at) * rows, rows, 1)
    along = contract("ai,kij->akj", one_own, own) + contract("ai,kij->akj", one_other, other)
    got = lax.all_to_all(
        along.reshape(count, share * half * cols // 128, 128), group, 0, 0, tiled=True
    ).reshape(count, share, half, cols)
    three = three.reshape(count, half, rank)
    unfold = contract("dakj,dkc->acj", got, three)
    weights = contract("acj,jb->acb", unfold, factor_two)
    product = contract("acj,acb->bj", unfold, weights)
    product = total(product)
    two_t = call(orthonormal_body, [near(*product.shape)], product)[0]

    unfold = contract("dakj,bj->dakb", got, two_t)
    weights = contract("dakb,dkc->abc", unfold, three)
    product = contract("dakb,abc->cdk", unfold, weights).reshape(rank, count * half)
    product = total(product)
    three_t = call(orthonormal_body, [near(*product.shape)], product)[0]
    core = contract("dakb,cdk->abc", unfold, three_t.reshape(rank, count, half))
    core = core.reshape(share, count, rank * rank // count).transpose(1, 0, 2)
    core = lax.all_to_all(core, group, 0, 0, tiled=True)
    core = core.reshape(count * share, rank * rank // count)[:rank]
    basis_three = lax.dynamic_slice_in_dim(three_t, lax.axis_index("wide") * depth, depth, 1).T
    return (one_own[:rank].T, two_t.T, basis_three, core)


def pack_one(field, two_far, three_far, out, sent, room, flat, two, three, sems, *, share, half, count):
    chunks, _, steps, rows, cols = room.shape
    rank = two.shape[0]
    pitch = flat.shape[0] // count
    at_core = lax.axis_index("narrow")

    def fetch(at, h):
        source = field.at[pl.ds(h * half + at * steps, steps)]
        return pltpu.make_async_copy(source, room.at[at, h], sems.at[2 * at + h])

    def hand(at):
        target = sent.at[pl.ds(at * steps, steps)]
        return pltpu.make_async_copy(room.at[at, 1 - at_core], target, sems.at[2 * chunks + at])

    copies = [
        pltpu.make_async_copy(three_far, three, sems.at[3 * chunks]),
        pltpu.make_async_copy(two_far, two, sems.at[3 * chunks + 1]),
    ]
    leave = pltpu.make_async_copy(flat, out, sems.at[3 * chunks + 2])
    for h in range(2):
        fetch(0, h).start()
    for copy in copies:
        copy.start()
    for at in range(1, chunks):
        for h in range(2):
            fetch(at, h).start()
    copies[0].wait()
    own = jnp.where(at_core == 0, three[:half], three[half:])
    empty = jnp.zeros((half // 2, lanes // 2 - rank), jnp.float32)
    both = jnp.concatenate([own[: half // 2], empty, own[half // 2 :], empty], axis=1)
    for r in range(half // 2):
        flat[pl.ds(half * share + r, count, stride=pitch), :] = jnp.broadcast_to(
            both[r : r + 1], (count, lanes)
        )
    copies[1].wait()
    two_high, two_low = split(two[...])
    both = jnp.concatenate([two_high, two_low])
    for at in range(chunks):
        for h in range(2):
            fetch(at, h).wait()
        hand(at).start()
        value = [room[at, h, q] for q in range(steps) for h in range(2)]
        high, low = split(jnp.concatenate(value))
        first = lax.dot_general(both, high, nt, preferred_element_type=jnp.float32)
        second = lax.dot_general(two_high, low, nt, preferred_element_type=jnp.float32)
        along = first[:rank] + (first[rank:] + second)
        for q in range(steps):
            for s in range(share):
                flat[pl.ds((at * steps + q) * share + s, count, stride=pitch), :] = along[
                    s * count : (s + 1) * count, q * lanes : (q + 1) * lanes
                ]
    leave.start()
    for at in range(chunks):
        hand(at).wait()
    leave.wait()


def prepare(field, other, high, low, own, sem):
    half, rows, cols = other.shape
    at = lax.axis_index("narrow")
    copy = pltpu.make_async_copy(field.at[pl.ds(at * half, half)], own, sem)
    copy.start()

    def put(value, core):
        top, rest = split(value[...])
        high[:, pl.ds(pl.multiple_of(core * rows, 16), rows), :] = top
        low[:, pl.ds(pl.multiple_of(core * rows, 16), rows), :] = rest

    put(other, 1 - at)
    copy.wait()
    put(own, at)


def work_one(got, own, other, out, three, table, *, share, half, count):
    rank = own.shape[1]
    part = lanes // 2
    pitch = got.shape[0] // count
    each = pitch // share
    size = count * each
    wide = count // 2
    at = lax.axis_index("narrow")
    low = jnp.where(at == 0, own[...], other[...])
    high = jnp.where(at == 0, other[...], own[...])
    one = jnp.concatenate([low, high])
    left = lax.broadcasted_iota(jnp.int32, (wide, lanes), 1) < part
    for r in range(half // 2):
        first, second = [
            got[pl.ds(half * share + r + h * pitch, wide, stride=2 * pitch), :] for h in range(2)
        ]
        first_turned, second_turned = pltpu.roll(first, part, 1), pltpu.roll(second, part, 1)
        for n in range(2):
            start = n * each + r
            table[pl.ds(start, wide, stride=2 * each), :] = jnp.where(left, first, second_turned)
            table[pl.ds(start + half // 2, wide, stride=2 * each), :] = jnp.where(
                left, first_turned, second
            )
        for at, value in enumerate((first, first_turned, second, second_turned)):
            three[pl.ds(at * half // 2 + r, wide, stride=2 * half), :] = value
    for r in range(half, each):
        for n in range(2):
            table[pl.ds(n * each + r, wide, stride=2 * each), :] = jnp.zeros(
                (wide, lanes), jnp.float32
            )
    value = table[...]
    row = lax.broadcasted_iota(jnp.int32, (size, lanes), 0)
    odd = (row // each) % 2 == 1
    value = jnp.concatenate([jnp.where(odd, 0.0, value), jnp.where(odd, value, 0.0)], axis=1)
    mixed = split(value)
    lane = lax.broadcasted_iota(jnp.int32, (rank, lanes), 1)
    pieces = []
    field = jnp.concatenate([got[pl.ds(s, size, stride=share), :] for s in range(share)], axis=1)
    field = dot3(mixed, field, tn)
    for s in range(share):
        value = field[:, s * lanes : (s + 1) * lanes]
        first = value[:rank] + pltpu.roll(value[part : part + rank], part, 1)
        second = (
            pltpu.roll(value[2 * part : 2 * part + rank], part, 1)
            + value[3 * part : 3 * part + rank]
        )
        pieces.append(jnp.where(lane < part, first, second))
    unfold = split(jnp.concatenate(pieces))
    out[...] = dot3(dot3(unfold, one), unfold, tn)


def pack_two(part, high, low, basis, out, flat, sems, *, share, half, count):
    rank = part.shape[0]
    parts = high.shape[2] // lanes
    slots = share * parts
    chunks = sems.shape[0]
    tall = half // chunks * slots

    def leave(at):
        source = flat.reshape(count, half * slots, lanes).at[:, at * tall : (at + 1) * tall]
        return pltpu.make_async_copy(source, out.at[:, at * tall : (at + 1) * tall], sems.at[at])

    value = orthonormal(part[...])
    basis[...] = value
    value = split(value)
    both = jnp.concatenate(value)
    for at in range(chunks):
        for k in range(at * half // chunks, (at + 1) * half // chunks):
            first = lax.dot_general(both, high[k], nn, preferred_element_type=jnp.float32)
            second = lax.dot_general(value[0], low[k], nn, preferred_element_type=jnp.float32)
            along = first[:rank] + (first[rank:] + second)
            for s in range(share):
                for h in range(parts):
                    start = k * slots + s * parts + h
                    flat[pl.ds(start, count, stride=half * slots), :] = along[
                        s * count : (s + 1) * count, h * lanes : (h + 1) * lanes
                    ]
        leave(at).start()
    for at in range(chunks):
        leave(at).wait()


def taken(got, s, parts, slots, size):
    return jnp.concatenate(
        [got[pl.ds(s * parts + h, size, stride=slots), :] for h in range(parts)], axis=1
    )


def work_two(got, two, three, out, high, low, *, share, half, count):
    parts = two.shape[0] // lanes
    size = count * half
    table = split(three[:, : two.shape[1]])
    field = []
    for s in range(share):
        value = split(taken(got, s, parts, share * parts, size))
        high[s], low[s] = value
        field.append(value)
    field = [jnp.concatenate(value, axis=1) for value in zip(*field)]
    field = dot3(table, tuple(field), tn)
    cols = parts * lanes
    unfold = split(jnp.concatenate([field[:, s * cols : (s + 1) * cols] for s in range(share)]))
    out[...] = dot3(dot3(unfold, two[...]), unfold, tn)


def laid(size):
    return size // lanes, size % lanes != 0


def work_three(
    part, high, low, three, basis, out, sent, room, flat, sem, *, share, half, count
):
    rank, cols = part.shape
    parts = cols // lanes
    size = count * half
    whole, rest = laid(size)
    pitch = flat.shape[0] // count
    value = orthonormal(part[...])
    basis[...] = value
    for h in range(parts):
        room[h * rank : (h + 1) * rank, :] = value[:, h * lanes : (h + 1) * lanes]
    second = split(
        jnp.concatenate(
            [
                jnp.concatenate(
                    [room[pl.ds(h * rank + b, count, stride=share), :] for h in range(parts)],
                    axis=1,
                )
                for b in range(share)
            ]
        )
    )
    pieces = [dot3(second, (high[s], low[s]), nt) for s in range(share)]
    ends = []
    for b in range(share):
        for s in range(share):
            value = pieces[s][b * count : (b + 1) * count]
            for h in range(whole):
                start = (b * share + s) * whole + h
                flat[pl.ds(start, count, stride=pitch), :] = value[:, h * lanes : (h + 1) * lanes]
            if rest:
                ends.append(value[:, whole * lanes :])
    if len(ends) % 2:
        ends.append(ends[-1])
    for at in range(0, len(ends), 2):
        flat[pl.ds(share * share * whole + at // 2, count, stride=pitch), :] = jnp.concatenate(
            ends[at : at + 2], axis=1
        )
    copy = pltpu.make_async_copy(flat, sent, sem)
    copy.start()
    value = split(jnp.concatenate(pieces))
    result = dot3(dot3(value, three[:, :rank]), value, tn)
    for h in range(whole):
        out[h * rank : (h + 1) * rank, :] = result[:, h * lanes : (h + 1) * lanes]
    if rest:
        end = result[:, whole * lanes :]
        out[whole * rank :, :] = jnp.concatenate([end[: rank // 2], end[rank // 2 :]], axis=1)
    copy.wait()


def finish(part, got, basis, core, room, block, sems, *, share, half, count):
    size, rank = room.shape
    whole, rest = laid(size)
    pitch = got.shape[0] // count
    value = [part[h * rank : (h + 1) * rank, :] for h in range(whole)]
    if rest:
        end = part[whole * rank :, :]
        value.append(jnp.concatenate([end[:, : lanes // 2], end[:, lanes // 2 :]]))
    value = orthonormal(jnp.concatenate(value, axis=1))
    room[...] = value.T
    depth = basis.shape[0]
    start = pl.multiple_of(lax.axis_index("wide") * depth, 8)
    copies = [
        pltpu.make_async_copy(room.at[pl.ds(start, depth), :], basis, sems.at[0]),
        pltpu.make_async_copy(block, core, sems.at[1]),
    ]
    copies[0].start()
    rows = []
    for b in range(share):
        for s in range(share):
            at = b * share + s
            pieces = [
                got[pl.ds(at * whole + h, count, stride=pitch), :] for h in range(whole)
            ]
            if rest:
                end = got[pl.ds(share * share * whole + at // 2, count, stride=pitch), :]
                pieces.append(end[:, lanes // 2 :] if at % 2 else end[:, : lanes // 2])
            rows.append(jnp.concatenate(pieces, axis=1))
    value = dot3(jnp.concatenate(rows), value, nt)
    for b in range(share):
        block[:, b * rank : (b + 1) * rank] = value[b * rank : (b + 1) * rank]
    copies[1].start()
    for copy in copies:
        copy.wait()


def exchange(value, count):
    rows = value.shape[0]
    flat = value.reshape(count, 1, rows // count * lanes)
    return lax.all_to_all(flat, group, 0, 0, tiled=True).reshape(rows, lanes)


def special(window_data, factor_one, factor_two, factor_three):
    wide = lax.axis_size("wide")
    count = wide * lax.axis_size("narrow")
    depth, rows, cols = window_data.shape
    rank = factor_one.shape[1]
    share = rank // count
    half = depth // 2
    size = count * half
    facts = {"share": share, "half": half, "count": count}
    core_at = lax.axis_index("narrow")

    def stage(body):
        def run(*refs):
            body(*refs, **facts)

        run.__name__ = body.__name__
        return run

    parts = cols // lanes
    chunks = 3 if half % 3 == 0 else 1
    pitch = half * share + half // 2
    packed, sent = call(
        stage(pack_one),
        [far(count * pitch, lanes), far(half, rows, cols)],
        window_data,
        factor_two.T,
        factor_three,
        away=(0, 1, 2),
        away_out=(0, 1),
        scratch_shapes=[
            near(chunks, 2, half // chunks, rows, cols),
            near(count * pitch, lanes),
            near(rank, cols),
            near(depth, rank),
            pltpu.SemaphoreType.DMA((3 * chunks + 3,)),
        ],
    )
    got = exchange(packed, count)
    high, low = call(
        prepare,
        [near(half, 2 * rows, cols, dtype=jnp.bfloat16)] * 2,
        window_data,
        swap(sent),
        away=(0,),
        scratch_shapes=[near(half, rows, cols), pltpu.SemaphoreType.DMA],
    )
    one_other = swap(factor_one)
    got, high, low = lax.optimization_barrier((got, high, low))
    product, three = call(
        stage(work_one),
        [near(rank, 2 * rows), near(size, lanes)],
        got,
        factor_one,
        one_other,
        scratch_shapes=[near(count * pitch // share, lanes)],
    )
    product = total(product)

    chunks = 3 if half % 3 == 0 and half // 3 * share * parts % 8 == 0 else 1
    one_t, packed = call(
        stage(pack_two),
        [near(*product.shape), far(count, half * share * parts, lanes)],
        product,
        high,
        low,
        away_out=(1,),
        scratch_shapes=[
            near(size * share * parts, lanes),
            pltpu.SemaphoreType.DMA((chunks,)),
        ],
    )
    got = exchange(packed.reshape(size * share * parts, lanes), count)
    product, high, low = call(
        stage(work_two),
        [near(rank, cols)] + [near(share, size, cols, dtype=jnp.bfloat16)] * 2,
        got,
        factor_two,
        three,
    )
    product = total(product, far_first=False)

    whole, rest = laid(size)
    pitch = share * share * whole + rest * -(-share * share // 2)
    pitch = -(-pitch // 8) * 8
    two_t, product, sent = call(
        stage(work_three),
        [
            near(*product.shape),
            near(rank * whole + rest * rank // 2, lanes),
            far(count * pitch, lanes),
        ],
        product,
        high,
        low,
        three,
        away_out=(2,),
        scratch_shapes=[
            near(parts * rank, lanes),
            near(count * pitch, lanes),
            pltpu.SemaphoreType.DMA,
        ],
    )
    got = exchange(sent, count)
    product = total(product)
    basis_three, core = call(
        stage(finish),
        [far(depth, rank), far(rank, share * rank)],
        product,
        got,
        away_out=(0, 1),
        scratch_shapes=[
            near(size, rank),
            near(rank, share * rank),
            pltpu.SemaphoreType.DMA((2,)),
        ],
    )
    basis_one = lax.dynamic_slice_in_dim(one_t, core_at * rows, rows, 1).T
    return (basis_one, two_t.T, basis_three, core)


def on_device(window_data, factor_one, factor_two, factor_three):
    count = lax.axis_size("wide") * lax.axis_size("narrow")
    depth, rows, cols = window_data.shape
    rank = factor_one.shape[1]
    fits = (
        lax.axis_size("narrow") == 2
        and rank % count == 0
        and count % 8 == 0
        and depth % 8 == 0
        and count * depth // 2 % (lanes // 2) == 0
        and rank % 16 == 0
        and depth // 4 % (rank // count) == 0
        and count * depth * (2 * (rank // count) + 1) // 4 % 8 == 0
        and (depth // 2) * (rank // count) * (cols // lanes) % 8 == 0
        and 2 * rows == lanes
        and 2 * rank <= lanes
        and cols % lanes == 0
    )
    return (special if fits else general)(window_data, factor_one, factor_two, factor_three)


def solution(mesh):
    return jax.shard_map(
        on_device,
        mesh=mesh,
        in_specs=(
            P(("win", "wide"), "narrow", None),
            P(("win", "narrow"), None),
            P("win", None),
            P(("win", "wide"), None),
        ),
        out_specs=(
            P(("win", "narrow"), None),
            P("win", None),
            P(("win", "wide"), None),
            P(None, ("win", "wide", "narrow")),
        ),
        check_vma=False,
    )
```
